32 devices in a mesh: dp: 4 (over z), expert: 8 (over y, x, core).
Axes of the slice: x: 2, y: 2, z: 4, core: 2. Of those that a mesh axis runs over, the one named last changes fastest.
Arguments:
- tokens: bfloat16 [4096, 2048], P(('dp', 'expert')), may hold values from -6 to 6
- expert_ids: int32 [4096, 1], P(('dp', 'expert')), may hold values from 0 to 7; in each aligned block of 128 rows (0 to 127, 128 to 255, ...) at most 32 rows name the same one
- route_weights: bfloat16 [4096, 1], P(('dp', 'expert')), may hold values from 0.099609375 to 1
- out_grad: bfloat16 [4096, 2048], P(('dp', 'expert')), may hold values from -6 to 6
- gate_weight: bfloat16 [8, 768, 2048], P('expert'), may hold values from -0.125 to 0.125
- down_weight: bfloat16 [8, 768, 2048], P('expert'), may hold values from -0.21875 to 0.21875
Outputs:
- token_grad: bfloat16 [4096, 2048], P(('dp', 'expert'))
- route_grad: bfloat16 [4096, 1], P(('dp', 'expert'))
- gate_grad: bfloat16 [8, 768, 2048], P('expert', 'dp')
- down_grad: bfloat16 [8, 768, 2048], P('expert', 'dp')
The draws below stay inside these ranges and needn't reach their ends.
Inputs may be any that keep to these rules, and one draw needn't show every extreme that they name: `expert_ids`: the 1 expert of a token differ. Among the 128 tokens of one device no expert is named more than 32 times, a bound that some block reaches.
All inputs are finite; a program needn't handle non-finite values.
Results may differ from the reference program's by a relative error of at most 0.015.
Values may be sent and summed in bfloat16 or wider, within the bound.
A program may use at most 64 MiB of HBM per device.

```python
import math
import jax
import jax.numpy as jnp
import numpy as np
from jax import lax

D = 2048
FF = 768
TOP = 1
TOK_DEV = 128
EXPERTS = 8
CAPACITY = 32
TOKENS = 4096
N_DP = 4
N_EXPERT = 8


def levels(key, extent, pieces, smallest, high):
    loudness, own = 1.0, jax.random.fold_in(key, 6)
    for dim, parts in pieces:
        steps = jnp.exp(jax.random.uniform(jax.random.fold_in(own, dim), (parts,), jnp.float32, smallest / len(pieces), high / len(pieces)))
        loudness = loudness * jnp.repeat(steps, extent[dim] // parts).reshape([-1 if axis == dim else 1 for axis in range(len(extent))])
    return loudness


def deal_out(own_key, own, number, rows, number_of, top, limit, lean):
    sequence = jax.random.permutation(own_key, number_of)
    packed, common = portions_of(number_of, rows * top, limit, lean, True), portions_of(number_of, rows * top, limit, lean, False)
    places = jnp.arange(number_of)

    def named(tallies, turn):
        used = int((tallies > 0).sum())
        fixed = max(1, used // 4)
        passed = fixed + (places - fixed + turn * (used - fixed)) % max(1, number_of - fixed)
        return jnp.zeros((number_of,), jnp.int32).at[sequence[jnp.where(places < fixed, places, passed)]].set(jnp.asarray(tallies, jnp.int32))

    tallies = jnp.where(number % 4 == 0, named(packed, number // 4), named(common, number - number // 4 - 1))
    mixed = jax.random.permutation(jax.random.fold_in(own, 3), number_of)
    source_of, taker = mixed[0:number_of // 2 * 2:2], mixed[1:number_of // 2 * 2:2]
    slack = jnp.minimum(tallies[source_of] - 1, limit - tallies[taker]) // 2
    slack = jnp.where((source_of == sequence[0]) | (taker == sequence[0]) | (tallies[taker] == 0), 0, jnp.maximum(slack, 0))
    passed = jax.random.randint(jax.random.fold_in(own, 4), (number_of // 2,), 0, 1 << 20) % (slack + 1)
    tallies = tallies.at[source_of].add(-passed).at[taker].add(passed)
    members = jnp.searchsorted(jnp.cumsum(tallies), jnp.arange(rows * top), side="right").astype(jnp.int32)
    listing = members.reshape(top, rows).T
    listing = listing[jax.random.permutation(jax.random.fold_in(own, 1), rows)]
    turn = jax.random.randint(jax.random.fold_in(own, 2), (rows, 1), 0, top)
    return jnp.take_along_axis(listing, (jnp.arange(top)[None, :] + turn) % top, axis=1)


def portions_of(count, total, reach, skew, full):
    portions = [(1 << 20) // math.isqrt(grade ** skew) + 1 for grade in range(1, count + 1)]
    largest = reach if full else min(reach, max(-(-total // count), total * portions[0] // sum(portions)))
    least = 1 if total - largest >= count - 1 else 0
    counts, spare = [largest] + [least] * (count - 1), total - largest - least * (count - 1)
    while spare > 0:
        candidates = [i for i in range(1, count) if counts[i] < largest] or [i for i in range(1, count) if counts[i] < reach]
        pool, budget = sum([portions[i] for i in candidates]), spare
        for i in candidates:
            extra = min(reach - counts[i], max(1, budget * portions[i] // pool), spare)
            counts[i] = counts[i] + extra
            spare = spare - extra
    return np.array(counts)


def scatter_about(rng, dims, width, limit, split=(), kind=jnp.bfloat16):
    result = jax.random.normal(rng, dims, jnp.float32) * width
    if len(split) > 0:
        result = levels(rng, dims, split, -0.22, 0.18) * result
    return jnp.clip(result, min=-limit, max=limit).astype(kind)


def setup_inputs(seed: int = 0) -> dict:
    key_of = jax.random.split(jax.random.key(seed), 7)
    tokens = scatter_about(key_of[0], (TOKENS, D), 1.0, 6.0, ((0, 32),))
    expert_ids_keys = jax.random.split(jax.random.fold_in(key_of[1], 1), TOKENS // TOK_DEV)
    expert_ids_turns = jax.random.permutation(jax.random.fold_in(key_of[1], 3), TOKENS // TOK_DEV)
    expert_ids = jax.vmap(lambda own, number: deal_out(jax.random.fold_in(key_of[1], 2), own, number, TOK_DEV, EXPERTS, TOP, CAPACITY, 2))(expert_ids_keys, expert_ids_turns).reshape((TOKENS, TOP))
    route_weights = jnp.clip(0.099609375 + 0.9003906 * jax.random.uniform(key_of[2], (TOKENS, TOP), jnp.float32) ** levels(key_of[2], (TOKENS, TOP), ((0, 32),), -0.2, 0.2), 0.099609375, 1.0).astype(jnp.bfloat16)
    out_grad = scatter_about(key_of[3], (TOKENS, D), 1.0, 6.0, ((0, 32),))
    gate_weight = scatter_about(key_of[4], (EXPERTS, FF, D), D ** -0.5, 0.125, ((0, 8),))
    down_weight = scatter_about(key_of[5], (EXPERTS, FF, D), FF ** -0.5, 0.21875, ((0, 8),))
    return {"tokens": tokens, "expert_ids": expert_ids, "route_weights": route_weights, "out_grad": out_grad, "gate_weight": gate_weight, "down_weight": down_weight}


def silu_slope(values):
    sigma = jax.nn.sigmoid(values)
    return sigma * (1.0 + values * (1.0 - sigma))


def reference(tokens, expert_ids, route_weights, out_grad, gate_weight, down_weight):
    devices = TOKENS // TOK_DEV
    per_device = TOK_DEV * TOP
    work_rows = N_EXPERT * CAPACITY
    routed = expert_ids.reshape(devices, per_device)
    one_hot = (routed[:, :, None] == jnp.arange(EXPERTS, dtype=jnp.int32)[None, None, :]).astype(jnp.int32)
    ranking = jnp.sum((jnp.cumsum(one_hot, axis=1) - 1) * one_hot, axis=2)
    device_index = jnp.arange(devices, dtype=jnp.int32)[:, None]
    replica = device_index // N_EXPERT
    source = device_index % N_EXPERT
    position = ((routed * N_DP + replica) * N_EXPERT + source) * CAPACITY + ranking
    pair_index = device_index * per_device + jnp.arange(per_device, dtype=jnp.int32)[None, :]
    total_slots = EXPERTS * N_DP * work_rows
    slot_pair = jnp.full((total_slots,), -1, jnp.int32).at[position.reshape(-1)].set(pair_index.reshape(-1))
    slot_pair = slot_pair.reshape(EXPERTS, N_DP, work_rows)
    weights_flat = route_weights.reshape(-1)

    def expert_work(operands):
        pairs, gate, down = operands

        def replica_work(running, pair_rows):
            valid = pair_rows >= 0
            safe = jnp.maximum(pair_rows, 0)
            token_rows = safe // TOP
            inputs = jnp.where(valid[:, None], tokens[token_rows], jnp.zeros((), jnp.bfloat16))
            upstream = jnp.where(valid[:, None], out_grad[token_rows], jnp.zeros((), jnp.bfloat16))
            scales = jnp.where(valid, weights_flat[safe], jnp.zeros((), jnp.bfloat16))
            preact = jnp.dot(inputs, gate.T, preferred_element_type=jnp.float32)
            hidden = jax.nn.silu(preact).astype(jnp.bfloat16)
            outputs = jnp.dot(hidden, down, preferred_element_type=jnp.float32)
            prob_rows = jnp.sum(upstream.astype(jnp.float32) * outputs, axis=1).astype(jnp.bfloat16)
            scaled = (scales.astype(jnp.float32)[:, None] * upstream.astype(jnp.float32)).astype(jnp.bfloat16)
            hidden_grad = jnp.dot(scaled, down.T, preferred_element_type=jnp.float32)
            pre_grad = (hidden_grad * silu_slope(preact)).astype(jnp.bfloat16)
            input_grad = jnp.dot(pre_grad, gate, preferred_element_type=jnp.float32).astype(jnp.bfloat16)
            gate_term = jnp.dot(pre_grad.T, inputs, preferred_element_type=jnp.float32).astype(jnp.bfloat16)
            down_term = jnp.dot(hidden.T, scaled, preferred_element_type=jnp.float32).astype(jnp.bfloat16)
            gate_term, down_term = lax.optimization_barrier((gate_term, down_term))
            running_gate, running_down = running
            updated = (running_gate + gate_term.astype(jnp.float32), running_down + down_term.astype(jnp.float32))
            return updated, (input_grad, prob_rows)

        start = (jnp.zeros((FF, D), jnp.float32), jnp.zeros((FF, D), jnp.float32))
        summed, (input_grads, prob_rows) = lax.scan(replica_work, start, pairs)
        return summed[0].astype(jnp.bfloat16), summed[1].astype(jnp.bfloat16), input_grads, prob_rows

    gate_grad, down_grad, input_grads, prob_rows = lax.map(expert_work, (slot_pair, gate_weight, down_weight))
    flat_position = position.reshape(-1)
    pair_grads = input_grads.reshape(-1, D)[flat_position].astype(jnp.float32)
    token_grad = jnp.sum(pair_grads.reshape(TOKENS, TOP, D), axis=1).astype(jnp.bfloat16)
    route_grad = prob_rows.reshape(-1)[flat_position].reshape(TOKENS, TOP)
    return token_grad, route_grad, gate_grad, down_grad
```

```python
import functools

import jax
import jax.numpy as jnp
from jax import lax
from jax.experimental import pallas as pl
from jax.experimental.pallas import tpu as pltpu
from jax.sharding import PartitionSpec as P

MESH = pl.DeviceIdType.MESH
BF16, F32 = jnp.bfloat16, jnp.float32
LANES = 128


def placement(ids, n_exp, cap):
    rows = ids.shape[1]
    slots = n_exp * cap
    names = lax.broadcasted_iota(jnp.int32, (max(n_exp, 16), rows), 0)
    one_hot = (names == ids).astype(F32)
    before = (
        lax.broadcasted_iota(jnp.int32, (rows, rows), 0)
        < lax.broadcasted_iota(jnp.int32, (rows, rows), 1)
    ).astype(F32)
    counts = jnp.dot(one_hot.astype(BF16), before.astype(BF16), preferred_element_type=F32)
    rank = jnp.sum(counts * one_hot, axis=0, keepdims=True).astype(jnp.int32)
    target = ids * cap + rank
    match = lax.broadcasted_iota(jnp.int32, (slots, rows), 0) == target
    return match.astype(F32).astype(BF16)


def kernel(
    n_dp, n_exp, cap, pieces,
    ids_ref, tokens_ref, weights_ref, grads_ref, gate_hbm, down_hbm,
    token_out, route_out, gate_out, down_out,
    sent, got, gate, down, preact, hid_t, da_t, back, returned, right_buf, left_buf,
    load_sem, send_sem, recv_sem, back_send, back_recv, r_send, r_recv, l_send, l_recv,
    x_send, x_recv, g_send, g_recv, cut_send, cut_recv,
):
    rows, width = tokens_ref.shape
    slots = n_exp * cap
    units = gate.shape[0]
    part = units // n_dp
    piece = width // pieces
    tile = 256 if units % 256 == 0 else part
    r = lax.axis_index("dp")
    me = lax.axis_index("expert")

    def peer(k):
        return lax.rem(me + k, n_exp)

    def block(e):
        return pl.ds(pl.multiple_of(e * cap, cap), cap)

    loads = [
        pltpu.make_async_copy(gate_hbm, gate, load_sem.at[0]),
        pltpu.make_async_copy(down_hbm, down, load_sem.at[1]),
    ]
    for load in loads:
        load.start()

    barrier = pltpu.get_barrier_semaphore()

    @pl.loop(1, n_exp)
    def _(k):
        pl.semaphore_signal(barrier, inc=1, device_id={"expert": peer(k)}, device_id_type=MESH)

    up, low = lax.rem(r + 1, n_dp), lax.rem(r + n_dp - 1, n_dp)

    @pl.loop(1, n_dp)
    def _(k):
        other = lax.rem(r + k, n_dp)
        pl.semaphore_signal(barrier, inc=1, device_id={"dp": other}, device_id_type=MESH)

    place = placement(ids_ref[...], n_exp, cap)
    sent[0] = jnp.dot(place, tokens_ref[...], preferred_element_type=F32).astype(BF16)
    pl.semaphore_wait(barrier, n_exp - 1 + n_dp - 1)

    def exchange(t, k):
        to = peer(k)
        return pltpu.make_async_remote_copy(
            src_ref=sent.at[t, block(to)],
            dst_ref=got.at[t, block(me)],
            send_sem=send_sem.at[t, to],
            recv_sem=recv_sem.at[t, me],
            device_id={"expert": to},
            device_id_type=MESH,
        )

    def arrival(t, k):
        of = peer(k)
        return pltpu.make_async_remote_copy(
            src_ref=sent.at[t, block(of)],
            dst_ref=got.at[t, block(of)],
            send_sem=send_sem.at[t, of],
            recv_sem=recv_sem.at[t, of],
            device_id={"expert": of},
            device_id_type=MESH,
        )

    @pl.loop(1, n_exp)
    def _(k):
        exchange(0, k).start()

    got[0, block(me)] = sent[0, block(me)]
    weights = jnp.transpose(
        jnp.broadcast_to(weights_ref[...].astype(F32), (LANES, rows))
    )[:, 0:1]
    scaled = (weights * grads_ref[...].astype(F32)).astype(BF16)
    sent[1] = jnp.dot(place, scaled, preferred_element_type=F32).astype(BF16)

    @pl.loop(1, n_exp)
    def _(k):
        exchange(1, k).start()

    got[1, block(me)] = sent[1, block(me)]

    for load in loads:
        load.wait()

    end = jnp.logical_or(r == 0, r == n_dp - 1)
    after_end = jnp.logical_or(r == 1, r == n_dp - 2)
    inner = jnp.where(r == 0, up, low)
    lower = r < n_dp // 2

    def hand_x(e):
        return pltpu.make_async_remote_copy(
            src_ref=got.at[0, block(e)],
            dst_ref=got.at[0, pl.ds(pl.multiple_of(slots + e * cap, cap), cap)],
            send_sem=x_send.at[e],
            recv_sem=x_recv.at[e],
            device_id={"dp": inner},
            device_id_type=MESH,
        )

    def hand_g(c):
        span = pl.ds(pl.multiple_of(c * piece, piece), piece)
        return pltpu.make_async_remote_copy(
            src_ref=got.at[1, pl.ds(0, slots), span],
            dst_ref=got.at[1, pl.ds(slots, slots), span],
            send_sem=g_send.at[c],
            recv_sem=g_recv.at[c],
            device_id={"dp": inner},
            device_id_type=MESH,
        )

    def hand_cut(t, d):
        left = da_t if t == 0 else hid_t
        own = pl.ds(pl.multiple_of(d * part, part), part)
        return pltpu.make_async_remote_copy(
            src_ref=left.at[own, pl.ds(0, slots)],
            dst_ref=left.at[own, pl.ds(slots, slots)],
            send_sem=cut_send.at[t, d],
            recv_sem=cut_recv.at[t, d],
            device_id={"dp": inner},
            device_id_type=MESH,
        )

    @pl.when(end)
    def _():
        hand_x(me).start()

    @pl.loop(1, n_exp)
    def _(k):
        arrival(0, k).wait_recv()

        @pl.when(end)
        def _():
            hand_x(peer(k)).start()

    nt = (((1,), (1,)), ((), ()))

    @pl.loop(0, units // tile)
    def _(j):
        span = pl.ds(pl.multiple_of(j * tile, tile), tile)
        value = lax.dot_general(
            gate[span, :], got[0, 0:slots, :], nt, preferred_element_type=F32
        )
        preact[span, :] = value
        hid_t[span, 0:slots] = (value * jax.nn.sigmoid(value)).astype(BF16)

    def hand_cuts(t):
        @pl.when(end)
        def _():
            @pl.loop(0, n_dp - 1)
            def _(j):
                hand_cut(t, jnp.where(r == 0, n_dp - 1 - j, j)).start()

    @pl.loop(1, n_exp)
    def _(k):
        arrival(1, k).wait_recv()

    def second(j, total):
        span = pl.ds(pl.multiple_of(j * tile, tile), tile)
        slope = lax.dot_general(
            down[span, :], got[1, 0:slots, :], nt, preferred_element_type=F32
        )
        value = preact[span, :]
        sigma = jax.nn.sigmoid(value)
        da_t[span, 0:slots] = (slope * (sigma * (1.0 + value * (1.0 - sigma)))).astype(BF16)
        return total + jnp.sum(hid_t[span, 0:slots].astype(F32) * slope, axis=0, keepdims=True)

    route = lax.fori_loop(0, units // tile, second, jnp.zeros((1, slots), F32))

    hand_cuts(0)
    hand_cuts(1)

    @pl.when(end)
    def _():
        @pl.loop(0, pieces)
        def _(c):
            hand_g(c).start()

    def term(t, d, span, wide):
        left = da_t if t == 0 else hid_t
        start = d * part if isinstance(d, int) else pl.multiple_of(d * part, part)
        depth = 2 * slots if wide else slots
        return jnp.dot(
            left[pl.ds(start, part), 0:depth],
            got[t, 0:depth, span],
            preferred_element_type=F32,
        )

    def columns(c):
        return pl.ds(pl.multiple_of(c * piece, piece), piece)

    def hop(buf, s_sem, r_sem, t, d, c, to):
        return pltpu.make_async_remote_copy(
            src_ref=buf.at[t, d, c],
            dst_ref=buf.at[t, d, c],
            send_sem=s_sem.at[t, d, c],
            recv_sem=r_sem.at[t, d, c],
            device_id={"dp": to},
            device_id_type=MESH,
        )

    def rightward(t, d, c, to=None):
        return hop(right_buf, r_send, r_recv, t, d - 1, c, up)

    def leftward(t, d, c, to=None):
        return hop(left_buf, l_send, l_recv, t, d, c, low)

    def pass_on(t, d, c, copy, buf, index, first):
        @pl.when(first)
        def _():
            buf[t, index, c] = term(t, d, columns(c), True).astype(BF16)

        @pl.when(jnp.logical_not(first))
        def _():
            own = term(t, d, columns(c), False)
            copy.wait_recv()
            buf[t, index, c] = (own + buf[t, index, c].astype(F32)).astype(BF16)

        copy.start()

    def go_right(t):
        for d in range(n_dp - 1, 1, -1):

            @pl.when(r == 1)
            def _():
                hand_cut(t, d).wait_recv()

            @pl.when(jnp.logical_and(r > 0, r < d))
            def _():
                @pl.loop(0, pieces)
                def _(c):
                    if t == 1 and d == n_dp - 1:

                        @pl.when(r == 1)
                        def _():
                            hand_g(c).wait_recv()

                    pass_on(t, d, c, rightward(t, d, c), right_buf, d - 1, r == 1)

    def go_left(t):
        for d in range(n_dp - 2):

            @pl.when(r == n_dp - 2)
            def _():
                hand_cut(t, d).wait_recv()

            @pl.when(jnp.logical_and(r < n_dp - 1, r > d))
            def _():
                @pl.loop(0, pieces)
                def _(c):
                    if t == 1 and d == 0:

                        @pl.when(r == n_dp - 2)
                        def _():
                            hand_g(c).wait_recv()

                    pass_on(t, d, c, leftward(t, d, c), left_buf, d, r == n_dp - 2)

    def returning(k):
        to = peer(k)
        return pltpu.make_async_remote_copy(
            src_ref=back.at[block(to)],
            dst_ref=returned.at[block(me)],
            send_sem=back_send.at[to],
            recv_sem=back_recv.at[me],
            device_id={"expert": to},
            device_id_type=MESH,
        )

    def homecoming(k):
        of = peer(k)
        return pltpu.make_async_remote_copy(
            src_ref=back.at[block(of)],
            dst_ref=returned.at[block(of)],
            send_sem=back_send.at[of],
            recv_sem=back_recv.at[of],
            device_id={"expert": of},
            device_id_type=MESH,
        )

    def send_back():
        tn = (((0,), (0,)), ((), ()))

        @pl.loop(0, pieces)
        def _(c):
            span = columns(c)
            back[:, span] = lax.dot_general(
                da_t[:, 0:slots], gate[:, span], tn, preferred_element_type=F32
            ).astype(BF16)

        tall = jnp.transpose(jnp.broadcast_to(route, (LANES, slots)))
        high = tall.astype(BF16)
        rest = (tall - high.astype(F32)).astype(BF16)
        lane = lax.broadcasted_iota(jnp.int32, (slots, LANES), 1)
        back[:, pl.ds(width, LANES)] = jnp.where(
            lane < 1, high.astype(F32), rest.astype(F32)
        ).astype(BF16)

        @pl.loop(1, n_exp)
        def _(k):
            returning(k).start()

        returned[block(me), :] = back[block(me), :]

    send_back()

    @pl.when(after_end)
    def _():
        @pl.loop(0, n_exp)
        def _(e):
            hand_x(e).wait_recv()

    for t in range(2):

        @pl.when(lower)
        def _():
            go_right(t)

        go_left(t)

        @pl.when(jnp.logical_not(lower))
        def _():
            go_right(t)

    @pl.loop(1, n_exp)
    def _(k):
        homecoming(k).wait_recv()

    tn = (((0,), (0,)), ((), ()))

    @pl.loop(0, pieces)
    def _(c):
        span = columns(c)
        token_out[:, span] = lax.dot_general(
            place, returned[:, span], tn, preferred_element_type=F32
        ).astype(BF16)

    pair = lax.dot_general(
        place, returned[:, pl.ds(width, LANES)], tn, preferred_element_type=F32
    )
    total = jnp.broadcast_to((pair[:, 0:1] + pair[:, 1:2]) / weights, (rows, LANES))
    route_out[...] = jnp.transpose(total)[0:1, :].astype(BF16)

    for t in range(2):
        out = gate_out if t == 0 else down_out

        @pl.when(after_end)
        def _():
            hand_cut(t, r).wait_recv()

        @pl.loop(0, pieces)
        def _(c):
            span = columns(c)

            def from_right():
                hop(left_buf, l_send, l_recv, t, r, c, low).wait_recv()
                return left_buf[t, r, c].astype(F32)

            def from_left():
                hop(right_buf, r_send, r_recv, t, r - 1, c, up).wait_recv()
                return right_buf[t, r - 1, c].astype(F32)

            @pl.when(r == 0)
            def _():
                out[:, span] = (term(t, r, span, False) + from_right()).astype(BF16)

            @pl.when(r == n_dp - 1)
            def _():
                out[:, span] = (term(t, r, span, False) + from_left()).astype(BF16)

            @pl.when(r == 1)
            def _():
                out[:, span] = (term(t, r, span, True) + from_right()).astype(BF16)

            @pl.when(r == n_dp - 2)
            def _():
                out[:, span] = (term(t, r, span, True) + from_left()).astype(BF16)

            @pl.when(jnp.logical_and(r > 1, r < n_dp - 2))
            def _():
                out[:, span] = (term(t, r, span, False) + from_right() + from_left()).astype(BF16)

    @pl.loop(1, n_exp)
    def _(k):
        exchange(0, k).wait_send()
        exchange(1, k).wait_send()
        returning(k).wait_send()

    @pl.when(end)
    def _():
        @pl.loop(0, n_exp)
        def _(e):
            hand_x(e).wait_send()

        @pl.loop(0, pieces)
        def _(c):
            hand_g(c).wait_send()

        for t in range(2):

            @pl.loop(0, n_dp - 1)
            def _(j):
                hand_cut(t, jnp.where(r == 0, n_dp - 1 - j, j)).wait_send()

    for t in range(2):
        for d in range(n_dp):

            @pl.loop(0, pieces)
            def _(c):
                if d > 1:

                    @pl.when(jnp.logical_and(r > 0, r < d))
                    def _():
                        rightward(t, d, c).wait_send()

                if d < n_dp - 2:

                    @pl.when(jnp.logical_and(r < n_dp - 1, r > d))
                    def _():
                        leftward(t, d, c).wait_send()


def kernel_four(
    n_exp, cap, pieces,
    ids_ref, tokens_ref, weights_ref, grads_ref, gate_hbm, down_hbm,
    token_out, route_out, gate_out, down_out,
    sent, got_x, got_g, gate, down, preact, hid_t, da_t, back, returned,
    scaled, raw, raw_ids, far_sent, chain_out, chain_in, pair_out, pair_in,
    load_sem, send_sem, recv_sem, raw_send, raw_recv, far_send, far_recv,
    slice_send, slice_recv, cut_send, cut_recv, x_send, x_recv,
    chain_send, chain_recv, on_send, on_recv, pair_send, pair_recv, back_send, back_recv,
):
    rows, width = tokens_ref.shape
    slots = n_exp * cap
    units = gate.shape[0]
    part = units // 4
    piece = width // pieces
    tile = 256 if units % 256 == 0 else part
    r = lax.axis_index("dp")
    me = lax.axis_index("expert")
    partner = r + 1 - 2 * lax.rem(r, 2)
    far = lax.rem(r + 2, 4)
    opposite = 3 - r
    inner = jnp.logical_or(r == 1, r == 2)
    outer = jnp.logical_or(r == 0, r == 3)

    def peer(k):
        return lax.rem(me + k, n_exp)

    def block(e):
        return pl.ds(pl.multiple_of(e * cap, cap), cap)

    def far_block(e):
        return pl.ds(pl.multiple_of(slots + e * cap, cap), cap)

    def units_of(d):
        return pl.ds(pl.multiple_of(d * part, part), part)

    def columns(c):
        return pl.ds(c * piece, piece)

    near_half, far_half = (
        pl.ds(pl.multiple_of(jnp.where(cond, 0, 2 * part), part), 2 * part)
        for cond in (r < 2, r > 1)
    )
    own_rows, more_rows = pl.ds(0, slots), pl.ds(slots, slots)

    loads = [
        pltpu.make_async_copy(gate_hbm, gate, load_sem.at[0]),
        pltpu.make_async_copy(down_hbm, down, load_sem.at[1]),
    ]
    for load in loads:
        load.start()

    barrier = pltpu.get_barrier_semaphore()

    @pl.loop(1, n_exp)
    def _(k):
        pl.semaphore_signal(barrier, inc=1, device_id={"expert": peer(k)}, device_id_type=MESH)

    @pl.loop(1, 4)
    def _(k):
        other = lax.rem(r + k, 4)
        pl.semaphore_signal(barrier, inc=1, device_id={"dp": other}, device_id_type=MESH)

    def over(src, dst, s_sem, r_sem, **to):
        return pltpu.make_async_remote_copy(
            src_ref=src, dst_ref=dst, send_sem=s_sem, recv_sem=r_sem,
            device_id=to, device_id_type=MESH,
        )

    def exchange(t, to, at, device):
        got = got_g if t else got_x
        return over(
            sent.at[t, block(to)], got.at[block(at)],
            send_sem.at[t, to], recv_sem.at[t, at], expert=device,
        )

    def far_exchange(c, to, at, device):
        return over(
            far_sent.at[block(to), columns(c)], got_g.at[far_block(at), columns(c)],
            far_send.at[c, to], far_recv.at[c, at], expert=device,
        )

    def returning(to, at, device):
        return over(
            back.at[block(to)], returned.at[block(at)],
            back_send.at[to], back_recv.at[at], expert=device,
        )

    def raw_copies():
        return [
            over(ids_ref, raw_ids, raw_send.at[0], raw_recv.at[0], dp=far),
            over(scaled, raw, raw_send.at[1], raw_recv.at[1], dp=far),
        ]

    def slice_copy(half):
        return over(
            hid_t.at[half, own_rows], hid_t.at[half, more_rows], slice_send, slice_recv, dp=far
        )

    def hand_x(c):
        return over(
            got_x.at[own_rows, columns(c)], got_x.at[more_rows, columns(c)],
            x_send.at[c], x_recv.at[c], dp=partner,
        )

    def hand_cut(d):
        return over(
            da_t.at[units_of(d), own_rows], da_t.at[units_of(d), more_rows],
            cut_send.at[d], cut_recv.at[d], dp=partner,
        )

    def chain(i, c):
        return over(
            chain_out.at[i, c], chain_in.at[i, c], chain_send.at[i, c], chain_recv.at[i, c],
            dp=opposite,
        )

    def pass_on(c):
        return over(
            chain_in.at[0, c], chain_in.at[0, c], on_send.at[c], on_recv.at[c], dp=partner
        )

    def pair(c):
        return over(
            pair_out.at[c], pair_in.at[c], pair_send.at[c], pair_recv.at[c], dp=partner
        )

    place = placement(ids_ref[...], n_exp, cap)
    sent[0] = jnp.dot(place, tokens_ref[...], preferred_element_type=F32).astype(BF16)
    pl.semaphore_wait(barrier, n_exp - 1 + 3)

    @pl.loop(1, n_exp)
    def _(k):
        exchange(0, peer(k), me, peer(k)).start()

    weights = jnp.transpose(
        jnp.broadcast_to(weights_ref[...].astype(F32), (LANES, rows))
    )[:, 0:1]
    scaled[...] = (weights * grads_ref[...].astype(F32)).astype(BF16)

    @pl.when(outer)
    def _():
        for copy in raw_copies():
            copy.start()

    sent[1] = jnp.dot(place, scaled[...], preferred_element_type=F32).astype(BF16)

    @pl.loop(1, n_exp)
    def _(k):
        exchange(1, peer(k), me, peer(k)).start()

    got_x[block(me)] = sent[0, block(me)]
    got_g[block(me)] = sent[1, block(me)]

    for load in loads:
        load.wait()

    @pl.loop(1, n_exp)
    def _(k):
        exchange(0, me, peer(k), peer(k)).wait_recv()

    @pl.when(outer)
    def _():
        hand_x(0).start()

    @pl.when(inner)
    def _():
        for copy in raw_copies():
            copy.start()

    nt = (((1,), (1,)), ((), ()))
    tn = (((0,), (0,)), ((), ()))

    @pl.loop(0, units // tile)
    def _(j):
        span = pl.ds(pl.multiple_of(j * tile, tile), tile)
        value = lax.dot_general(
            gate[span, :], got_x[0:slots, :], nt, preferred_element_type=F32
        )
        preact[span, :] = value
        hid_t[span, 0:slots] = (value * jax.nn.sigmoid(value)).astype(BF16)

    slice_copy(far_half).start()

    @pl.when(outer)
    def _():
        hand_x(1).start()

    def far_dispatch():
        for copy in raw_copies():
            copy.wait_recv()
        far_place = placement(raw_ids[...], n_exp, cap)
        for c in range(pieces):
            span = columns(c)
            far_sent[:, span] = jnp.dot(
                far_place, raw[:, span], preferred_element_type=F32
            ).astype(BF16)

            @pl.loop(1, n_exp)
            def _(k):
                far_exchange(c, peer(k), me, peer(k)).start()

        got_g[far_block(me)] = far_sent[block(me)]

    @pl.when(inner)
    def _():
        far_dispatch()

    @pl.loop(1, n_exp)
    def _(k):
        exchange(1, me, peer(k), peer(k)).wait_recv()

    def second(j, total):
        span = pl.ds(pl.multiple_of(j * tile, tile), tile)
        slope = lax.dot_general(
            down[span, :], got_g[0:slots, :], nt, preferred_element_type=F32
        )
        value = preact[span, :]
        sigma = jax.nn.sigmoid(value)
        da_t[span, 0:slots] = (slope * (sigma * (1.0 + value * (1.0 - sigma)))).astype(BF16)
        return total + jnp.sum(hid_t[span, 0:slots].astype(F32) * slope, axis=0, keepdims=True)

    route = lax.fori_loop(0, units // tile, second, jnp.zeros((1, slots), F32))

    @pl.when(outer)
    def _():
        for d in (opposite, far, partner):
            hand_cut(d).start()
        for c in range(2, pieces):
            hand_x(c).start()
        far_dispatch()

    for c in range(pieces):
        span = columns(c)
        back[:, span] = lax.dot_general(
            da_t[:, 0:slots], gate[:, span], tn, preferred_element_type=F32
        ).astype(BF16)

    tall = jnp.transpose(jnp.broadcast_to(route, (LANES, slots)))
    high = tall.astype(BF16)
    rest = (tall - high.astype(F32)).astype(BF16)
    lane = lax.broadcasted_iota(jnp.int32, (slots, LANES), 1)
    back[:, pl.ds(width, LANES)] = jnp.where(
        lane < 1, high.astype(F32), rest.astype(F32)
    ).astype(BF16)

    @pl.loop(1, n_exp)
    def _(k):
        returning(peer(k), me, peer(k)).start()

    returned[block(me), :] = back[block(me), :]

    def gate_term(d, c, depth):
        return jnp.dot(
            da_t[units_of(d), 0:depth], got_x[0:depth, columns(c)], preferred_element_type=F32
        )

    def down_term(d, c):
        return jnp.dot(
            hid_t[units_of(d), :], got_g[:, columns(c)], preferred_element_type=F32
        )

    def send_pair(c):
        @pl.loop(1, n_exp)
        def _(k):
            far_exchange(c, me, peer(k), peer(k)).wait_recv()

        pair_out[c] = down_term(partner, c).astype(BF16)
        pair(c).start()

    def send_chain(i, c):
        d = opposite if i else far
        if c == 0:
            hand_cut(d).wait_recv()
        if i == 0:
            hand_x(c).wait_recv()
        chain_out[i, c] = gate_term(d, c, 2 * slots).astype(BF16)
        chain(i, c).start()

    def forward(c):
        own = gate_term(partner, c, slots)
        chain(0, c).wait_recv()
        chain_in[0, c] = (own + chain_in[0, c].astype(F32)).astype(BF16)
        pass_on(c).start()

    slice_copy(near_half).wait_recv()

    @pl.when(inner)
    def _():
        steps = [(send_pair, 0), (send_chain, 0, 0)]
        for c in range(1, pieces):
            steps += [(send_pair, c), (send_chain, 0, c), (send_chain, 1, c - 1), (forward, c - 1)]
        for step, *args in steps + [(send_chain, 1, pieces - 1)]:
            step(*args)

    @pl.when(outer)
    def _():
        for c in range(pieces):
            send_pair(c)

    @pl.loop(1, n_exp)
    def _(k):
        returning(me, peer(k), peer(k)).wait_recv()

    for c in range(pieces):
        span = columns(c)
        token_out[:, span] = lax.dot_general(
            place, returned[:, span], tn, preferred_element_type=F32
        ).astype(BF16)

    both = lax.dot_general(
        place, returned[:, pl.ds(width, LANES)], tn, preferred_element_type=F32
    )
    total = jnp.broadcast_to((both[:, 0:1] + both[:, 1:2]) / weights, (rows, LANES))
    route_out[...] = jnp.transpose(total)[0:1, :].astype(BF16)

    @pl.when(inner)
    def _():
        forward(pieces - 1)

    for c in range(pieces):
        own = down_term(r, c)
        pair(c).wait_recv()
        down_out[:, columns(c)] = (own + pair_in[c].astype(F32)).astype(BF16)

    @pl.when(inner)
    def _():
        hand_cut(r).wait_recv()
        for c in range(pieces):
            own = gate_term(r, c, 2 * slots)
            chain(1, c).wait_recv()
            gate_out[:, columns(c)] = (own + chain_in[1, c].astype(F32)).astype(BF16)

    @pl.when(outer)
    def _():
        for c in range(pieces):
            own = gate_term(r, c, slots)
            pass_on(c).wait_recv()
            gate_out[:, columns(c)] = (own + chain_in[0, c].astype(F32)).astype(BF16)

    @pl.loop(1, n_exp)
    def _(k):
        exchange(0, peer(k), me, peer(k)).wait_send()
        exchange(1, peer(k), me, peer(k)).wait_send()
        returning(peer(k), me, peer(k)).wait_send()
        for c in range(pieces):
            far_exchange(c, peer(k), me, peer(k)).wait_send()

    for copy in raw_copies():
        copy.wait_send()
    slice_copy(far_half).wait_send()
    for c in range(pieces):
        pair(c).wait_send()

    @pl.when(inner)
    def _():
        for c in range(pieces):
            chain(0, c).wait_send()
            chain(1, c).wait_send()
            pass_on(c).wait_send()

    @pl.when(outer)
    def _():
        for d in (opposite, far, partner):
            hand_cut(d).wait_send()
        for c in range(pieces):
            hand_x(c).wait_send()


def settle(*refs):
    half = len(refs) // 2
    for source, out in zip(refs[:half], refs[half:]):
        out[...] = source[...]


def chain_scratch(n_dp, n_exp, pieces, slots, units, part, width, piece, rows):
    dma = pltpu.SemaphoreType.DMA
    return [
        pltpu.VMEM((2, slots, width), BF16),
        pltpu.VMEM((2, 2 * slots, width), BF16),
        pltpu.VMEM((units, width), BF16),
        pltpu.VMEM((units, width), BF16),
        pltpu.VMEM((units, slots), F32),
        pltpu.VMEM((units, 2 * slots), BF16),
        pltpu.VMEM((units, 2 * slots), BF16),
        pltpu.VMEM((slots, width + LANES), BF16),
        pltpu.VMEM((slots, width + LANES), BF16),
        pltpu.VMEM((2, n_dp - 1, pieces, part, piece), BF16),
        pltpu.VMEM((2, n_dp - 1, pieces, part, piece), BF16),
        dma((2,)),
        dma((2, n_exp)), dma((2, n_exp)), dma((n_exp,)), dma((n_exp,)),
        dma((2, n_dp - 1, pieces)), dma((2, n_dp - 1, pieces)),
        dma((2, n_dp - 1, pieces)), dma((2, n_dp - 1, pieces)),
        dma((n_exp,)), dma((n_exp,)), dma((pieces,)), dma((pieces,)),
        dma((2, n_dp)), dma((2, n_dp)),
    ]


def four_scratch(n_dp, n_exp, pieces, slots, units, part, width, piece, rows):
    dma = pltpu.SemaphoreType.DMA
    return [
        pltpu.VMEM((2, slots, width), BF16),
        pltpu.VMEM((2 * slots, width), BF16),
        pltpu.VMEM((2 * slots, width), BF16),
        pltpu.VMEM((units, width), BF16),
        pltpu.VMEM((units, width), BF16),
        pltpu.VMEM((units, slots), F32),
        pltpu.VMEM((units, 2 * slots), BF16),
        pltpu.VMEM((units, 2 * slots), BF16),
        pltpu.VMEM((slots, width + LANES), BF16),
        pltpu.VMEM((slots, width + LANES), BF16),
        pltpu.VMEM((rows, width), BF16),
        pltpu.VMEM((rows, width), BF16),
        pltpu.VMEM((1, rows), jnp.int32),
        pltpu.VMEM((slots, width), BF16),
        pltpu.VMEM((2, pieces, part, piece), BF16),
        pltpu.VMEM((2, pieces, part, piece), BF16),
        pltpu.VMEM((pieces, part, piece), BF16),
        pltpu.VMEM((pieces, part, piece), BF16),
        dma((2,)), dma((2, n_exp)), dma((2, n_exp)), dma((2,)), dma((2,)),
        dma((pieces, n_exp)), dma((pieces, n_exp)),
        dma, dma, dma((n_dp,)), dma((n_dp,)), dma((pieces,)), dma((pieces,)),
        dma((2, pieces)), dma((2, pieces)), dma((pieces,)), dma((pieces,)),
        dma((pieces,)), dma((pieces,)), dma((n_exp,)), dma((n_exp,)),
    ]


def per_device(tokens, expert_ids, route_weights, out_grad, gate_weight, down_weight):
    rows, width = tokens.shape
    n_exp, n_dp = lax.axis_size("expert"), lax.axis_size("dp")
    top = expert_ids.shape[1]
    assert top == 1 and n_dp >= 4
    cap = -(-max(2, 2 * rows * top // n_exp) // 16) * 16
    slots = n_exp * cap
    units = gate_weight.shape[1]
    part = units // n_dp
    pieces = max(1, width // 512)
    piece = width // pieces
    vmem = pl.BlockSpec(memory_space=pltpu.VMEM)
    hbm = pl.BlockSpec(memory_space=pl.ANY)
    four = n_dp == 4
    body = (
        functools.partial(kernel_four, n_exp, cap, pieces)
        if four
        else functools.partial(kernel, n_dp, n_exp, cap, pieces)
    )
    scratch = four_scratch if four else chain_scratch
    results = pl.pallas_call(
        body,
        out_shape=(
            jax.ShapeDtypeStruct((rows, width), BF16),
            jax.ShapeDtypeStruct((1, rows), BF16),
            jax.ShapeDtypeStruct((part, width), BF16),
            jax.ShapeDtypeStruct((part, width), BF16),
        ),
        in_specs=[vmem, vmem, vmem, vmem, hbm, hbm],
        out_specs=(vmem, vmem, vmem, vmem),
        scratch_shapes=scratch(n_dp, n_exp, pieces, slots, units, part, width, piece, rows),
        compiler_params=pltpu.CompilerParams(
            collective_id=0, has_side_effects=True, vmem_limit_bytes=67_000_000
        ),
    )(
        expert_ids.reshape(1, rows), tokens, route_weights.reshape(1, rows), out_grad,
        gate_weight[0], down_weight[0],
    )
    token_grad, route_grad, gate_grad, down_grad = pl.pallas_call(
        settle,
        out_shape=tuple(jax.ShapeDtypeStruct(a.shape, a.dtype) for a in results),
        in_specs=[vmem] * 4,
        out_specs=(vmem,) * 4,
    )(*results)
    return token_grad, route_grad.reshape(rows, 1), gate_grad[None], down_grad[None]


def solution(mesh):
    placed = (
        P(("dp", "expert"), None),
        P(("dp", "expert"), None),
        P(("dp", "expert"), None),
        P(("dp", "expert"), None),
        P("expert", None, None),
        P("expert", None, None),
    )
    return jax.shard_map(
        per_device,
        mesh=mesh,
        in_specs=placed,
        out_specs=(
            P(("dp", "expert"), None),
            P(("dp", "expert"), None),
            P("expert", "dp", None),
            P("expert", "dp", None),
        ),
        check_vma=False,
    )
```

```python
import functools

import jax
import jax.numpy as jnp
from jax import lax
from jax.experimental import pallas as pl
from jax.experimental.pallas import tpu as pltpu
from jax.sharding import PartitionSpec as P

MESH = pl.DeviceIdType.MESH
BF16, F32 = jnp.bfloat16, jnp.float32
LANES = 128


def placement(ids, n_exp, cap):
    rows = ids.shape[1]
    slots = n_exp * cap
    names = lax.broadcasted_iota(jnp.int32, (max(n_exp, 16), rows), 0)
    one_hot = (names == ids).astype(F32)
    before = (
        lax.broadcasted_iota(jnp.int32, (rows, rows), 0)
        < lax.broadcasted_iota(jnp.int32, (rows, rows), 1)
    ).astype(F32)
    counts = jnp.dot(one_hot.astype(BF16), before.astype(BF16), preferred_element_type=F32)
    rank = jnp.sum(counts * one_hot, axis=0, keepdims=True).astype(jnp.int32)
    target = ids * cap + rank
    match = lax.broadcasted_iota(jnp.int32, (slots, rows), 0) == target
    return match.astype(F32).astype(BF16)


def kernel(
    n_dp, n_exp, cap, pieces,
    ids_ref, tokens_ref, weights_ref, grads_ref, gate_hbm, down_hbm,
    token_out, route_out, gate_out, down_out,
    sent, got, gate, down, preact, hid_t, da_t, back, returned, right_buf, left_buf,
    load_sem, send_sem, recv_sem, back_send, back_recv, r_send, r_recv, l_send, l_recv,
    x_send, x_recv, g_send, g_recv, cut_send, cut_recv,
):
    rows, width = tokens_ref.shape
    slots = n_exp * cap
    units = gate.shape[0]
    part = units // n_dp
    piece = width // pieces
    tile = 256 if units % 256 == 0 else part
    r = lax.axis_index("dp")
    me = lax.axis_index("expert")

    def peer(k):
        return lax.rem(me + k, n_exp)

    def block(e):
        return pl.ds(pl.multiple_of(e * cap, cap), cap)

    loads = [
        pltpu.make_async_copy(gate_hbm, gate, load_sem.at[0]),
        pltpu.make_async_copy(down_hbm, down, load_sem.at[1]),
    ]
    for load in loads:
        load.start()

    barrier = pltpu.get_barrier_semaphore()

    @pl.loop(1, n_exp)
    def _(k):
        pl.semaphore_signal(barrier, inc=1, device_id={"expert": peer(k)}, device_id_type=MESH)

    up, low = lax.rem(r + 1, n_dp), lax.rem(r + n_dp - 1, n_dp)

    @pl.loop(1, n_dp)
    def _(k):
        other = lax.rem(r + k, n_dp)
        pl.semaphore_signal(barrier, inc=1, device_id={"dp": other}, device_id_type=MESH)

    place = placement(ids_ref[...], n_exp, cap)
    sent[0] = jnp.dot(place, tokens_ref[...], preferred_element_type=F32).astype(BF16)
    pl.semaphore_wait(barrier, n_exp - 1 + n_dp - 1)

    def exchange(t, k):
        to = peer(k)
        return pltpu.make_async_remote_copy(
            src_ref=sent.at[t, block(to)],
            dst_ref=got.at[t, block(me)],
            send_sem=send_sem.at[t, to],
            recv_sem=recv_sem.at[t, me],
            device_id={"expert": to},
            device_id_type=MESH,
        )

    def arrival(t, k):
        of = peer(k)
        return pltpu.make_async_remote_copy(
            src_ref=sent.at[t, block(of)],
            dst_ref=got.at[t, block(of)],
            send_sem=send_sem.at[t, of],
            recv_sem=recv_sem.at[t, of],
            device_id={"expert": of},
            device_id_type=MESH,
        )

    @pl.loop(1, n_exp)
    def _(k):
        exchange(0, k).start()

    got[0, block(me)] = sent[0, block(me)]
    weights = jnp.transpose(
        jnp.broadcast_to(weights_ref[...].astype(F32), (LANES, rows))
    )[:, 0:1]
    scaled = (weights * grads_ref[...].astype(F32)).astype(BF16)
    sent[1] = jnp.dot(place, scaled, preferred_element_type=F32).astype(BF16)

    @pl.loop(1, n_exp)
    def _(k):
        exchange(1, k).start()

    got[1, block(me)] = sent[1, block(me)]

    for load in loads:
        load.wait()

    end = jnp.logical_or(r == 0, r == n_dp - 1)
    after_end = jnp.logical_or(r == 1, r == n_dp - 2)
    inner = jnp.where(r == 0, up, low)
    lower = r < n_dp // 2

    def hand_x(e):
        return pltpu.make_async_remote_copy(
            src_ref=got.at[0, block(e)],
            dst_ref=got.at[0, pl.ds(pl.multiple_of(slots + e * cap, cap), cap)],
            send_sem=x_send.at[e],
            recv_sem=x_recv.at[e],
            device_id={"dp": inner},
            device_id_type=MESH,
        )

    def hand_g(c):
        span = pl.ds(pl.multiple_of(c * piece, piece), piece)
        return pltpu.make_async_remote_copy(
            src_ref=got.at[1, pl.ds(0, slots), span],
            dst_ref=got.at[1, pl.ds(slots, slots), span],
            send_sem=g_send.at[c],
            recv_sem=g_recv.at[c],
            device_id={"dp": inner},
            device_id_type=MESH,
        )

    def hand_cut(t, d):
        left = da_t if t == 0 else hid_t
        own = pl.ds(pl.multiple_of(d * part, part), part)
        return pltpu.make_async_remote_copy(
            src_ref=left.at[own, pl.ds(0, slots)],
            dst_ref=left.at[own, pl.ds(slots, slots)],
            send_sem=cut_send.at[t, d],
            recv_sem=cut_recv.at[t, d],
            device_id={"dp": inner},
            device_id_type=MESH,
        )

    @pl.when(end)
    def _():
        hand_x(me).start()

    @pl.loop(1, n_exp)
    def _(k):
        arrival(0, k).wait_recv()

        @pl.when(end)
        def _():
            hand_x(peer(k)).start()

    nt = (((1,), (1,)), ((), ()))

    @pl.loop(0, units // tile)
    def _(j):
        span = pl.ds(pl.multiple_of(j * tile, tile), tile)
        value = lax.dot_general(
            gate[span, :], got[0, 0:slots, :], nt, preferred_element_type=F32
        )
        preact[span, :] = value
        hid_t[span, 0:slots] = (value * jax.nn.sigmoid(value)).astype(BF16)

    def hand_cuts(t):
        @pl.when(end)
        def _():
            @pl.loop(0, n_dp - 1)
            def _(j):
                hand_cut(t, jnp.where(r == 0, n_dp - 1 - j, j)).start()

    @pl.loop(1, n_exp)
    def _(k):
        arrival(1, k).wait_recv()

    def second(j, total):
        span = pl.ds(pl.multiple_of(j * tile, tile), tile)
        slope = lax.dot_general(
            down[span, :], got[1, 0:slots, :], nt, preferred_element_type=F32
        )
        value = preact[span, :]
        sigma = jax.nn.sigmoid(value)
        da_t[span, 0:slots] = (slope * (sigma * (1.0 + value * (1.0 - sigma)))).astype(BF16)
        return total + jnp.sum(hid_t[span, 0:slots].astype(F32) * slope, axis=0, keepdims=True)

    route = lax.fori_loop(0, units // tile, second, jnp.zeros((1, slots), F32))

    hand_cuts(0)
    hand_cuts(1)

    @pl.when(end)
    def _():
        @pl.loop(0, pieces)
        def _(c):
            hand_g(c).start()

    def term(t, d, span, wide):
        left = da_t if t == 0 else hid_t
        start = d * part if isinstance(d, int) else pl.multiple_of(d * part, part)
        depth = 2 * slots if wide else slots
        return jnp.dot(
            left[pl.ds(start, part), 0:depth],
            got[t, 0:depth, span],
            preferred_element_type=F32,
        )

    def columns(c):
        return pl.ds(pl.multiple_of(c * piece, piece), piece)

    def hop(buf, s_sem, r_sem, t, d, c, to):
        return pltpu.make_async_remote_copy(
            src_ref=buf.at[t, d, c],
            dst_ref=buf.at[t, d, c],
            send_sem=s_sem.at[t, d, c],
            recv_sem=r_sem.at[t, d, c],
            device_id={"dp": to},
            device_id_type=MESH,
        )

    def rightward(t, d, c, to=None):
        return hop(right_buf, r_send, r_recv, t, d - 1, c, up)

    def leftward(t, d, c, to=None):
        return hop(left_buf, l_send, l_recv, t, d, c, low)

    def pass_on(t, d, c, copy, buf, index, first):
        @pl.when(first)
        def _():
            buf[t, index, c] = term(t, d, columns(c), True).astype(BF16)

        @pl.when(jnp.logical_not(first))
        def _():
            own = term(t, d, columns(c), False)
            copy.wait_recv()
            buf[t, index, c] = (own + buf[t, index, c].astype(F32)).astype(BF16)

        copy.start()

    def go_right(t):
        for d in range(n_dp - 1, 1, -1):

            @pl.when(r == 1)
            def _():
                hand_cut(t, d).wait_recv()

            @pl.when(jnp.logical_and(r > 0, r < d))
            def _():
                @pl.loop(0, pieces)
                def _(c):
                    if t == 1 and d == n_dp - 1:

                        @pl.when(r == 1)
                        def _():
                            hand_g(c).wait_recv()

                    pass_on(t, d, c, rightward(t, d, c), right_buf, d - 1, r == 1)

    def go_left(t):
        for d in range(n_dp - 2):

            @pl.when(r == n_dp - 2)
            def _():
                hand_cut(t, d).wait_recv()

            @pl.when(jnp.logical_and(r < n_dp - 1, r > d))
            def _():
                @pl.loop(0, pieces)
                def _(c):
                    if t == 1 and d == 0:

                        @pl.when(r == n_dp - 2)
                        def _():
                            hand_g(c).wait_recv()

                    pass_on(t, d, c, leftward(t, d, c), left_buf, d, r == n_dp - 2)

    def returning(k):
        to = peer(k)
        return pltpu.make_async_remote_copy(
            src_ref=back.at[block(to)],
            dst_ref=returned.at[block(me)],
            send_sem=back_send.at[to],
            recv_sem=back_recv.at[me],
            device_id={"expert": to},
            device_id_type=MESH,
        )

    def homecoming(k):
        of = peer(k)
        return pltpu.make_async_remote_copy(
            src_ref=back.at[block(of)],
            dst_ref=returned.at[block(of)],
            send_sem=back_send.at[of],
            recv_sem=back_recv.at[of],
            device_id={"expert": of},
            device_id_type=MESH,
        )

    def send_back():
        tn = (((0,), (0,)), ((), ()))

        @pl.loop(0, pieces)
        def _(c):
            span = columns(c)
            back[:, span] = lax.dot_general(
                da_t[:, 0:slots], gate[:, span], tn, preferred_element_type=F32
            ).astype(BF16)

        tall = jnp.transpose(jnp.broadcast_to(route, (LANES, slots)))
        high = tall.astype(BF16)
        rest = (tall - high.astype(F32)).astype(BF16)
        lane = lax.broadcasted_iota(jnp.int32, (slots, LANES), 1)
        back[:, pl.ds(width, LANES)] = jnp.where(
            lane < 1, high.astype(F32), rest.astype(F32)
        ).astype(BF16)

        @pl.loop(1, n_exp)
        def _(k):
            returning(k).start()

        returned[block(me), :] = back[block(me), :]

    send_back()

    @pl.when(after_end)
    def _():
        @pl.loop(0, n_exp)
        def _(e):
            hand_x(e).wait_recv()

    for t in range(2):

        @pl.when(lower)
        def _():
            go_right(t)

        go_left(t)

        @pl.when(jnp.logical_not(lower))
        def _():
            go_right(t)

    @pl.loop(1, n_exp)
    def _(k):
        homecoming(k).wait_recv()

    tn = (((0,), (0,)), ((), ()))

    @pl.loop(0, pieces)
    def _(c):
        span = columns(c)
        token_out[:, span] = lax.dot_general(
            place, returned[:, span], tn, preferred_element_type=F32
        ).astype(BF16)

    pair = lax.dot_general(
        place, returned[:, pl.ds(width, LANES)], tn, preferred_element_type=F32
    )
    total = jnp.broadcast_to((pair[:, 0:1] + pair[:, 1:2]) / weights, (rows, LANES))
    route_out[...] = jnp.transpose(total)[0:1, :].astype(BF16)

    for t in range(2):
        out = gate_out if t == 0 else down_out

        @pl.when(after_end)
        def _():
            hand_cut(t, r).wait_recv()

        @pl.loop(0, pieces)
        def _(c):
            span = columns(c)

            def from_right():
                hop(left_buf, l_send, l_recv, t, r, c, low).wait_recv()
                return left_buf[t, r, c].astype(F32)

            def from_left():
                hop(right_buf, r_send, r_recv, t, r - 1, c, up).wait_recv()
                return right_buf[t, r - 1, c].astype(F32)

            @pl.when(r == 0)
            def _():
                out[:, span] = (term(t, r, span, False) + from_right()).astype(BF16)

            @pl.when(r == n_dp - 1)
            def _():
                out[:, span] = (term(t, r, span, False) + from_left()).astype(BF16)

            @pl.when(r == 1)
            def _():
                out[:, span] = (term(t, r, span, True) + from_right()).astype(BF16)

            @pl.when(r == n_dp - 2)
            def _():
                out[:, span] = (term(t, r, span, True) + from_left()).astype(BF16)

            @pl.when(jnp.logical_and(r > 1, r < n_dp - 2))
            def _():
                out[:, span] = (term(t, r, span, False) + from_right() + from_left()).astype(BF16)

    @pl.loop(1, n_exp)
    def _(k):
        exchange(0, k).wait_send()
        exchange(1, k).wait_send()
        returning(k).wait_send()

    @pl.when(end)
    def _():
        @pl.loop(0, n_exp)
        def _(e):
            hand_x(e).wait_send()

        @pl.loop(0, pieces)
        def _(c):
            hand_g(c).wait_send()

        for t in range(2):

            @pl.loop(0, n_dp - 1)
            def _(j):
                hand_cut(t, jnp.where(r == 0, n_dp - 1 - j, j)).wait_send()

    for t in range(2):
        for d in range(n_dp):

            @pl.loop(0, pieces)
            def _(c):
                if d > 1:

                    @pl.when(jnp.logical_and(r > 0, r < d))
                    def _():
                        rightward(t, d, c).wait_send()

                if d < n_dp - 2:

                    @pl.when(jnp.logical_and(r < n_dp - 1, r > d))
                    def _():
                        leftward(t, d, c).wait_send()


def kernel_four(
    n_exp, cap, pieces,
    ids_hbm, tokens_hbm, weights_hbm, grads_hbm, gate_hbm, down_hbm,
    token_out, route_out, gate_out, down_out,
    ids_ref, tokens_ref, weights_ref, grads_ref,
    sent, got_x, got_g, gate, down, preact, hid_t, da_t, back, returned,
    scaled, raw, raw_ids, far_sent, chain_out, chain_in, pair_out, pair_in,
    load_sem, send_sem, recv_sem, raw_send, raw_recv, far_send, far_recv,
    slice_send, slice_recv, cut_send, cut_recv, x_send, x_recv,
    chain_send, chain_recv, on_send, on_recv, pair_send, pair_recv, back_send, back_recv,
):
    rows, width = tokens_ref.shape
    slots = n_exp * cap
    units = gate.shape[0]
    part = units // 4
    piece = width // pieces
    tile = 256 if units % 256 == 0 else part
    r = lax.axis_index("dp")
    me = lax.axis_index("expert")
    partner = r + 1 - 2 * lax.rem(r, 2)
    far = lax.rem(r + 2, 4)
    opposite = 3 - r
    inner = jnp.logical_or(r == 1, r == 2)
    outer = jnp.logical_or(r == 0, r == 3)

    def peer(k):
        return lax.rem(me + k, n_exp)

    def block(e):
        return pl.ds(pl.multiple_of(e * cap, cap), cap)

    def far_block(e):
        return pl.ds(pl.multiple_of(slots + e * cap, cap), cap)

    def units_of(d):
        return pl.ds(pl.multiple_of(d * part, part), part)

    def columns(c):
        return pl.ds(c * piece, piece)

    near_half, far_half = (
        pl.ds(pl.multiple_of(jnp.where(cond, 0, 2 * part), part), 2 * part)
        for cond in (r < 2, r > 1)
    )
    own_rows, more_rows = pl.ds(0, slots), pl.ds(slots, slots)

    loads = [
        pltpu.make_async_copy(source, held, load_sem.at[i])
        for i, (source, held) in enumerate((
            (ids_hbm, ids_ref), (tokens_hbm, tokens_ref), (weights_hbm, weights_ref),
            (grads_hbm, grads_ref),
            (gate_hbm, gate), (down_hbm, down),
        ))
    ]
    for load in loads[:4]:
        load.start()

    barrier = pltpu.get_barrier_semaphore()

    @pl.loop(1, n_exp)
    def _(k):
        pl.semaphore_signal(barrier, inc=1, device_id={"expert": peer(k)}, device_id_type=MESH)

    @pl.loop(1, 4)
    def _(k):
        other = lax.rem(r + k, 4)
        pl.semaphore_signal(barrier, inc=1, device_id={"dp": other}, device_id_type=MESH)

    for load in loads[4:]:
        load.start()

    def over(src, dst, s_sem, r_sem, **to):
        return pltpu.make_async_remote_copy(
            src_ref=src, dst_ref=dst, send_sem=s_sem, recv_sem=r_sem,
            device_id=to, device_id_type=MESH,
        )

    def exchange(t, to, at, device):
        got = got_g if t else got_x
        return over(
            sent.at[t, block(to)], got.at[block(at)],
            send_sem.at[t, to], recv_sem.at[t, at], expert=device,
        )

    def far_exchange(c, to, at, device):
        return over(
            far_sent.at[block(to), columns(c)], got_g.at[far_block(at), columns(c)],
            far_send.at[c, to], far_recv.at[c, at], expert=device,
        )

    def returning(to, at, device):
        return over(
            back.at[block(to)], returned.at[block(at)],
            back_send.at[to], back_recv.at[at], expert=device,
        )

    def raw_copies():
        return [
            over(ids_ref, raw_ids, raw_send.at[0], raw_recv.at[0], dp=far),
            over(scaled, raw, raw_send.at[1], raw_recv.at[1], dp=far),
        ]

    def slice_copy(half):
        return over(
            hid_t.at[half, own_rows], hid_t.at[half, more_rows], slice_send, slice_recv, dp=far
        )

    def hand_x(c):
        return over(
            got_x.at[own_rows, columns(c)], got_x.at[more_rows, columns(c)],
            x_send.at[c], x_recv.at[c], dp=partner,
        )

    def hand_cut(d):
        return over(
            da_t.at[units_of(d), own_rows], da_t.at[units_of(d), more_rows],
            cut_send.at[d], cut_recv.at[d], dp=partner,
        )

    def chain(i, c):
        return over(
            chain_out.at[i, c], chain_in.at[i, c], chain_send.at[i, c], chain_recv.at[i, c],
            dp=opposite,
        )

    def pass_on(c):
        return over(
            chain_in.at[0, c], chain_in.at[0, c], on_send.at[c], on_recv.at[c], dp=partner
        )

    def pair(c):
        return over(
            pair_out.at[c], pair_in.at[c], pair_send.at[c], pair_recv.at[c], dp=partner
        )

    loads[0].wait()
    place = placement(ids_ref[...], n_exp, cap)
    loads[1].wait()
    sent[0] = jnp.dot(place, tokens_ref[...], preferred_element_type=F32).astype(BF16)
    pl.semaphore_wait(barrier, n_exp - 1 + 3)

    @pl.loop(1, n_exp)
    def _(k):
        exchange(0, peer(k), me, peer(k)).start()

    loads[2].wait()
    weights = jnp.transpose(
        jnp.broadcast_to(weights_ref[...].astype(F32), (LANES, rows))
    )[:, 0:1]
    loads[3].wait()
    scaled[...] = (weights * grads_ref[...].astype(F32)).astype(BF16)

    @pl.when(outer)
    def _():
        for copy in raw_copies():
            copy.start()

    sent[1] = jnp.dot(place, scaled[...], preferred_element_type=F32).astype(BF16)

    @pl.loop(1, n_exp)
    def _(k):
        exchange(1, peer(k), me, peer(k)).start()

    got_x[block(me)] = sent[0, block(me)]
    got_g[block(me)] = sent[1, block(me)]

    for load in loads[4:]:
        load.wait()

    @pl.loop(1, n_exp)
    def _(k):
        exchange(0, me, peer(k), peer(k)).wait_recv()

    @pl.when(outer)
    def _():
        hand_x(0).start()

    @pl.when(inner)
    def _():
        for copy in raw_copies():
            copy.start()

    nt = (((1,), (1,)), ((), ()))
    tn = (((0,), (0,)), ((), ()))

    @pl.loop(0, units // tile)
    def _(j):
        span = pl.ds(pl.multiple_of(j * tile, tile), tile)
        value = lax.dot_general(
            gate[span, :], got_x[0:slots, :], nt, preferred_element_type=F32
        )
        preact[span, :] = value
        hid_t[span, 0:slots] = (value * jax.nn.sigmoid(value)).astype(BF16)

    @pl.when(outer)
    def _():
        hand_x(1).start()

    @pl.when(inner)
    def _():
        slice_copy(far_half).start()

    def far_dispatch():
        for copy in raw_copies():
            copy.wait_recv()
        far_place = placement(raw_ids[...], n_exp, cap)
        for c in range(pieces):
            span = columns(c)
            far_sent[:, span] = jnp.dot(
                far_place, raw[:, span], preferred_element_type=F32
            ).astype(BF16)

            @pl.loop(1, n_exp)
            def _(k):
                far_exchange(c, peer(k), me, peer(k)).start()

        got_g[far_block(me)] = far_sent[block(me)]

    @pl.when(inner)
    def _():
        far_dispatch()

    @pl.loop(1, n_exp)
    def _(k):
        exchange(1, me, peer(k), peer(k)).wait_recv()

    @pl.when(outer)
    def _():
        slice_copy(far_half).start()

    def second(j, total):
        span = pl.ds(pl.multiple_of(j * tile, tile), tile)
        slope = lax.dot_general(
            down[span, :], got_g[0:slots, :], nt, preferred_element_type=F32
        )
        value = preact[span, :]
        sigma = jax.nn.sigmoid(value)
        da_t[span, 0:slots] = (slope * (sigma * (1.0 + value * (1.0 - sigma)))).astype(BF16)
        return total + jnp.sum(hid_t[span, 0:slots].astype(F32) * slope, axis=0, keepdims=True)

    route = lax.fori_loop(0, units // tile, second, jnp.zeros((1, slots), F32))

    @pl.when(outer)
    def _():
        for d in (opposite, far, partner):
            hand_cut(d).start()
        for c in range(2, pieces):
            hand_x(c).start()
        far_dispatch()

    for c in range(pieces):
        span = columns(c)
        back[:, span] = lax.dot_general(
            da_t[:, 0:slots], gate[:, span], tn, preferred_element_type=F32
        ).astype(BF16)

    tall = jnp.transpose(jnp.broadcast_to(route, (LANES, slots)))
    high = tall.astype(BF16)
    rest = (tall - high.astype(F32)).astype(BF16)
    lane = lax.broadcasted_iota(jnp.int32, (slots, LANES), 1)
    back[:, pl.ds(width, LANES)] = jnp.where(
        lane < 1, high.astype(F32), rest.astype(F32)
    ).astype(BF16)

    @pl.loop(1, n_exp)
    def _(k):
        returning(peer(k), me, peer(k)).start()

    returned[block(me), :] = back[block(me), :]

    def gate_term(d, c, depth):
        return jnp.dot(
            da_t[units_of(d), 0:depth], got_x[0:depth, columns(c)], preferred_element_type=F32
        )

    def down_term(d, c):
        return jnp.dot(
            hid_t[units_of(d), :], got_g[:, columns(c)], preferred_element_type=F32
        )

    def send_pair(c):
        @pl.loop(1, n_exp)
        def _(k):
            far_exchange(c, me, peer(k), peer(k)).wait_recv()

        pair_out[c] = down_term(partner, c).astype(BF16)
        pair(c).start()

    def send_chain(i, c):
        d = opposite if i else far
        if c == 0:
            hand_cut(d).wait_recv()
        if i == 0:
            hand_x(c).wait_recv()
        chain_out[i, c] = gate_term(d, c, 2 * slots).astype(BF16)
        chain(i, c).start()

    def forward(c):
        own = gate_term(partner, c, slots)
        chain(0, c).wait_recv()
        chain_in[0, c] = (own + chain_in[0, c].astype(F32)).astype(BF16)
        pass_on(c).start()

    slice_copy(near_half).wait_recv()

    @pl.when(inner)
    def _():
        steps = [(send_pair, 0), (send_chain, 0, 0)]
        for c in range(1, pieces):
            steps += [(send_pair, c), (send_chain, 0, c), (send_chain, 1, c - 1), (forward, c - 1)]
        for step, *args in steps + [(send_chain, 1, pieces - 1)]:
            step(*args)

    @pl.when(outer)
    def _():
        for c in range(pieces):
            send_pair(c)

    @pl.loop(1, n_exp)
    def _(k):
        returning(me, peer(k), peer(k)).wait_recv()

    for c in range(pieces):
        span = columns(c)
        token_out[:, span] = lax.dot_general(
            place, returned[:, span], tn, preferred_element_type=F32
        ).astype(BF16)

    both = lax.dot_general(
        place, returned[:, pl.ds(width, LANES)], tn, preferred_element_type=F32
    )
    total = jnp.broadcast_to((both[:, 0:1] + both[:, 1:2]) / weights, (rows, LANES))
    route_out[...] = jnp.transpose(total)[0:1, :].astype(BF16)

    @pl.when(inner)
    def _():
        forward(pieces - 1)

    for c in range(pieces):
        own = down_term(r, c)
        pair(c).wait_recv()
        down_out[:, columns(c)] = (own + pair_in[c].astype(F32)).astype(BF16)

    @pl.when(inner)
    def _():
        hand_cut(r).wait_recv()
        for c in range(pieces):
            own = gate_term(r, c, 2 * slots)
            chain(1, c).wait_recv()
            gate_out[:, columns(c)] = (own + chain_in[1, c].astype(F32)).astype(BF16)

    @pl.when(outer)
    def _():
        for c in range(pieces):
            own = gate_term(r, c, slots)
            pass_on(c).wait_recv()
            gate_out[:, columns(c)] = (own + chain_in[0, c].astype(F32)).astype(BF16)

    @pl.loop(1, n_exp)
    def _(k):
        exchange(0, peer(k), me, peer(k)).wait_send()
        exchange(1, peer(k), me, peer(k)).wait_send()
        returning(peer(k), me, peer(k)).wait_send()
        for c in range(pieces):
            far_exchange(c, peer(k), me, peer(k)).wait_send()

    for copy in raw_copies():
        copy.wait_send()
    slice_copy(far_half).wait_send()
    for c in range(pieces):
        pair(c).wait_send()

    @pl.when(inner)
    def _():
        for c in range(pieces):
            chain(0, c).wait_send()
            chain(1, c).wait_send()
            pass_on(c).wait_send()

    @pl.when(outer)
    def _():
        for d in (opposite, far, partner):
            hand_cut(d).wait_send()
        for c in range(pieces):
            hand_x(c).wait_send()


def settle(token, route, gate, down, token_out, route_out, gate_out, down_out, sems):
    copies = [
        pltpu.make_async_copy(source, out, sems.at[i])
        for i, (source, out) in enumerate((
            (gate, gate_out), (down, down_out), (token, token_out), (route, route_out),
        ))
    ]
    for copy in copies:
        copy.start()
    for copy in copies:
        copy.wait()


def chain_scratch(n_dp, n_exp, pieces, slots, units, part, width, piece, rows):
    dma = pltpu.SemaphoreType.DMA
    return [
        pltpu.VMEM((2, slots, width), BF16),
        pltpu.VMEM((2, 2 * slots, width), BF16),
        pltpu.VMEM((units, width), BF16),
        pltpu.VMEM((units, width), BF16),
        pltpu.VMEM((units, slots), F32),
        pltpu.VMEM((units, 2 * slots), BF16),
        pltpu.VMEM((units, 2 * slots), BF16),
        pltpu.VMEM((slots, width + LANES), BF16),
        pltpu.VMEM((slots, width + LANES), BF16),
        pltpu.VMEM((2, n_dp - 1, pieces, part, piece), BF16),
        pltpu.VMEM((2, n_dp - 1, pieces, part, piece), BF16),
        dma((2,)),
        dma((2, n_exp)), dma((2, n_exp)), dma((n_exp,)), dma((n_exp,)),
        dma((2, n_dp - 1, pieces)), dma((2, n_dp - 1, pieces)),
        dma((2, n_dp - 1, pieces)), dma((2, n_dp - 1, pieces)),
        dma((n_exp,)), dma((n_exp,)), dma((pieces,)), dma((pieces,)),
        dma((2, n_dp)), dma((2, n_dp)),
    ]


def four_scratch(n_dp, n_exp, pieces, slots, units, part, width, piece, rows):
    dma = pltpu.SemaphoreType.DMA
    return [
        pltpu.VMEM((1, rows), jnp.int32),
        pltpu.VMEM((rows, width), BF16),
        pltpu.VMEM((1, rows), BF16),
        pltpu.VMEM((rows, width), BF16),
        pltpu.VMEM((2, slots, width), BF16),
        pltpu.VMEM((2 * slots, width), BF16),
        pltpu.VMEM((2 * slots, width), BF16),
        pltpu.VMEM((units, width), BF16),
        pltpu.VMEM((units, width), BF16),
        pltpu.VMEM((units, slots), F32),
        pltpu.VMEM((units, 2 * slots), BF16),
        pltpu.VMEM((units, 2 * slots), BF16),
        pltpu.VMEM((slots, width + LANES), BF16),
        pltpu.VMEM((slots, width + LANES), BF16),
        pltpu.VMEM((rows, width), BF16),
        pltpu.VMEM((rows, width), BF16),
        pltpu.VMEM((1, rows), jnp.int32),
        pltpu.VMEM((slots, width), BF16),
        pltpu.VMEM((2, pieces, part, piece), BF16),
        pltpu.VMEM((2, pieces, part, piece), BF16),
        pltpu.VMEM((pieces, part, piece), BF16),
        pltpu.VMEM((pieces, part, piece), BF16),
        dma((6,)), dma((2, n_exp)), dma((2, n_exp)), dma((2,)), dma((2,)),
        dma((pieces, n_exp)), dma((pieces, n_exp)),
        dma, dma, dma((n_dp,)), dma((n_dp,)), dma((pieces,)), dma((pieces,)),
        dma((2, pieces)), dma((2, pieces)), dma((pieces,)), dma((pieces,)),
        dma((pieces,)), dma((pieces,)), dma((n_exp,)), dma((n_exp,)),
    ]


def per_device(tokens, expert_ids, route_weights, out_grad, gate_weight, down_weight):
    rows, width = tokens.shape
    n_exp, n_dp = lax.axis_size("expert"), lax.axis_size("dp")
    top = expert_ids.shape[1]
    assert top == 1 and n_dp >= 4
    cap = -(-max(2, 2 * rows * top // n_exp) // 16) * 16
    slots = n_exp * cap
    units = gate_weight.shape[1]
    part = units // n_dp
    pieces = max(1, width // 512)
    piece = width // pieces
    shapes = (
        jax.ShapeDtypeStruct((rows, width), BF16),
        jax.ShapeDtypeStruct((1, rows), BF16),
        jax.ShapeDtypeStruct((part, width), BF16),
        jax.ShapeDtypeStruct((part, width), BF16),
    )
    vmem = pl.BlockSpec(memory_space=pltpu.VMEM)
    hbm = pl.BlockSpec(memory_space=pl.ANY)
    four = n_dp == 4
    body = (
        functools.partial(kernel_four, n_exp, cap, pieces)
        if four
        else functools.partial(kernel, n_dp, n_exp, cap, pieces)
    )
    scratch = four_scratch if four else chain_scratch
    results = pl.pallas_call(
        body,
        out_shape=tuple(pltpu.VMEM(a.shape, a.dtype) for a in shapes) if four else shapes,
        in_specs=[hbm] * 6 if four else [vmem] * 4 + [hbm] * 2,
        out_specs=(vmem,) * 4,
        scratch_shapes=scratch(n_dp, n_exp, pieces, slots, units, part, width, piece, rows),
        compiler_params=pltpu.CompilerParams(
            collective_id=0, has_side_effects=True,
            vmem_limit_bytes=60_000_000 if four else 67_000_000,

        ),
    )(
        expert_ids.reshape(1, rows), tokens, route_weights.reshape(1, rows), out_grad,
        gate_weight[0], down_weight[0],
    )
    if four:
        results = [pltpu.with_memory_space_constraint(a, pltpu.VMEM) for a in results]
    token_grad, route_grad, gate_grad, down_grad = pl.pallas_call(
        settle,
        out_shape=shapes,
        in_specs=[vmem] * 4,
        out_specs=(hbm,) * 4,
        scratch_shapes=[pltpu.SemaphoreType.DMA((4,))],
    )(*results)
    return token_grad, route_grad.reshape(rows, 1), gate_grad[None], down_grad[None]


def solution(mesh):
    placed = (
        P(("dp", "expert"), None),
        P(("dp", "expert"), None),
        P(("dp", "expert"), None),
        P(("dp", "expert"), None),
        P("expert", None, None),
        P("expert", None, None),
    )
    return jax.shard_map(
        per_device,
        mesh=mesh,
        in_specs=placed,
        out_specs=(
            P(("dp", "expert"), None),
            P(("dp", "expert"), None),
            P("expert", "dp", None),
            P("expert", "dp", None),
        ),
        check_vma=False,
    )
```

```python
import functools

import jax
import jax.numpy as jnp
from jax import lax
from jax.experimental import pallas as pl
from jax.experimental.pallas import tpu as pltpu
from jax.sharding import PartitionSpec as P

MESH = pl.DeviceIdType.MESH
BF16, F32 = jnp.bfloat16, jnp.float32
LANES = 128


def placement(ids, n_exp, cap):
    rows = ids.shape[1]
    slots = n_exp * cap
    names = lax.broadcasted_iota(jnp.int32, (max(n_exp, 16), rows), 0)
    one_hot = (names == ids).astype(F32)
    before = (
        lax.broadcasted_iota(jnp.int32, (rows, rows), 0)
        < lax.broadcasted_iota(jnp.int32, (rows, rows), 1)
    ).astype(F32)
    counts = jnp.dot(one_hot.astype(BF16), before.astype(BF16), preferred_element_type=F32)
    rank = jnp.sum(counts * one_hot, axis=0, keepdims=True).astype(jnp.int32)
    target = ids * cap + rank
    match = lax.broadcasted_iota(jnp.int32, (slots, rows), 0) == target
    return match.astype(F32).astype(BF16)


def kernel(
    n_dp, n_exp, cap, pieces,
    ids_ref, tokens_ref, weights_ref, grads_ref, gate_hbm, down_hbm,
    token_out, route_out, gate_out, down_out,
    sent, got, gate, down, preact, hid_t, da_t, back, returned, right_buf, left_buf,
    load_sem, send_sem, recv_sem, back_send, back_recv, r_send, r_recv, l_send, l_recv,
    x_send, x_recv, g_send, g_recv, cut_send, cut_recv,
):
    rows, width = tokens_ref.shape
    slots = n_exp * cap
    units = gate.shape[0]
    part = units // n_dp
    piece = width // pieces
    tile = 256 if units % 256 == 0 else part
    r = lax.axis_index("dp")
    me = lax.axis_index("expert")

    def peer(k):
        return lax.rem(me + k, n_exp)

    def block(e):
        return pl.ds(pl.multiple_of(e * cap, cap), cap)

    loads = [
        pltpu.make_async_copy(gate_hbm, gate, load_sem.at[0]),
        pltpu.make_async_copy(down_hbm, down, load_sem.at[1]),
    ]
    for load in loads:
        load.start()

    barrier = pltpu.get_barrier_semaphore()

    @pl.loop(1, n_exp)
    def _(k):
        pl.semaphore_signal(barrier, inc=1, device_id={"expert": peer(k)}, device_id_type=MESH)

    up, low = lax.rem(r + 1, n_dp), lax.rem(r + n_dp - 1, n_dp)

    @pl.loop(1, n_dp)
    def _(k):
        other = lax.rem(r + k, n_dp)
        pl.semaphore_signal(barrier, inc=1, device_id={"dp": other}, device_id_type=MESH)

    place = placement(ids_ref[...], n_exp, cap)
    sent[0] = jnp.dot(place, tokens_ref[...], preferred_element_type=F32).astype(BF16)
    pl.semaphore_wait(barrier, n_exp - 1 + n_dp - 1)

    def exchange(t, k):
        to = peer(k)
        return pltpu.make_async_remote_copy(
            src_ref=sent.at[t, block(to)],
            dst_ref=got.at[t, block(me)],
            send_sem=send_sem.at[t, to],
            recv_sem=recv_sem.at[t, me],
            device_id={"expert": to},
            device_id_type=MESH,
        )

    def arrival(t, k):
        of = peer(k)
        return pltpu.make_async_remote_copy(
            src_ref=sent.at[t, block(of)],
            dst_ref=got.at[t, block(of)],
            send_sem=send_sem.at[t, of],
            recv_sem=recv_sem.at[t, of],
            device_id={"expert": of},
            device_id_type=MESH,
        )

    @pl.loop(1, n_exp)
    def _(k):
        exchange(0, k).start()

    got[0, block(me)] = sent[0, block(me)]
    weights = jnp.transpose(
        jnp.broadcast_to(weights_ref[...].astype(F32), (LANES, rows))
    )[:, 0:1]
    scaled = (weights * grads_ref[...].astype(F32)).astype(BF16)
    sent[1] = jnp.dot(place, scaled, preferred_element_type=F32).astype(BF16)

    @pl.loop(1, n_exp)
    def _(k):
        exchange(1, k).start()

    got[1, block(me)] = sent[1, block(me)]

    for load in loads:
        load.wait()

    end = jnp.logical_or(r == 0, r == n_dp - 1)
    after_end = jnp.logical_or(r == 1, r == n_dp - 2)
    inner = jnp.where(r == 0, up, low)
    lower = r < n_dp // 2

    def hand_x(e):
        return pltpu.make_async_remote_copy(
            src_ref=got.at[0, block(e)],
            dst_ref=got.at[0, pl.ds(pl.multiple_of(slots + e * cap, cap), cap)],
            send_sem=x_send.at[e],
            recv_sem=x_recv.at[e],
            device_id={"dp": inner},
            device_id_type=MESH,
        )

    def hand_g(c):
        span = pl.ds(pl.multiple_of(c * piece, piece), piece)
        return pltpu.make_async_remote_copy(
            src_ref=got.at[1, pl.ds(0, slots), span],
            dst_ref=got.at[1, pl.ds(slots, slots), span],
            send_sem=g_send.at[c],
            recv_sem=g_recv.at[c],
            device_id={"dp": inner},
            device_id_type=MESH,
        )

    def hand_cut(t, d):
        left = da_t if t == 0 else hid_t
        own = pl.ds(pl.multiple_of(d * part, part), part)
        return pltpu.make_async_remote_copy(
            src_ref=left.at[own, pl.ds(0, slots)],
            dst_ref=left.at[own, pl.ds(slots, slots)],
            send_sem=cut_send.at[t, d],
            recv_sem=cut_recv.at[t, d],
            device_id={"dp": inner},
            device_id_type=MESH,
        )

    @pl.when(end)
    def _():
        hand_x(me).start()

    @pl.loop(1, n_exp)
    def _(k):
        arrival(0, k).wait_recv()

        @pl.when(end)
        def _():
            hand_x(peer(k)).start()

    nt = (((1,), (1,)), ((), ()))

    @pl.loop(0, units // tile)
    def _(j):
        span = pl.ds(pl.multiple_of(j * tile, tile), tile)
        value = lax.dot_general(
            gate[span, :], got[0, 0:slots, :], nt, preferred_element_type=F32
        )
        preact[span, :] = value
        hid_t[span, 0:slots] = (value * jax.nn.sigmoid(value)).astype(BF16)

    def hand_cuts(t):
        @pl.when(end)
        def _():
            @pl.loop(0, n_dp - 1)
            def _(j):
                hand_cut(t, jnp.where(r == 0, n_dp - 1 - j, j)).start()

    @pl.loop(1, n_exp)
    def _(k):
        arrival(1, k).wait_recv()

    def second(j, total):
        span = pl.ds(pl.multiple_of(j * tile, tile), tile)
        slope = lax.dot_general(
            down[span, :], got[1, 0:slots, :], nt, preferred_element_type=F32
        )
        value = preact[span, :]
        sigma = jax.nn.sigmoid(value)
        da_t[span, 0:slots] = (slope * (sigma * (1.0 + value * (1.0 - sigma)))).astype(BF16)
        return total + jnp.sum(hid_t[span, 0:slots].astype(F32) * slope, axis=0, keepdims=True)

    route = lax.fori_loop(0, units // tile, second, jnp.zeros((1, slots), F32))

    hand_cuts(0)
    hand_cuts(1)

    @pl.when(end)
    def _():
        @pl.loop(0, pieces)
        def _(c):
            hand_g(c).start()

    def term(t, d, span, wide):
        left = da_t if t == 0 else hid_t
        start = d * part if isinstance(d, int) else pl.multiple_of(d * part, part)
        depth = 2 * slots if wide else slots
        return jnp.dot(
            left[pl.ds(start, part), 0:depth],
            got[t, 0:depth, span],
            preferred_element_type=F32,
        )

    def columns(c):
        return pl.ds(pl.multiple_of(c * piece, piece), piece)

    def hop(buf, s_sem, r_sem, t, d, c, to):
        return pltpu.make_async_remote_copy(
            src_ref=buf.at[t, d, c],
            dst_ref=buf.at[t, d, c],
            send_sem=s_sem.at[t, d, c],
            recv_sem=r_sem.at[t, d, c],
            device_id={"dp": to},
            device_id_type=MESH,
        )

    def rightward(t, d, c, to=None):
        return hop(right_buf, r_send, r_recv, t, d - 1, c, up)

    def leftward(t, d, c, to=None):
        return hop(left_buf, l_send, l_recv, t, d, c, low)

    def pass_on(t, d, c, copy, buf, index, first):
        @pl.when(first)
        def _():
            buf[t, index, c] = term(t, d, columns(c), True).astype(BF16)

        @pl.when(jnp.logical_not(first))
        def _():
            own = term(t, d, columns(c), False)
            copy.wait_recv()
            buf[t, index, c] = (own + buf[t, index, c].astype(F32)).astype(BF16)

        copy.start()

    def go_right(t):
        for d in range(n_dp - 1, 1, -1):

            @pl.when(r == 1)
            def _():
                hand_cut(t, d).wait_recv()

            @pl.when(jnp.logical_and(r > 0, r < d))
            def _():
                @pl.loop(0, pieces)
                def _(c):
                    if t == 1 and d == n_dp - 1:

                        @pl.when(r == 1)
                        def _():
                            hand_g(c).wait_recv()

                    pass_on(t, d, c, rightward(t, d, c), right_buf, d - 1, r == 1)

    def go_left(t):
        for d in range(n_dp - 2):

            @pl.when(r == n_dp - 2)
            def _():
                hand_cut(t, d).wait_recv()

            @pl.when(jnp.logical_and(r < n_dp - 1, r > d))
            def _():
                @pl.loop(0, pieces)
                def _(c):
                    if t == 1 and d == 0:

                        @pl.when(r == n_dp - 2)
                        def _():
                            hand_g(c).wait_recv()

                    pass_on(t, d, c, leftward(t, d, c), left_buf, d, r == n_dp - 2)

    def returning(k):
        to = peer(k)
        return pltpu.make_async_remote_copy(
            src_ref=back.at[block(to)],
            dst_ref=returned.at[block(me)],
            send_sem=back_send.at[to],
            recv_sem=back_recv.at[me],
            device_id={"expert": to},
            device_id_type=MESH,
        )

    def homecoming(k):
        of = peer(k)
        return pltpu.make_async_remote_copy(
            src_ref=back.at[block(of)],
            dst_ref=returned.at[block(of)],
            send_sem=back_send.at[of],
            recv_sem=back_recv.at[of],
            device_id={"expert": of},
            device_id_type=MESH,
        )

    def send_back():
        tn = (((0,), (0,)), ((), ()))

        @pl.loop(0, pieces)
        def _(c):
            span = columns(c)
            back[:, span] = lax.dot_general(
                da_t[:, 0:slots], gate[:, span], tn, preferred_element_type=F32
            ).astype(BF16)

        tall = jnp.transpose(jnp.broadcast_to(route, (LANES, slots)))
        high = tall.astype(BF16)
        rest = (tall - high.astype(F32)).astype(BF16)
        lane = lax.broadcasted_iota(jnp.int32, (slots, LANES), 1)
        back[:, pl.ds(width, LANES)] = jnp.where(
            lane < 1, high.astype(F32), rest.astype(F32)
        ).astype(BF16)

        @pl.loop(1, n_exp)
        def _(k):
            returning(k).start()

        returned[block(me), :] = back[block(me), :]

    send_back()

    @pl.when(after_end)
    def _():
        @pl.loop(0, n_exp)
        def _(e):
            hand_x(e).wait_recv()

    for t in range(2):

        @pl.when(lower)
        def _():
            go_right(t)

        go_left(t)

        @pl.when(jnp.logical_not(lower))
        def _():
            go_right(t)

    @pl.loop(1, n_exp)
    def _(k):
        homecoming(k).wait_recv()

    tn = (((0,), (0,)), ((), ()))

    @pl.loop(0, pieces)
    def _(c):
        span = columns(c)
        token_out[:, span] = lax.dot_general(
            place, returned[:, span], tn, preferred_element_type=F32
        ).astype(BF16)

    pair = lax.dot_general(
        place, returned[:, pl.ds(width, LANES)], tn, preferred_element_type=F32
    )
    total = jnp.broadcast_to((pair[:, 0:1] + pair[:, 1:2]) / weights, (rows, LANES))
    route_out[...] = jnp.transpose(total)[0:1, :].astype(BF16)

    for t in range(2):
        out = gate_out if t == 0 else down_out

        @pl.when(after_end)
        def _():
            hand_cut(t, r).wait_recv()

        @pl.loop(0, pieces)
        def _(c):
            span = columns(c)

            def from_right():
                hop(left_buf, l_send, l_recv, t, r, c, low).wait_recv()
                return left_buf[t, r, c].astype(F32)

            def from_left():
                hop(right_buf, r_send, r_recv, t, r - 1, c, up).wait_recv()
                return right_buf[t, r - 1, c].astype(F32)

            @pl.when(r == 0)
            def _():
                out[:, span] = (term(t, r, span, False) + from_right()).astype(BF16)

            @pl.when(r == n_dp - 1)
            def _():
                out[:, span] = (term(t, r, span, False) + from_left()).astype(BF16)

            @pl.when(r == 1)
            def _():
                out[:, span] = (term(t, r, span, True) + from_right()).astype(BF16)

            @pl.when(r == n_dp - 2)
            def _():
                out[:, span] = (term(t, r, span, True) + from_left()).astype(BF16)

            @pl.when(jnp.logical_and(r > 1, r < n_dp - 2))
            def _():
                out[:, span] = (term(t, r, span, False) + from_right() + from_left()).astype(BF16)

    @pl.loop(1, n_exp)
    def _(k):
        exchange(0, k).wait_send()
        exchange(1, k).wait_send()
        returning(k).wait_send()

    @pl.when(end)
    def _():
        @pl.loop(0, n_exp)
        def _(e):
            hand_x(e).wait_send()

        @pl.loop(0, pieces)
        def _(c):
            hand_g(c).wait_send()

        for t in range(2):

            @pl.loop(0, n_dp - 1)
            def _(j):
                hand_cut(t, jnp.where(r == 0, n_dp - 1 - j, j)).wait_send()

    for t in range(2):
        for d in range(n_dp):

            @pl.loop(0, pieces)
            def _(c):
                if d > 1:

                    @pl.when(jnp.logical_and(r > 0, r < d))
                    def _():
                        rightward(t, d, c).wait_send()

                if d < n_dp - 2:

                    @pl.when(jnp.logical_and(r < n_dp - 1, r > d))
                    def _():
                        leftward(t, d, c).wait_send()


def kernel_four(
    n_exp, cap, pieces,
    ids_hbm, tokens_hbm, weights_hbm, grads_hbm, gate_hbm, down_hbm,
    token_out, route_out, gate_out, down_out,
    ids_ref, tokens_ref, weights_ref, grads_ref,
    sent, got_x, got_g, gate, down, preact, hid_t, da_t, back, returned,
    scaled, raw, raw_ids, far_sent, chain_out, chain_in, pair_out, pair_in,
    load_sem, send_sem, recv_sem, raw_send, raw_recv, far_send, far_recv,
    slice_send, slice_recv, cut_send, cut_recv, x_send, x_recv,
    chain_send, chain_recv, on_send, on_recv, pair_send, pair_recv, back_send, back_recv,
):
    rows, width = tokens_ref.shape
    slots = n_exp * cap
    units = gate.shape[0]
    part = units // 4
    piece = width // pieces
    tile = 256 if units % 256 == 0 else part
    r = lax.axis_index("dp")
    me = lax.axis_index("expert")
    partner = r + 1 - 2 * lax.rem(r, 2)
    far = lax.rem(r + 2, 4)
    opposite = 3 - r
    inner = jnp.logical_or(r == 1, r == 2)
    outer = jnp.logical_or(r == 0, r == 3)

    def peer(k):
        return lax.rem(me + k, n_exp)

    def block(e):
        return pl.ds(pl.multiple_of(e * cap, cap), cap)

    def far_block(e):
        return pl.ds(pl.multiple_of(slots + e * cap, cap), cap)

    def units_of(d):
        return pl.ds(pl.multiple_of(d * part, part), part)

    def columns(c):
        return pl.ds(c * piece, piece)

    near_half, far_half = (
        pl.ds(pl.multiple_of(jnp.where(cond, 0, 2 * part), part), 2 * part)
        for cond in (r < 2, r > 1)
    )
    own_rows, more_rows = pl.ds(0, slots), pl.ds(slots, slots)

    loads = [
        pltpu.make_async_copy(source, held, load_sem.at[i])
        for i, (source, held) in enumerate((
            (ids_hbm, ids_ref), (tokens_hbm, tokens_ref), (weights_hbm, weights_ref),
            (grads_hbm, grads_ref),
            (gate_hbm, gate), (down_hbm, down),
        ))
    ]
    for load in loads[:4]:
        load.start()

    barrier = pltpu.get_barrier_semaphore()

    @pl.loop(1, n_exp)
    def _(k):
        pl.semaphore_signal(barrier, inc=1, device_id={"expert": peer(k)}, device_id_type=MESH)

    @pl.loop(1, 4)
    def _(k):
        other = lax.rem(r + k, 4)
        pl.semaphore_signal(barrier, inc=1, device_id={"dp": other}, device_id_type=MESH)

    for load in loads[4:]:
        load.start()

    def over(src, dst, s_sem, r_sem, **to):
        return pltpu.make_async_remote_copy(
            src_ref=src, dst_ref=dst, send_sem=s_sem, recv_sem=r_sem,
            device_id=to, device_id_type=MESH,
        )

    def exchange(t, to, at, device):
        got = got_g if t else got_x
        return over(
            sent.at[t, block(to)], got.at[block(at)],
            send_sem.at[t], recv_sem.at[t], expert=device,
        )

    def far_exchange(c, to, at, device):
        return over(
            far_sent.at[block(to), columns(c)], got_g.at[far_block(at), columns(c)],
            far_send.at[c], far_recv.at[c], expert=device,
        )

    def returning(to, at, device):
        return over(
            back.at[block(to)], returned.at[block(at)],
            back_send, back_recv, expert=device,
        )

    def raw_copies():
        return [
            over(ids_ref, raw_ids, raw_send.at[0], raw_recv.at[0], dp=far),
            over(scaled, raw, raw_send.at[1], raw_recv.at[1], dp=far),
        ]

    def slice_copy(half):
        return over(
            hid_t.at[half, own_rows], hid_t.at[half, more_rows], slice_send, slice_recv, dp=far
        )

    def hand_x(c):
        return over(
            got_x.at[own_rows, columns(c)], got_x.at[more_rows, columns(c)],
            x_send, x_recv.at[c], dp=partner,
        )

    def hand_cut(d):
        return over(
            da_t.at[units_of(d), own_rows], da_t.at[units_of(d), more_rows],
            cut_send, cut_recv.at[d], dp=partner,
        )

    def chain(i, c):
        return over(
            chain_out.at[i, c], chain_in.at[i, c], chain_send, chain_recv.at[i, c],
            dp=opposite,
        )

    def pass_on(c):
        return over(
            chain_in.at[0, c], chain_in.at[0, c], on_send, on_recv.at[c], dp=partner
        )

    def pair(c):
        return over(
            pair_out.at[c], pair_in.at[c], pair_send, pair_recv.at[c], dp=partner
        )

    loads[0].wait()
    others = pl.ds(0, (n_exp - 1) * cap)

    def exchanged(t):
        return over(
            sent.at[t, others], (got_g if t else got_x).at[others],
            send_sem.at[t], recv_sem.at[t], dp=partner,
        )

    def far_exchanged(c):
        return over(
            far_sent.at[others, columns(c)], got_g.at[others, columns(c)],
            far_send.at[c], far_recv.at[c], dp=partner,
        )

    def returned_all():
        return over(back.at[others], returned.at[others], back_send, back_recv, dp=partner)

    place = placement(ids_ref[...], n_exp, cap)
    loads[1].wait()
    sent[0] = jnp.dot(place, tokens_ref[...], preferred_element_type=F32).astype(BF16)
    loads[2].wait()
    weights = jnp.transpose(
        jnp.broadcast_to(weights_ref[...].astype(F32), (LANES, rows))
    )[:, 0:1]
    loads[3].wait()
    scaled[...] = (weights * grads_ref[...].astype(F32)).astype(BF16)

    pl.semaphore_wait(barrier, n_exp - 1 + 3)

    @pl.when(outer)
    def _():
        for copy in raw_copies():
            copy.start()

    @pl.loop(1, n_exp)
    def _(k):
        exchange(0, peer(k), me, peer(k)).start()

    sent[1] = jnp.dot(place, scaled[...], preferred_element_type=F32).astype(BF16)

    @pl.loop(1, n_exp)
    def _(k):
        exchange(1, peer(k), me, peer(k)).start()

    got_x[block(me)] = sent[0, block(me)]
    got_g[block(me)] = sent[1, block(me)]

    for load in loads[4:]:
        load.wait()

    exchanged(0).wait_recv()

    @pl.when(outer)
    def _():
        hand_x(0).start()

    @pl.when(inner)
    def _():
        for copy in raw_copies():
            copy.start()

    nt = (((1,), (1,)), ((), ()))
    tn = (((0,), (0,)), ((), ()))

    @pl.loop(0, units // tile)
    def _(j):
        span = pl.ds(pl.multiple_of(j * tile, tile), tile)
        value = lax.dot_general(
            gate[span, :], got_x[0:slots, :], nt, preferred_element_type=F32
        )
        preact[span, :] = value
        hid_t[span, 0:slots] = (value * jax.nn.sigmoid(value)).astype(BF16)

    @pl.when(outer)
    def _():
        hand_x(1).start()

    @pl.when(inner)
    def _():
        slice_copy(far_half).start()

    def far_dispatch():
        for copy in raw_copies():
            copy.wait_recv()
        far_place = placement(raw_ids[...], n_exp, cap)
        for c in range(pieces):
            span = columns(c)
            far_sent[:, span] = jnp.dot(
                far_place, raw[:, span], preferred_element_type=F32
            ).astype(BF16)

            @pl.loop(1, n_exp)
            def _(k):
                far_exchange(c, peer(k), me, peer(k)).start()

        got_g[far_block(me)] = far_sent[block(me)]

    @pl.when(inner)
    def _():
        far_dispatch()

    exchanged(1).wait_recv()

    @pl.when(outer)
    def _():
        slice_copy(far_half).start()

    def second(j, total):
        span = pl.ds(pl.multiple_of(j * tile, tile), tile)
        slope = lax.dot_general(
            down[span, :], got_g[0:slots, :], nt, preferred_element_type=F32
        )
        value = preact[span, :]
        sigma = jax.nn.sigmoid(value)
        da_t[span, 0:slots] = (slope * (sigma * (1.0 + value * (1.0 - sigma)))).astype(BF16)
        return total + jnp.sum(hid_t[span, 0:slots].astype(F32) * slope, axis=0, keepdims=True)

    route = lax.fori_loop(0, units // tile, second, jnp.zeros((1, slots), F32))

    @pl.when(outer)
    def _():
        for d in (opposite, far, partner):
            hand_cut(d).start()
        for c in range(2, pieces):
            hand_x(c).start()
        far_dispatch()

    for c in range(pieces):
        span = columns(c)
        back[:, span] = lax.dot_general(
            da_t[:, 0:slots], gate[:, span], tn, preferred_element_type=F32
        ).astype(BF16)

    tall = jnp.transpose(jnp.broadcast_to(route, (LANES, slots)))
    high = tall.astype(BF16)
    rest = (tall - high.astype(F32)).astype(BF16)
    lane = lax.broadcasted_iota(jnp.int32, (slots, LANES), 1)
    back[:, pl.ds(width, LANES)] = jnp.where(
        lane < 1, high.astype(F32), rest.astype(F32)
    ).astype(BF16)

    @pl.loop(1, n_exp)
    def _(k):
        returning(peer(k), me, peer(k)).start()

    returned[block(me), :] = back[block(me), :]

    def gate_term(d, c, depth):
        return jnp.dot(
            da_t[units_of(d), 0:depth], got_x[0:depth, columns(c)], preferred_element_type=F32
        )

    def down_term(d, c):
        return jnp.dot(
            hid_t[units_of(d), :], got_g[:, columns(c)], preferred_element_type=F32
        )

    def send_pair(c):
        far_exchanged(c).wait_recv()
        pair_out[c] = down_term(partner, c).astype(BF16)
        pair(c).start()

    def send_chain(i, c):
        d = opposite if i else far
        if c == 0:
            hand_cut(d).wait_recv()
        if i == 0:
            hand_x(c).wait_recv()
        chain_out[i, c] = gate_term(d, c, 2 * slots).astype(BF16)
        chain(i, c).start()

    def forward(c):
        own = gate_term(partner, c, slots)
        chain(0, c).wait_recv()
        chain_in[0, c] = (own + chain_in[0, c].astype(F32)).astype(BF16)
        pass_on(c).start()

    slice_copy(near_half).wait_recv()

    @pl.when(inner)
    def _():
        steps = [(send_pair, 0), (send_chain, 0, 0)]
        for c in range(1, pieces):
            steps += [(send_pair, c), (send_chain, 0, c), (send_chain, 1, c - 1), (forward, c - 1)]
        for step, *args in steps + [(send_chain, 1, pieces - 1)]:
            step(*args)

    @pl.when(outer)
    def _():
        for c in range(pieces):
            send_pair(c)

    returned_all().wait_recv()

    for c in range(pieces):
        span = columns(c)
        token_out[:, span] = lax.dot_general(
            place, returned[:, span], tn, preferred_element_type=F32
        ).astype(BF16)

    both = lax.dot_general(
        place, returned[:, pl.ds(width, LANES)], tn, preferred_element_type=F32
    )
    total = jnp.broadcast_to((both[:, 0:1] + both[:, 1:2]) / weights, (rows, LANES))
    route_out[...] = jnp.transpose(total)[0:1, :].astype(BF16)

    @pl.when(inner)
    def _():
        forward(pieces - 1)

    for c in range(pieces):
        own = down_term(r, c)
        pair(c).wait_recv()
        down_out[:, columns(c)] = (own + pair_in[c].astype(F32)).astype(BF16)

    @pl.when(inner)
    def _():
        hand_cut(r).wait_recv()
        for c in range(pieces):
            own = gate_term(r, c, 2 * slots)
            chain(1, c).wait_recv()
            gate_out[:, columns(c)] = (own + chain_in[1, c].astype(F32)).astype(BF16)

    @pl.when(outer)
    def _():
        for c in range(pieces):
            own = gate_term(r, c, slots)
            pass_on(c).wait_recv()
            gate_out[:, columns(c)] = (own + chain_in[0, c].astype(F32)).astype(BF16)

    for t in range(2):
        exchanged(t).wait_send()
    for c in range(pieces):
        far_exchanged(c).wait_send()
    returned_all().wait_send()
    for copy in raw_copies():
        copy.wait_send()
    slice_copy(far_half).wait_send()
    over(pair_out, pair_in, pair_send, pair_recv.at[0], dp=partner).wait_send()

    @pl.when(inner)
    def _():
        over(chain_out, chain_in, chain_send, chain_recv.at[0, 0], dp=opposite).wait_send()
        over(chain_in.at[0], chain_in.at[0], on_send, on_recv.at[0], dp=partner).wait_send()

    @pl.when(outer)
    def _():
        cuts = pl.ds(0, 3 * part)
        over(
            da_t.at[cuts, own_rows], da_t.at[cuts, more_rows], cut_send, cut_recv.at[0], dp=partner
        ).wait_send()
        over(
            got_x.at[own_rows], got_x.at[more_rows], x_send, x_recv.at[0], dp=partner
        ).wait_send()


def settle(token, route, gate, down, token_out, route_out, gate_out, down_out, sems):
    copies = [
        pltpu.make_async_copy(source, out, sems.at[i])
        for i, (source, out) in enumerate((
            (gate, gate_out), (down, down_out), (token, token_out), (route, route_out),
        ))
    ]
    for copy in copies:
        copy.start()
    for copy in copies:
        copy.wait()


def chain_scratch(n_dp, n_exp, pieces, slots, units, part, width, piece, rows):
    dma = pltpu.SemaphoreType.DMA
    return [
        pltpu.VMEM((2, slots, width), BF16),
        pltpu.VMEM((2, 2 * slots, width), BF16),
        pltpu.VMEM((units, width), BF16),
        pltpu.VMEM((units, width), BF16),
        pltpu.VMEM((units, slots), F32),
        pltpu.VMEM((units, 2 * slots), BF16),
        pltpu.VMEM((units, 2 * slots), BF16),
        pltpu.VMEM((slots, width + LANES), BF16),
        pltpu.VMEM((slots, width + LANES), BF16),
        pltpu.VMEM((2, n_dp - 1, pieces, part, piece), BF16),
        pltpu.VMEM((2, n_dp - 1, pieces, part, piece), BF16),
        dma((2,)),
        dma((2, n_exp)), dma((2, n_exp)), dma((n_exp,)), dma((n_exp,)),
        dma((2, n_dp - 1, pieces)), dma((2, n_dp - 1, pieces)),
        dma((2, n_dp - 1, pieces)), dma((2, n_dp - 1, pieces)),
        dma((n_exp,)), dma((n_exp,)), dma((pieces,)), dma((pieces,)),
        dma((2, n_dp)), dma((2, n_dp)),
    ]


def four_scratch(n_dp, n_exp, pieces, slots, units, part, width, piece, rows):
    dma = pltpu.SemaphoreType.DMA
    return [
        pltpu.VMEM((1, rows), jnp.int32),
        pltpu.VMEM((rows, width), BF16),
        pltpu.VMEM((1, rows), BF16),
        pltpu.VMEM((rows, width), BF16),
        pltpu.VMEM((2, slots, width), BF16),
        pltpu.VMEM((2 * slots, width), BF16),
        pltpu.VMEM((2 * slots, width), BF16),
        pltpu.VMEM((units, width), BF16),
        pltpu.VMEM((units, width), BF16),
        pltpu.VMEM((units, slots), F32),
        pltpu.VMEM((units, 2 * slots), BF16),
        pltpu.VMEM((units, 2 * slots), BF16),
        pltpu.VMEM((slots, width + LANES), BF16),
        pltpu.VMEM((slots, width + LANES), BF16),
        pltpu.VMEM((rows, width), BF16),
        pltpu.VMEM((rows, width), BF16),
        pltpu.VMEM((1, rows), jnp.int32),
        pltpu.VMEM((slots, width), BF16),
        pltpu.VMEM((2, pieces, part, piece), BF16),
        pltpu.VMEM((2, pieces, part, piece), BF16),
        pltpu.VMEM((pieces, part, piece), BF16),
        pltpu.VMEM((pieces, part, piece), BF16),
        dma((6,)), dma((2,)), dma((2,)), dma((2,)), dma((2,)), dma((pieces,)), dma((pieces,)),
        dma, dma, dma, dma((n_dp,)), dma, dma((pieces,)),
        dma, dma((2, pieces)), dma, dma((pieces,)), dma, dma((pieces,)), dma, dma,
    ]


def per_device(tokens, expert_ids, route_weights, out_grad, gate_weight, down_weight):
    rows, width = tokens.shape
    n_exp, n_dp = lax.axis_size("expert"), lax.axis_size("dp")
    top = expert_ids.shape[1]
    assert top == 1 and n_dp >= 4
    cap = -(-max(2, 2 * rows * top // n_exp) // 16) * 16
    slots = n_exp * cap
    units = gate_weight.shape[1]
    part = units // n_dp
    pieces = max(1, width // 512)
    piece = width // pieces
    shapes = (
        jax.ShapeDtypeStruct((rows, width), BF16),
        jax.ShapeDtypeStruct((1, rows), BF16),
        jax.ShapeDtypeStruct((part, width), BF16),
        jax.ShapeDtypeStruct((part, width), BF16),
    )
    vmem = pl.BlockSpec(memory_space=pltpu.VMEM)
    hbm = pl.BlockSpec(memory_space=pl.ANY)
    four = n_dp == 4
    body = (
        functools.partial(kernel_four, n_exp, cap, pieces)
        if four
        else functools.partial(kernel, n_dp, n_exp, cap, pieces)
    )
    scratch = four_scratch if four else chain_scratch
    results = pl.pallas_call(
        body,
        out_shape=tuple(pltpu.VMEM(a.shape, a.dtype) for a in shapes) if four else shapes,
        in_specs=[hbm] * 6 if four else [vmem] * 4 + [hbm] * 2,
        out_specs=(vmem,) * 4,
        scratch_shapes=scratch(n_dp, n_exp, pieces, slots, units, part, width, piece, rows),
        compiler_params=pltpu.CompilerParams(
            collective_id=0, has_side_effects=True,
            vmem_limit_bytes=60_000_000 if four else 67_000_000,

        ),
    )(
        expert_ids.reshape(1, rows), tokens, route_weights.reshape(1, rows), out_grad,
        gate_weight[0], down_weight[0],
    )
    if four:
        results = [pltpu.with_memory_space_constraint(a, pltpu.VMEM) for a in results]
    token_grad, route_grad, gate_grad, down_grad = pl.pallas_call(
        settle,
        out_shape=shapes,
        in_specs=[vmem] * 4,
        out_specs=(hbm,) * 4,
        scratch_shapes=[pltpu.SemaphoreType.DMA((4,))],
    )(*results)
    return token_grad, route_grad.reshape(rows, 1), gate_grad[None], down_grad[None]


def solution(mesh):
    placed = (
        P(("dp", "expert"), None),
        P(("dp", "expert"), None),
        P(("dp", "expert"), None),
        P(("dp", "expert"), None),
        P("expert", None, None),
        P("expert", None, None),
    )
    return jax.shard_map(
        per_device,
        mesh=mesh,
        in_specs=placed,
        out_specs=(
            P(("dp", "expert"), None),
            P(("dp", "expert"), None),
            P("expert", "dp", None),
            P("expert", "dp", None),
        ),
        check_vma=False,
    )
```

```python
import functools

import jax
import jax.numpy as jnp
from jax import lax
from jax.experimental import pallas as pl
from jax.experimental.pallas import tpu as pltpu
from jax.sharding import PartitionSpec as P

MESH = pl.DeviceIdType.MESH
BF16, F32 = jnp.bfloat16, jnp.float32
LANES = 128


def placement(ids, n_exp, cap):
    rows = ids.shape[1]
    slots = n_exp * cap
    names = lax.broadcasted_iota(jnp.int32, (max(n_exp, 16), rows), 0)
    one_hot = (names == ids).astype(F32)
    before = (
        lax.broadcasted_iota(jnp.int32, (rows, rows), 0)
        < lax.broadcasted_iota(jnp.int32, (rows, rows), 1)
    ).astype(F32)
    counts = jnp.dot(one_hot.astype(BF16), before.astype(BF16), preferred_element_type=F32)
    rank = jnp.sum(counts * one_hot, axis=0, keepdims=True).astype(jnp.int32)
    target = ids * cap + rank
    match = lax.broadcasted_iota(jnp.int32, (slots, rows), 0) == target
    return match.astype(F32).astype(BF16)


def kernel(
    n_dp, n_exp, cap, pieces,
    ids_ref, tokens_ref, weights_ref, grads_ref, gate_hbm, down_hbm,
    token_out, route_out, gate_out, down_out,
    sent, got, gate, down, preact, hid_t, da_t, back, returned, right_buf, left_buf,
    load_sem, send_sem, recv_sem, back_send, back_recv, r_send, r_recv, l_send, l_recv,
    x_send, x_recv, g_send, g_recv, cut_send, cut_recv,
):
    rows, width = tokens_ref.shape
    slots = n_exp * cap
    units = gate.shape[0]
    part = units // n_dp
    piece = width // pieces
    tile = 256 if units % 256 == 0 else part
    r = lax.axis_index("dp")
    me = lax.axis_index("expert")

    def peer(k):
        return lax.rem(me + k, n_exp)

    def block(e):
        return pl.ds(pl.multiple_of(e * cap, cap), cap)

    loads = [
        pltpu.make_async_copy(gate_hbm, gate, load_sem.at[0]),
        pltpu.make_async_copy(down_hbm, down, load_sem.at[1]),
    ]
    for load in loads:
        load.start()

    barrier = pltpu.get_barrier_semaphore()

    @pl.loop(1, n_exp)
    def _(k):
        pl.semaphore_signal(barrier, inc=1, device_id={"expert": peer(k)}, device_id_type=MESH)

    up, low = lax.rem(r + 1, n_dp), lax.rem(r + n_dp - 1, n_dp)

    @pl.loop(1, n_dp)
    def _(k):
        other = lax.rem(r + k, n_dp)
        pl.semaphore_signal(barrier, inc=1, device_id={"dp": other}, device_id_type=MESH)

    place = placement(ids_ref[...], n_exp, cap)
    sent[0] = jnp.dot(place, tokens_ref[...], preferred_element_type=F32).astype(BF16)
    pl.semaphore_wait(barrier, n_exp - 1 + n_dp - 1)

    def exchange(t, k):
        to = peer(k)
        return pltpu.make_async_remote_copy(
            src_ref=sent.at[t, block(to)],
            dst_ref=got.at[t, block(me)],
            send_sem=send_sem.at[t, to],
            recv_sem=recv_sem.at[t, me],
            device_id={"expert": to},
            device_id_type=MESH,
        )

    def arrival(t, k):
        of = peer(k)
        return pltpu.make_async_remote_copy(
            src_ref=sent.at[t, block(of)],
            dst_ref=got.at[t, block(of)],
            send_sem=send_sem.at[t, of],
            recv_sem=recv_sem.at[t, of],
            device_id={"expert": of},
            device_id_type=MESH,
        )

    @pl.loop(1, n_exp)
    def _(k):
        exchange(0, k).start()

    got[0, block(me)] = sent[0, block(me)]
    weights = jnp.transpose(
        jnp.broadcast_to(weights_ref[...].astype(F32), (LANES, rows))
    )[:, 0:1]
    scaled = (weights * grads_ref[...].astype(F32)).astype(BF16)
    sent[1] = jnp.dot(place, scaled, preferred_element_type=F32).astype(BF16)

    @pl.loop(1, n_exp)
    def _(k):
        exchange(1, k).start()

    got[1, block(me)] = sent[1, block(me)]

    for load in loads:
        load.wait()

    end = jnp.logical_or(r == 0, r == n_dp - 1)
    after_end = jnp.logical_or(r == 1, r == n_dp - 2)
    inner = jnp.where(r == 0, up, low)
    lower = r < n_dp // 2

    def hand_x(e):
        return pltpu.make_async_remote_copy(
            src_ref=got.at[0, block(e)],
            dst_ref=got.at[0, pl.ds(pl.multiple_of(slots + e * cap, cap), cap)],
            send_sem=x_send.at[e],
            recv_sem=x_recv.at[e],
            device_id={"dp": inner},
            device_id_type=MESH,
        )

    def hand_g(c):
        span = pl.ds(pl.multiple_of(c * piece, piece), piece)
        return pltpu.make_async_remote_copy(
            src_ref=got.at[1, pl.ds(0, slots), span],
            dst_ref=got.at[1, pl.ds(slots, slots), span],
            send_sem=g_send.at[c],
            recv_sem=g_recv.at[c],
            device_id={"dp": inner},
            device_id_type=MESH,
        )

    def hand_cut(t, d):
        left = da_t if t == 0 else hid_t
        own = pl.ds(pl.multiple_of(d * part, part), part)
        return pltpu.make_async_remote_copy(
            src_ref=left.at[own, pl.ds(0, slots)],
            dst_ref=left.at[own, pl.ds(slots, slots)],
            send_sem=cut_send.at[t, d],
            recv_sem=cut_recv.at[t, d],
            device_id={"dp": inner},
            device_id_type=MESH,
        )

    @pl.when(end)
    def _():
        hand_x(me).start()

    @pl.loop(1, n_exp)
    def _(k):
        arrival(0, k).wait_recv()

        @pl.when(end)
        def _():
            hand_x(peer(k)).start()

    nt = (((1,), (1,)), ((), ()))

    @pl.loop(0, units // tile)
    def _(j):
        span = pl.ds(pl.multiple_of(j * tile, tile), tile)
        value = lax.dot_general(
            gate[span, :], got[0, 0:slots, :], nt, preferred_element_type=F32
        )
        preact[span, :] = value
        hid_t[span, 0:slots] = (value * jax.nn.sigmoid(value)).astype(BF16)

    def hand_cuts(t):
        @pl.when(end)
        def _():
            @pl.loop(0, n_dp - 1)
            def _(j):
                hand_cut(t, jnp.where(r == 0, n_dp - 1 - j, j)).start()

    @pl.loop(1, n_exp)
    def _(k):
        arrival(1, k).wait_recv()

    def second(j, total):
        span = pl.ds(pl.multiple_of(j * tile, tile), tile)
        slope = lax.dot_general(
            down[span, :], got[1, 0:slots, :], nt, preferred_element_type=F32
        )
        value = preact[span, :]
        sigma = jax.nn.sigmoid(value)
        da_t[span, 0:slots] = (slope * (sigma * (1.0 + value * (1.0 - sigma)))).astype(BF16)
        return total + jnp.sum(hid_t[span, 0:slots].astype(F32) * slope, axis=0, keepdims=True)

    route = lax.fori_loop(0, units // tile, second, jnp.zeros((1, slots), F32))

    hand_cuts(0)
    hand_cuts(1)

    @pl.when(end)
    def _():
        @pl.loop(0, pieces)
        def _(c):
            hand_g(c).start()

    def term(t, d, span, wide):
        left = da_t if t == 0 else hid_t
        start = d * part if isinstance(d, int) else pl.multiple_of(d * part, part)
        depth = 2 * slots if wide else slots
        return jnp.dot(
            left[pl.ds(start, part), 0:depth],
            got[t, 0:depth, span],
            preferred_element_type=F32,
        )

    def columns(c):
        return pl.ds(pl.multiple_of(c * piece, piece), piece)

    def hop(buf, s_sem, r_sem, t, d, c, to):
        return pltpu.make_async_remote_copy(
            src_ref=buf.at[t, d, c],
            dst_ref=buf.at[t, d, c],
            send_sem=s_sem.at[t, d, c],
            recv_sem=r_sem.at[t, d, c],
            device_id={"dp": to},
            device_id_type=MESH,
        )

    def rightward(t, d, c, to=None):
        return hop(right_buf, r_send, r_recv, t, d - 1, c, up)

    def leftward(t, d, c, to=None):
        return hop(left_buf, l_send, l_recv, t, d, c, low)

    def pass_on(t, d, c, copy, buf, index, first):
        @pl.when(first)
        def _():
            buf[t, index, c] = term(t, d, columns(c), True).astype(BF16)

        @pl.when(jnp.logical_not(first))
        def _():
            own = term(t, d, columns(c), False)
            copy.wait_recv()
            buf[t, index, c] = (own + buf[t, index, c].astype(F32)).astype(BF16)

        copy.start()

    def go_right(t):
        for d in range(n_dp - 1, 1, -1):

            @pl.when(r == 1)
            def _():
                hand_cut(t, d).wait_recv()

            @pl.when(jnp.logical_and(r > 0, r < d))
            def _():
                @pl.loop(0, pieces)
                def _(c):
                    if t == 1 and d == n_dp - 1:

                        @pl.when(r == 1)
                        def _():
                            hand_g(c).wait_recv()

                    pass_on(t, d, c, rightward(t, d, c), right_buf, d - 1, r == 1)

    def go_left(t):
        for d in range(n_dp - 2):

            @pl.when(r == n_dp - 2)
            def _():
                hand_cut(t, d).wait_recv()

            @pl.when(jnp.logical_and(r < n_dp - 1, r > d))
            def _():
                @pl.loop(0, pieces)
                def _(c):
                    if t == 1 and d == 0:

                        @pl.when(r == n_dp - 2)
                        def _():
                            hand_g(c).wait_recv()

                    pass_on(t, d, c, leftward(t, d, c), left_buf, d, r == n_dp - 2)

    def returning(k):
        to = peer(k)
        return pltpu.make_async_remote_copy(
            src_ref=back.at[block(to)],
            dst_ref=returned.at[block(me)],
            send_sem=back_send.at[to],
            recv_sem=back_recv.at[me],
            device_id={"expert": to},
            device_id_type=MESH,
        )

    def homecoming(k):
        of = peer(k)
        return pltpu.make_async_remote_copy(
            src_ref=back.at[block(of)],
            dst_ref=returned.at[block(of)],
            send_sem=back_send.at[of],
            recv_sem=back_recv.at[of],
            device_id={"expert": of},
            device_id_type=MESH,
        )

    def send_back():
        tn = (((0,), (0,)), ((), ()))

        @pl.loop(0, pieces)
        def _(c):
            span = columns(c)
            back[:, span] = lax.dot_general(
                da_t[:, 0:slots], gate[:, span], tn, preferred_element_type=F32
            ).astype(BF16)

        tall = jnp.transpose(jnp.broadcast_to(route, (LANES, slots)))
        high = tall.astype(BF16)
        rest = (tall - high.astype(F32)).astype(BF16)
        lane = lax.broadcasted_iota(jnp.int32, (slots, LANES), 1)
        back[:, pl.ds(width, LANES)] = jnp.where(
            lane < 1, high.astype(F32), rest.astype(F32)
        ).astype(BF16)

        @pl.loop(1, n_exp)
        def _(k):
            returning(k).start()

        returned[block(me), :] = back[block(me), :]

    send_back()

    @pl.when(after_end)
    def _():
        @pl.loop(0, n_exp)
        def _(e):
            hand_x(e).wait_recv()

    for t in range(2):

        @pl.when(lower)
        def _():
            go_right(t)

        go_left(t)

        @pl.when(jnp.logical_not(lower))
        def _():
            go_right(t)

    @pl.loop(1, n_exp)
    def _(k):
        homecoming(k).wait_recv()

    tn = (((0,), (0,)), ((), ()))

    @pl.loop(0, pieces)
    def _(c):
        span = columns(c)
        token_out[:, span] = lax.dot_general(
            place, returned[:, span], tn, preferred_element_type=F32
        ).astype(BF16)

    pair = lax.dot_general(
        place, returned[:, pl.ds(width, LANES)], tn, preferred_element_type=F32
    )
    total = jnp.broadcast_to((pair[:, 0:1] + pair[:, 1:2]) / weights, (rows, LANES))
    route_out[...] = jnp.transpose(total)[0:1, :].astype(BF16)

    for t in range(2):
        out = gate_out if t == 0 else down_out

        @pl.when(after_end)
        def _():
            hand_cut(t, r).wait_recv()

        @pl.loop(0, pieces)
        def _(c):
            span = columns(c)

            def from_right():
                hop(left_buf, l_send, l_recv, t, r, c, low).wait_recv()
                return left_buf[t, r, c].astype(F32)

            def from_left():
                hop(right_buf, r_send, r_recv, t, r - 1, c, up).wait_recv()
                return right_buf[t, r - 1, c].astype(F32)

            @pl.when(r == 0)
            def _():
                out[:, span] = (term(t, r, span, False) + from_right()).astype(BF16)

            @pl.when(r == n_dp - 1)
            def _():
                out[:, span] = (term(t, r, span, False) + from_left()).astype(BF16)

            @pl.when(r == 1)
            def _():
                out[:, span] = (term(t, r, span, True) + from_right()).astype(BF16)

            @pl.when(r == n_dp - 2)
            def _():
                out[:, span] = (term(t, r, span, True) + from_left()).astype(BF16)

            @pl.when(jnp.logical_and(r > 1, r < n_dp - 2))
            def _():
                out[:, span] = (term(t, r, span, False) + from_right() + from_left()).astype(BF16)

    @pl.loop(1, n_exp)
    def _(k):
        exchange(0, k).wait_send()
        exchange(1, k).wait_send()
        returning(k).wait_send()

    @pl.when(end)
    def _():
        @pl.loop(0, n_exp)
        def _(e):
            hand_x(e).wait_send()

        @pl.loop(0, pieces)
        def _(c):
            hand_g(c).wait_send()

        for t in range(2):

            @pl.loop(0, n_dp - 1)
            def _(j):
                hand_cut(t, jnp.where(r == 0, n_dp - 1 - j, j)).wait_send()

    for t in range(2):
        for d in range(n_dp):

            @pl.loop(0, pieces)
            def _(c):
                if d > 1:

                    @pl.when(jnp.logical_and(r > 0, r < d))
                    def _():
                        rightward(t, d, c).wait_send()

                if d < n_dp - 2:

                    @pl.when(jnp.logical_and(r < n_dp - 1, r > d))
                    def _():
                        leftward(t, d, c).wait_send()


def kernel_four(
    n_exp, cap, pieces,
    ids_hbm, tokens_hbm, weights_hbm, grads_hbm, gate_hbm, down_hbm,
    token_out, route_out, gate_out, down_out,
    ids_ref, tokens_ref, weights_ref, grads_ref,
    sent, got_x, got_g, gate, down, preact, hid_t, da_t, back, returned,
    scaled, raw, raw_ids, relay, far_sent, chain_out, chain_in, pair_out, pair_in,
    load_sem, send_sem, recv_sem, raw_send, raw_recv, relay_send, relay_recv, far_send, far_recv,
    slice_send, slice_recv, cut_send, cut_recv, x_send, x_recv,
    chain_send, chain_recv, on_send, on_recv, pair_send, pair_recv, back_send, back_recv,
):
    rows, width = tokens_ref.shape
    slots = n_exp * cap
    units = gate.shape[0]
    part = units // 4
    piece = width // pieces
    early = (pieces + 1) // 2
    half = early * piece
    tile = 256 if units % 256 == 0 else part
    r = lax.axis_index("dp")
    me = lax.axis_index("expert")
    partner = r + 1 - 2 * lax.rem(r, 2)
    far = lax.rem(r + 2, 4)
    opposite = 3 - r
    inner = jnp.logical_or(r == 1, r == 2)
    outer = jnp.logical_or(r == 0, r == 3)

    def peer(k):
        return lax.rem(me + k, n_exp)

    def block(e):
        return pl.ds(pl.multiple_of(e * cap, cap), cap)

    def far_block(e):
        return pl.ds(pl.multiple_of(slots + e * cap, cap), cap)

    def units_of(d):
        return pl.ds(pl.multiple_of(d * part, part), part)

    def columns(c):
        return pl.ds(c * piece, piece)

    near_half, far_half = (
        pl.ds(pl.multiple_of(jnp.where(cond, 0, 2 * part), part), 2 * part)
        for cond in (r < 2, r > 1)
    )
    own_rows, more_rows = pl.ds(0, slots), pl.ds(slots, slots)

    loads = [
        pltpu.make_async_copy(source, held, load_sem.at[i])
        for i, (source, held) in enumerate((
            (weights_hbm, weights_ref), (grads_hbm, grads_ref), (ids_hbm, ids_ref),
            (tokens_hbm, tokens_ref),
            (gate_hbm, gate), (down_hbm, down),
        ))
    ]
    for load in loads[:4]:
        load.start()

    barrier = pltpu.get_barrier_semaphore()

    @pl.loop(1, n_exp)
    def _(k):
        pl.semaphore_signal(barrier, inc=1, device_id={"expert": peer(k)}, device_id_type=MESH)

    @pl.loop(1, 4)
    def _(k):
        other = lax.rem(r + k, 4)
        pl.semaphore_signal(barrier, inc=1, device_id={"dp": other}, device_id_type=MESH)

    for load in loads[4:]:
        load.start()

    def over(src, dst, s_sem, r_sem, **to):
        return pltpu.make_async_remote_copy(
            src_ref=src, dst_ref=dst, send_sem=s_sem, recv_sem=r_sem,
            device_id=to, device_id_type=MESH,
        )

    def exchange(t, to, at, device):
        got = got_g if t else got_x
        return over(
            sent.at[t, block(to)], got.at[block(at)],
            send_sem.at[t], recv_sem.at[t], expert=device,
        )

    def far_exchange(c, to, at, device):
        return over(
            far_sent.at[block(to), columns(c)], got_g.at[far_block(at), columns(c)],
            far_send.at[c], far_recv.at[c], expert=device,
        )

    def returning(to, at, device):
        return over(
            back.at[block(to)], returned.at[block(at)],
            back_send, back_recv, expert=device,
        )

    first, last = pl.ds(0, half), pl.ds(half, width - half)

    def raw_first():
        return [
            over(ids_ref, raw_ids, raw_send.at[0], raw_recv.at[0], dp=far),
            over(scaled.at[:, first], raw.at[:, first], raw_send.at[1], raw_recv.at[1], dp=far),
        ]

    def raw_last():
        return over(scaled.at[:, last], raw.at[:, last], raw_send.at[2], raw_recv.at[2], dp=far)

    def to_relay():
        return over(scaled.at[:, last], relay, relay_send, relay_recv, dp=partner)

    def from_relay():
        return over(relay, raw.at[:, last], relay_send, raw_recv.at[2], dp=opposite)

    def slice_copy(half):
        return over(
            hid_t.at[half, own_rows], hid_t.at[half, more_rows], slice_send, slice_recv, dp=far
        )

    def hand_x(c):
        return over(
            got_x.at[own_rows, columns(c)], got_x.at[more_rows, columns(c)],
            x_send, x_recv.at[c], dp=partner,
        )

    def hand_cut(d):
        return over(
            da_t.at[units_of(d), own_rows], da_t.at[units_of(d), more_rows],
            cut_send, cut_recv.at[d], dp=partner,
        )

    def chain(i, c):
        return over(
            chain_out.at[i, c], chain_in.at[i, c], chain_send, chain_recv.at[i, c],
            dp=opposite,
        )

    def pass_on(c):
        return over(
            chain_in.at[0, c], chain_in.at[0, c], on_send, on_recv.at[c], dp=partner
        )

    def pair(c):
        return over(
            pair_out.at[c], pair_in.at[c], pair_send, pair_recv.at[c], dp=partner
        )

    others = pl.ds(0, (n_exp - 1) * cap)

    def exchanged(t):
        return over(
            sent.at[t, others], (got_g if t else got_x).at[others],
            send_sem.at[t], recv_sem.at[t], dp=partner,
        )

    def far_exchanged(c):
        return over(
            far_sent.at[others, columns(c)], got_g.at[others, columns(c)],
            far_send.at[c], far_recv.at[c], dp=partner,
        )

    def returned_all():
        return over(back.at[others], returned.at[others], back_send, back_recv, dp=partner)

    loads[0].wait()
    weights = jnp.transpose(
        jnp.broadcast_to(weights_ref[...].astype(F32), (LANES, rows))
    )[:, 0:1]
    loads[1].wait()
    scaled[...] = (weights * grads_ref[...].astype(F32)).astype(BF16)
    loads[2].wait()
    place = placement(ids_ref[...], n_exp, cap)
    pl.semaphore_wait(barrier, n_exp - 1 + 3)

    for copy in raw_first():
        copy.start()

    @pl.when(inner)
    def _():
        raw_last().start()

    @pl.when(outer)
    def _():
        to_relay().start()

    loads[3].wait()
    sent[0] = jnp.dot(place, tokens_ref[...], preferred_element_type=F32).astype(BF16)

    @pl.loop(1, n_exp)
    def _(k):
        exchange(0, peer(k), me, peer(k)).start()

    sent[1] = jnp.dot(place, scaled[...], preferred_element_type=F32).astype(BF16)

    @pl.loop(1, n_exp)
    def _(k):
        exchange(1, peer(k), me, peer(k)).start()

    got_x[block(me)] = sent[0, block(me)]
    got_g[block(me)] = sent[1, block(me)]

    for load in loads[4:]:
        load.wait()

    exchanged(0).wait_recv()

    @pl.when(outer)
    def _():
        hand_x(0).start()

    nt = (((1,), (1,)), ((), ()))
    tn = (((0,), (0,)), ((), ()))

    @pl.loop(0, units // tile)
    def _(j):
        span = pl.ds(pl.multiple_of(j * tile, tile), tile)
        value = lax.dot_general(
            gate[span, :], got_x[0:slots, :], nt, preferred_element_type=F32
        )
        preact[span, :] = value
        hid_t[span, 0:slots] = (value * jax.nn.sigmoid(value)).astype(BF16)

    slice_copy(far_half).start()

    @pl.when(inner)
    def _():
        to_relay().wait_recv()
        from_relay().start()

    @pl.when(outer)
    def _():
        hand_x(1).start()

    def far_dispatch(chunks):
        for c in chunks:
            span = columns(c)
            far_sent[:, span] = jnp.dot(
                far_place, raw[:, span], preferred_element_type=F32
            ).astype(BF16)

            @pl.loop(1, n_exp)
            def _(k):
                far_exchange(c, peer(k), me, peer(k)).start()

            got_g[far_block(me), span] = far_sent[block(me), span]

    for copy in raw_first():
        copy.wait_recv()
    far_place = placement(raw_ids[...], n_exp, cap)
    far_dispatch(range(early))

    def far_rest():
        raw_last().wait_recv()
        far_dispatch(range(early, pieces))

    @pl.when(outer)
    def _():
        far_rest()

    exchanged(1).wait_recv()

    def second(j, total):
        span = pl.ds(pl.multiple_of(j * tile, tile), tile)
        slope = lax.dot_general(
            down[span, :], got_g[0:slots, :], nt, preferred_element_type=F32
        )
        value = preact[span, :]
        sigma = jax.nn.sigmoid(value)
        da_t[span, 0:slots] = (slope * (sigma * (1.0 + value * (1.0 - sigma)))).astype(BF16)
        return total + jnp.sum(hid_t[span, 0:slots].astype(F32) * slope, axis=0, keepdims=True)

    route = lax.fori_loop(0, units // tile, second, jnp.zeros((1, slots), F32))

    @pl.when(outer)
    def _():
        for d in (opposite, far, partner):
            hand_cut(d).start()
        for c in range(2, pieces):
            hand_x(c).start()

    def gate_term(d, c, depth):
        return jnp.dot(
            da_t[units_of(d), 0:depth], got_x[0:depth, columns(c)], preferred_element_type=F32
        )

    def down_term(d, c):
        return jnp.dot(
            hid_t[units_of(d), :], got_g[:, columns(c)], preferred_element_type=F32
        )

    def send_pair(c):
        far_exchanged(c).wait_recv()
        pair_out[c] = down_term(partner, c).astype(BF16)
        pair(c).start()

    def send_chain(i, c):
        d = opposite if i else far
        if c == 0:
            hand_cut(d).wait_recv()
        if i == 0:
            hand_x(c).wait_recv()
        chain_out[i, c] = gate_term(d, c, 2 * slots).astype(BF16)
        chain(i, c).start()

    def forward(c):
        own = gate_term(partner, c, slots)
        chain(0, c).wait_recv()
        chain_in[0, c] = (own + chain_in[0, c].astype(F32)).astype(BF16)
        pass_on(c).start()

    def send_back():
        for c in range(pieces):
            span = columns(c)
            back[:, span] = lax.dot_general(
                da_t[:, 0:slots], gate[:, span], tn, preferred_element_type=F32
            ).astype(BF16)

        tall = jnp.transpose(jnp.broadcast_to(route, (LANES, slots)))
        high = tall.astype(BF16)
        rest = (tall - high.astype(F32)).astype(BF16)
        lane = lax.broadcasted_iota(jnp.int32, (slots, LANES), 1)
        back[:, pl.ds(width, LANES)] = jnp.where(
            lane < 1, high.astype(F32), rest.astype(F32)
        ).astype(BF16)

        @pl.loop(1, n_exp)
        def _(k):
            returning(peer(k), me, peer(k)).start()

        returned[block(me), :] = back[block(me), :]

    slice_copy(near_half).wait_recv()

    @pl.when(inner)
    def _():
        steps = [(send_pair, 0), (send_chain, 0, 0), (far_rest,)]
        for c in range(1, pieces):
            steps += [(send_pair, c), (send_chain, 0, c), (send_chain, 1, c - 1), (forward, c - 1)]
            if c == pieces - 1:
                steps.insert(-2, (send_back,))
        steps += [(send_chain, 1, pieces - 1), (forward, pieces - 1)]
        for step, *args in steps:
            step(*args)

    @pl.when(outer)
    def _():
        for c in range(pieces):
            send_pair(c)
        send_back()

    returned_all().wait_recv()

    for c in range(pieces):
        span = columns(c)
        token_out[:, span] = lax.dot_general(
            place, returned[:, span], tn, preferred_element_type=F32
        ).astype(BF16)

    both = lax.dot_general(
        place, returned[:, pl.ds(width, LANES)], tn, preferred_element_type=F32
    )
    total = jnp.broadcast_to((both[:, 0:1] + both[:, 1:2]) / weights, (rows, LANES))
    route_out[...] = jnp.transpose(total)[0:1, :].astype(BF16)

    for c in range(pieces):
        own = down_term(r, c)
        pair(c).wait_recv()
        down_out[:, columns(c)] = (own + pair_in[c].astype(F32)).astype(BF16)

    @pl.when(inner)
    def _():
        hand_cut(r).wait_recv()
        for c in range(pieces):
            own = gate_term(r, c, 2 * slots)
            chain(1, c).wait_recv()
            gate_out[:, columns(c)] = (own + chain_in[1, c].astype(F32)).astype(BF16)

    @pl.when(outer)
    def _():
        for c in range(pieces):
            own = gate_term(r, c, slots)
            pass_on(c).wait_recv()
            gate_out[:, columns(c)] = (own + chain_in[0, c].astype(F32)).astype(BF16)

    for t in range(2):
        exchanged(t).wait_send()
    for c in range(pieces):
        far_exchanged(c).wait_send()
    returned_all().wait_send()
    for copy in raw_first():
        copy.wait_send()
    slice_copy(far_half).wait_send()
    over(pair_out, pair_in, pair_send, pair_recv.at[0], dp=partner).wait_send()

    @pl.when(inner)
    def _():
        raw_last().wait_send()
        from_relay().wait_send()
        over(chain_out, chain_in, chain_send, chain_recv.at[0, 0], dp=opposite).wait_send()
        over(chain_in.at[0], chain_in.at[0], on_send, on_recv.at[0], dp=partner).wait_send()

    @pl.when(outer)
    def _():
        to_relay().wait_send()
        cuts = pl.ds(0, 3 * part)
        over(
            da_t.at[cuts, own_rows], da_t.at[cuts, more_rows], cut_send, cut_recv.at[0], dp=partner
        ).wait_send()
        over(
            got_x.at[own_rows], got_x.at[more_rows], x_send, x_recv.at[0], dp=partner
        ).wait_send()


def settle(token, route, gate, down, token_out, route_out, gate_out, down_out, sems):
    copies = [
        pltpu.make_async_copy(source, out, sems.at[i])
        for i, (source, out) in enumerate((
            (gate, gate_out), (down, down_out), (token, token_out), (route, route_out),
        ))
    ]
    for copy in copies:
        copy.start()
    for copy in copies:
        copy.wait()


def chain_scratch(n_dp, n_exp, pieces, slots, units, part, width, piece, rows):
    dma = pltpu.SemaphoreType.DMA
    return [
        pltpu.VMEM((2, slots, width), BF16),
        pltpu.VMEM((2, 2 * slots, width), BF16),
        pltpu.VMEM((units, width), BF16),
        pltpu.VMEM((units, width), BF16),
        pltpu.VMEM((units, slots), F32),
        pltpu.VMEM((units, 2 * slots), BF16),
        pltpu.VMEM((units, 2 * slots), BF16),
        pltpu.VMEM((slots, width + LANES), BF16),
        pltpu.VMEM((slots, width + LANES), BF16),
        pltpu.VMEM((2, n_dp - 1, pieces, part, piece), BF16),
        pltpu.VMEM((2, n_dp - 1, pieces, part, piece), BF16),
        dma((2,)),
        dma((2, n_exp)), dma((2, n_exp)), dma((n_exp,)), dma((n_exp,)),
        dma((2, n_dp - 1, pieces)), dma((2, n_dp - 1, pieces)),
        dma((2, n_dp - 1, pieces)), dma((2, n_dp - 1, pieces)),
        dma((n_exp,)), dma((n_exp,)), dma((pieces,)), dma((pieces,)),
        dma((2, n_dp)), dma((2, n_dp)),
    ]


def four_scratch(n_dp, n_exp, pieces, slots, units, part, width, piece, rows):
    dma = pltpu.SemaphoreType.DMA
    return [
        pltpu.VMEM((1, rows), jnp.int32),
        pltpu.VMEM((rows, width), BF16),
        pltpu.VMEM((1, rows), BF16),
        pltpu.VMEM((rows, width), BF16),
        pltpu.VMEM((2, slots, width), BF16),
        pltpu.VMEM((2 * slots, width), BF16),
        pltpu.VMEM((2 * slots, width), BF16),
        pltpu.VMEM((units, width), BF16),
        pltpu.VMEM((units, width), BF16),
        pltpu.VMEM((units, slots), F32),
        pltpu.VMEM((units, 2 * slots), BF16),
        pltpu.VMEM((units, 2 * slots), BF16),
        pltpu.VMEM((slots, width + LANES), BF16),
        pltpu.VMEM((slots, width + LANES), BF16),
        pltpu.VMEM((rows, width), BF16),
        pltpu.VMEM((rows, width), BF16),
        pltpu.VMEM((1, rows), jnp.int32),
        pltpu.VMEM((rows, pieces // 2 * piece), BF16),
        pltpu.VMEM((slots, width), BF16),
        pltpu.VMEM((2, pieces, part, piece), BF16),
        pltpu.VMEM((2, pieces, part, piece), BF16),
        pltpu.VMEM((pieces, part, piece), BF16),
        pltpu.VMEM((pieces, part, piece), BF16),
        dma((6,)), dma((2,)), dma((2,)), dma((3,)), dma((3,)), dma, dma, dma((pieces,)), dma((pieces,)),
        dma, dma, dma, dma((n_dp,)), dma, dma((pieces,)),
        dma, dma((2, pieces)), dma, dma((pieces,)), dma, dma((pieces,)), dma, dma,
    ]


def per_device(tokens, expert_ids, route_weights, out_grad, gate_weight, down_weight):
    rows, width = tokens.shape
    n_exp, n_dp = lax.axis_size("expert"), lax.axis_size("dp")
    top = expert_ids.shape[1]
    assert top == 1 and n_dp >= 4
    cap = -(-max(2, 2 * rows * top // n_exp) // 16) * 16
    slots = n_exp * cap
    units = gate_weight.shape[1]
    part = units // n_dp
    pieces = max(1, width // 512)
    piece = width // pieces
    shapes = (
        jax.ShapeDtypeStruct((rows, width), BF16),
        jax.ShapeDtypeStruct((1, rows), BF16),
        jax.ShapeDtypeStruct((part, width), BF16),
        jax.ShapeDtypeStruct((part, width), BF16),
    )
    vmem = pl.BlockSpec(memory_space=pltpu.VMEM)
    hbm = pl.BlockSpec(memory_space=pl.ANY)
    four = n_dp == 4
    body = (
        functools.partial(kernel_four, n_exp, cap, pieces)
        if four
        else functools.partial(kernel, n_dp, n_exp, cap, pieces)
    )
    scratch = four_scratch if four else chain_scratch
    results = pl.pallas_call(
        body,
        out_shape=tuple(pltpu.VMEM(a.shape, a.dtype) for a in shapes) if four else shapes,
        in_specs=[hbm] * 6 if four else [vmem] * 4 + [hbm] * 2,
        out_specs=(vmem,) * 4,
        scratch_shapes=scratch(n_dp, n_exp, pieces, slots, units, part, width, piece, rows),
        compiler_params=pltpu.CompilerParams(
            collective_id=0, has_side_effects=True,
            vmem_limit_bytes=60_000_000 if four else 67_000_000,

        ),
    )(
        expert_ids.reshape(1, rows), tokens, route_weights.reshape(1, rows), out_grad,
        gate_weight[0], down_weight[0],
    )
    if four:
        results = [pltpu.with_memory_space_constraint(a, pltpu.VMEM) for a in results]
    token_grad, route_grad, gate_grad, down_grad = pl.pallas_call(
        settle,
        out_shape=shapes,
        in_specs=[vmem] * 4,
        out_specs=(hbm,) * 4,
        scratch_shapes=[pltpu.SemaphoreType.DMA((4,))],
    )(*results)
    return token_grad, route_grad.reshape(rows, 1), gate_grad[None], down_grad[None]


def solution(mesh):
    placed = (
        P(("dp", "expert"), None),
        P(("dp", "expert"), None),
        P(("dp", "expert"), None),
        P(("dp", "expert"), None),
        P("expert", None, None),
        P("expert", None, None),
    )
    return jax.shard_map(
        per_device,
        mesh=mesh,
        in_specs=placed,
        out_specs=(
            P(("dp", "expert"), None),
            P(("dp", "expert"), None),
            P("expert", "dp", None),
            P("expert", "dp", None),
        ),
        check_vma=False,
    )
```

```python
import functools

import jax
import jax.numpy as jnp
from jax import lax
from jax.experimental import pallas as pl
from jax.experimental.pallas import tpu as pltpu
from jax.sharding import PartitionSpec as P

MESH = pl.DeviceIdType.MESH
BF16, F32 = jnp.bfloat16, jnp.float32
LANES = 128


def placement(ids, n_exp, cap):
    rows = ids.shape[1]
    slots = n_exp * cap
    names = lax.broadcasted_iota(jnp.int32, (max(n_exp, 16), rows), 0)
    one_hot = (names == ids).astype(F32)
    before = (
        lax.broadcasted_iota(jnp.int32, (rows, rows), 0)
        < lax.broadcasted_iota(jnp.int32, (rows, rows), 1)
    ).astype(F32)
    counts = jnp.dot(one_hot.astype(BF16), before.astype(BF16), preferred_element_type=F32)
    rank = jnp.sum(counts * one_hot, axis=0, keepdims=True).astype(jnp.int32)
    target = ids * cap + rank
    match = lax.broadcasted_iota(jnp.int32, (slots, rows), 0) == target
    return match.astype(F32).astype(BF16)


def kernel(
    n_dp, n_exp, cap, pieces,
    ids_ref, tokens_ref, weights_ref, grads_ref, gate_hbm, down_hbm,
    token_out, route_out, gate_out, down_out,
    sent, got, gate, down, preact, hid_t, da_t, back, returned, right_buf, left_buf,
    load_sem, send_sem, recv_sem, back_send, back_recv, r_send, r_recv, l_send, l_recv,
    x_send, x_recv, g_send, g_recv, cut_send, cut_recv,
):
    rows, width = tokens_ref.shape
    slots = n_exp * cap
    units = gate.shape[0]
    part = units // n_dp
    piece = width // pieces
    tile = 256 if units % 256 == 0 else part
    r = lax.axis_index("dp")
    me = lax.axis_index("expert")

    def peer(k):
        return lax.rem(me + k, n_exp)

    def block(e):
        return pl.ds(pl.multiple_of(e * cap, cap), cap)

    loads = [
        pltpu.make_async_copy(gate_hbm, gate, load_sem.at[0]),
        pltpu.make_async_copy(down_hbm, down, load_sem.at[1]),
    ]
    for load in loads:
        load.start()

    barrier = pltpu.get_barrier_semaphore()

    @pl.loop(1, n_exp)
    def _(k):
        pl.semaphore_signal(barrier, inc=1, device_id={"expert": peer(k)}, device_id_type=MESH)

    up, low = lax.rem(r + 1, n_dp), lax.rem(r + n_dp - 1, n_dp)

    @pl.loop(1, n_dp)
    def _(k):
        other = lax.rem(r + k, n_dp)
        pl.semaphore_signal(barrier, inc=1, device_id={"dp": other}, device_id_type=MESH)

    place = placement(ids_ref[...], n_exp, cap)
    sent[0] = jnp.dot(place, tokens_ref[...], preferred_element_type=F32).astype(BF16)
    pl.semaphore_wait(barrier, n_exp - 1 + n_dp - 1)

    def exchange(t, k):
        to = peer(k)
        return pltpu.make_async_remote_copy(
            src_ref=sent.at[t, block(to)],
            dst_ref=got.at[t, block(me)],
            send_sem=send_sem.at[t, to],
            recv_sem=recv_sem.at[t, me],
            device_id={"expert": to},
            device_id_type=MESH,
        )

    def arrival(t, k):
        of = peer(k)
        return pltpu.make_async_remote_copy(
            src_ref=sent.at[t, block(of)],
            dst_ref=got.at[t, block(of)],
            send_sem=send_sem.at[t, of],
            recv_sem=recv_sem.at[t, of],
            device_id={"expert": of},
            device_id_type=MESH,
        )

    @pl.loop(1, n_exp)
    def _(k):
        exchange(0, k).start()

    got[0, block(me)] = sent[0, block(me)]
    weights = jnp.transpose(
        jnp.broadcast_to(weights_ref[...].astype(F32), (LANES, rows))
    )[:, 0:1]
    scaled = (weights * grads_ref[...].astype(F32)).astype(BF16)
    sent[1] = jnp.dot(place, scaled, preferred_element_type=F32).astype(BF16)

    @pl.loop(1, n_exp)
    def _(k):
        exchange(1, k).start()

    got[1, block(me)] = sent[1, block(me)]

    for load in loads:
        load.wait()

    end = jnp.logical_or(r == 0, r == n_dp - 1)
    after_end = jnp.logical_or(r == 1, r == n_dp - 2)
    inner = jnp.where(r == 0, up, low)
    lower = r < n_dp // 2

    def hand_x(e):
        return pltpu.make_async_remote_copy(
            src_ref=got.at[0, block(e)],
            dst_ref=got.at[0, pl.ds(pl.multiple_of(slots + e * cap, cap), cap)],
            send_sem=x_send.at[e],
            recv_sem=x_recv.at[e],
            device_id={"dp": inner},
            device_id_type=MESH,
        )

    def hand_g(c):
        span = pl.ds(pl.multiple_of(c * piece, piece), piece)
        return pltpu.make_async_remote_copy(
            src_ref=got.at[1, pl.ds(0, slots), span],
            dst_ref=got.at[1, pl.ds(slots, slots), span],
            send_sem=g_send.at[c],
            recv_sem=g_recv.at[c],
            device_id={"dp": inner},
            device_id_type=MESH,
        )

    def hand_cut(t, d):
        left = da_t if t == 0 else hid_t
        own = pl.ds(pl.multiple_of(d * part, part), part)
        return pltpu.make_async_remote_copy(
            src_ref=left.at[own, pl.ds(0, slots)],
            dst_ref=left.at[own, pl.ds(slots, slots)],
            send_sem=cut_send.at[t, d],
            recv_sem=cut_recv.at[t, d],
            device_id={"dp": inner},
            device_id_type=MESH,
        )

    @pl.when(end)
    def _():
        hand_x(me).start()

    @pl.loop(1, n_exp)
    def _(k):
        arrival(0, k).wait_recv()

        @pl.when(end)
        def _():
            hand_x(peer(k)).start()

    nt = (((1,), (1,)), ((), ()))

    @pl.loop(0, units // tile)
    def _(j):
        span = pl.ds(pl.multiple_of(j * tile, tile), tile)
        value = lax.dot_general(
            gate[span, :], got[0, 0:slots, :], nt, preferred_element_type=F32
        )
        preact[span, :] = value
        hid_t[span, 0:slots] = (value * jax.nn.sigmoid(value)).astype(BF16)

    def hand_cuts(t):
        @pl.when(end)
        def _():
            @pl.loop(0, n_dp - 1)
            def _(j):
                hand_cut(t, jnp.where(r == 0, n_dp - 1 - j, j)).start()

    @pl.loop(1, n_exp)
    def _(k):
        arrival(1, k).wait_recv()

    def second(j, total):
        span = pl.ds(pl.multiple_of(j * tile, tile), tile)
        slope = lax.dot_general(
            down[span, :], got[1, 0:slots, :], nt, preferred_element_type=F32
        )
        value = preact[span, :]
        sigma = jax.nn.sigmoid(value)
        da_t[span, 0:slots] = (slope * (sigma * (1.0 + value * (1.0 - sigma)))).astype(BF16)
        return total + jnp.sum(hid_t[span, 0:slots].astype(F32) * slope, axis=0, keepdims=True)

    route = lax.fori_loop(0, units // tile, second, jnp.zeros((1, slots), F32))

    hand_cuts(0)
    hand_cuts(1)

    @pl.when(end)
    def _():
        @pl.loop(0, pieces)
        def _(c):
            hand_g(c).start()

    def term(t, d, span, wide):
        left = da_t if t == 0 else hid_t
        start = d * part if isinstance(d, int) else pl.multiple_of(d * part, part)
        depth = 2 * slots if wide else slots
        return jnp.dot(
            left[pl.ds(start, part), 0:depth],
            got[t, 0:depth, span],
            preferred_element_type=F32,
        )

    def columns(c):
        return pl.ds(pl.multiple_of(c * piece, piece), piece)

    def hop(buf, s_sem, r_sem, t, d, c, to):
        return pltpu.make_async_remote_copy(
            src_ref=buf.at[t, d, c],
            dst_ref=buf.at[t, d, c],
            send_sem=s_sem.at[t, d, c],
            recv_sem=r_sem.at[t, d, c],
            device_id={"dp": to},
            device_id_type=MESH,
        )

    def rightward(t, d, c, to=None):
        return hop(right_buf, r_send, r_recv, t, d - 1, c, up)

    def leftward(t, d, c, to=None):
        return hop(left_buf, l_send, l_recv, t, d, c, low)

    def pass_on(t, d, c, copy, buf, index, first):
        @pl.when(first)
        def _():
            buf[t, index, c] = term(t, d, columns(c), True).astype(BF16)

        @pl.when(jnp.logical_not(first))
        def _():
            own = term(t, d, columns(c), False)
            copy.wait_recv()
            buf[t, index, c] = (own + buf[t, index, c].astype(F32)).astype(BF16)

        copy.start()

    def go_right(t):
        for d in range(n_dp - 1, 1, -1):

            @pl.when(r == 1)
            def _():
                hand_cut(t, d).wait_recv()

            @pl.when(jnp.logical_and(r > 0, r < d))
            def _():
                @pl.loop(0, pieces)
                def _(c):
                    if t == 1 and d == n_dp - 1:

                        @pl.when(r == 1)
                        def _():
                            hand_g(c).wait_recv()

                    pass_on(t, d, c, rightward(t, d, c), right_buf, d - 1, r == 1)

    def go_left(t):
        for d in range(n_dp - 2):

            @pl.when(r == n_dp - 2)
            def _():
                hand_cut(t, d).wait_recv()

            @pl.when(jnp.logical_and(r < n_dp - 1, r > d))
            def _():
                @pl.loop(0, pieces)
                def _(c):
                    if t == 1 and d == 0:

                        @pl.when(r == n_dp - 2)
                        def _():
                            hand_g(c).wait_recv()

                    pass_on(t, d, c, leftward(t, d, c), left_buf, d, r == n_dp - 2)

    def returning(k):
        to = peer(k)
        return pltpu.make_async_remote_copy(
            src_ref=back.at[block(to)],
            dst_ref=returned.at[block(me)],
            send_sem=back_send.at[to],
            recv_sem=back_recv.at[me],
            device_id={"expert": to},
            device_id_type=MESH,
        )

    def homecoming(k):
        of = peer(k)
        return pltpu.make_async_remote_copy(
            src_ref=back.at[block(of)],
            dst_ref=returned.at[block(of)],
            send_sem=back_send.at[of],
            recv_sem=back_recv.at[of],
            device_id={"expert": of},
            device_id_type=MESH,
        )

    def send_back():
        tn = (((0,), (0,)), ((), ()))

        @pl.loop(0, pieces)
        def _(c):
            span = columns(c)
            back[:, span] = lax.dot_general(
                da_t[:, 0:slots], gate[:, span], tn, preferred_element_type=F32
            ).astype(BF16)

        tall = jnp.transpose(jnp.broadcast_to(route, (LANES, slots)))
        high = tall.astype(BF16)
        rest = (tall - high.astype(F32)).astype(BF16)
        lane = lax.broadcasted_iota(jnp.int32, (slots, LANES), 1)
        back[:, pl.ds(width, LANES)] = jnp.where(
            lane < 1, high.astype(F32), rest.astype(F32)
        ).astype(BF16)

        @pl.loop(1, n_exp)
        def _(k):
            returning(k).start()

        returned[block(me), :] = back[block(me), :]

    send_back()

    @pl.when(after_end)
    def _():
        @pl.loop(0, n_exp)
        def _(e):
            hand_x(e).wait_recv()

    for t in range(2):

        @pl.when(lower)
        def _():
            go_right(t)

        go_left(t)

        @pl.when(jnp.logical_not(lower))
        def _():
            go_right(t)

    @pl.loop(1, n_exp)
    def _(k):
        homecoming(k).wait_recv()

    tn = (((0,), (0,)), ((), ()))

    @pl.loop(0, pieces)
    def _(c):
        span = columns(c)
        token_out[:, span] = lax.dot_general(
            place, returned[:, span], tn, preferred_element_type=F32
        ).astype(BF16)

    pair = lax.dot_general(
        place, returned[:, pl.ds(width, LANES)], tn, preferred_element_type=F32
    )
    total = jnp.broadcast_to((pair[:, 0:1] + pair[:, 1:2]) / weights, (rows, LANES))
    route_out[...] = jnp.transpose(total)[0:1, :].astype(BF16)

    for t in range(2):
        out = gate_out if t == 0 else down_out

        @pl.when(after_end)
        def _():
            hand_cut(t, r).wait_recv()

        @pl.loop(0, pieces)
        def _(c):
            span = columns(c)

            def from_right():
                hop(left_buf, l_send, l_recv, t, r, c, low).wait_recv()
                return left_buf[t, r, c].astype(F32)

            def from_left():
                hop(right_buf, r_send, r_recv, t, r - 1, c, up).wait_recv()
                return right_buf[t, r - 1, c].astype(F32)

            @pl.when(r == 0)
            def _():
                out[:, span] = (term(t, r, span, False) + from_right()).astype(BF16)

            @pl.when(r == n_dp - 1)
            def _():
                out[:, span] = (term(t, r, span, False) + from_left()).astype(BF16)

            @pl.when(r == 1)
            def _():
                out[:, span] = (term(t, r, span, True) + from_right()).astype(BF16)

            @pl.when(r == n_dp - 2)
            def _():
                out[:, span] = (term(t, r, span, True) + from_left()).astype(BF16)

            @pl.when(jnp.logical_and(r > 1, r < n_dp - 2))
            def _():
                out[:, span] = (term(t, r, span, False) + from_right() + from_left()).astype(BF16)

    @pl.loop(1, n_exp)
    def _(k):
        exchange(0, k).wait_send()
        exchange(1, k).wait_send()
        returning(k).wait_send()

    @pl.when(end)
    def _():
        @pl.loop(0, n_exp)
        def _(e):
            hand_x(e).wait_send()

        @pl.loop(0, pieces)
        def _(c):
            hand_g(c).wait_send()

        for t in range(2):

            @pl.loop(0, n_dp - 1)
            def _(j):
                hand_cut(t, jnp.where(r == 0, n_dp - 1 - j, j)).wait_send()

    for t in range(2):
        for d in range(n_dp):

            @pl.loop(0, pieces)
            def _(c):
                if d > 1:

                    @pl.when(jnp.logical_and(r > 0, r < d))
                    def _():
                        rightward(t, d, c).wait_send()

                if d < n_dp - 2:

                    @pl.when(jnp.logical_and(r < n_dp - 1, r > d))
                    def _():
                        leftward(t, d, c).wait_send()


def kernel_four(
    n_exp, cap, pieces,
    ids_hbm, tokens_hbm, weights_hbm, grads_hbm, gate_hbm, down_hbm,
    token_out, route_out, gate_out, down_out,
    ids_ref, tokens_ref, weights_ref, grads_ref,
    sent, got_x, got_g, gate, down, preact, hid_t, da_t, back, returned,
    scaled, raw, raw_ids, relay, far_sent, chain_out, chain_in, pair_out, pair_in,
    load_sem, send_sem, recv_sem, raw_send, raw_recv, relay_send, relay_recv, far_send, far_recv,
    slice_send, slice_recv, cut_send, cut_recv, x_send, x_recv,
    chain_send, chain_recv, on_send, on_recv, pair_send, pair_recv, back_send, back_recv,
):
    rows, width = tokens_ref.shape
    slots = n_exp * cap
    units = gate.shape[0]
    part = units // 4
    piece = width // pieces
    early = (pieces + 1) // 2
    half = early * piece
    tile = 256 if units % 256 == 0 else part
    r = lax.axis_index("dp")
    me = lax.axis_index("expert")
    partner = r + 1 - 2 * lax.rem(r, 2)
    far = lax.rem(r + 2, 4)
    opposite = 3 - r
    inner = jnp.logical_or(r == 1, r == 2)
    outer = jnp.logical_or(r == 0, r == 3)

    def peer(k):
        return lax.rem(me + k, n_exp)

    def block(e):
        return pl.ds(pl.multiple_of(e * cap, cap), cap)

    def far_block(e):
        return pl.ds(pl.multiple_of(slots + e * cap, cap), cap)

    def units_of(d):
        return pl.ds(pl.multiple_of(d * part, part), part)

    def columns(c):
        return pl.ds(c * piece, piece)

    near_half, far_half = (
        pl.ds(pl.multiple_of(jnp.where(cond, 0, 2 * part), part), 2 * part)
        for cond in (r < 2, r > 1)
    )
    own_rows, more_rows = pl.ds(0, slots), pl.ds(slots, slots)

    loads = [
        pltpu.make_async_copy(source, held, load_sem.at[i])
        for i, (source, held) in enumerate((
            (weights_hbm, weights_ref), (grads_hbm, grads_ref), (ids_hbm, ids_ref),
            (tokens_hbm, tokens_ref),
            (gate_hbm, gate), (down_hbm, down),
        ))
    ]
    for load in loads[:4]:
        load.start()

    barrier = pltpu.get_barrier_semaphore()

    @pl.loop(1, n_exp)
    def _(k):
        pl.semaphore_signal(barrier, inc=1, device_id={"expert": peer(k)}, device_id_type=MESH)

    @pl.loop(1, 4)
    def _(k):
        other = lax.rem(r + k, 4)
        pl.semaphore_signal(barrier, inc=1, device_id={"dp": other}, device_id_type=MESH)

    for load in loads[4:]:
        load.start()

    def over(src, dst, s_sem, r_sem, **to):
        return pltpu.make_async_remote_copy(
            src_ref=src, dst_ref=dst, send_sem=s_sem, recv_sem=r_sem,
            device_id=to, device_id_type=MESH,
        )

    def exchange(t, to, at, device):
        got = got_g if t else got_x
        return over(
            sent.at[t, block(to)], got.at[block(at)],
            send_sem.at[t], recv_sem.at[t], expert=device,
        )

    def far_exchange(c, to, at, device):
        return over(
            far_sent.at[block(to), columns(c)], got_g.at[far_block(at), columns(c)],
            far_send.at[c], far_recv.at[c], expert=device,
        )

    def returning(to, at, device):
        return over(
            back.at[block(to)], returned.at[block(at)],
            back_send, back_recv, expert=device,
        )

    first, last = pl.ds(0, half), pl.ds(half, width - half)

    def raw_first():
        return [
            over(ids_ref, raw_ids, raw_send.at[0], raw_recv.at[0], dp=far),
            over(scaled.at[:, first], raw.at[:, first], raw_send.at[1], raw_recv.at[1], dp=far),
        ]

    def raw_last():
        return over(scaled.at[:, last], raw.at[:, last], raw_send.at[2], raw_recv.at[2], dp=far)

    def to_relay():
        return over(scaled.at[:, last], relay, relay_send, relay_recv, dp=partner)

    def from_relay():
        return over(relay, raw.at[:, last], relay_send, raw_recv.at[2], dp=opposite)

    def slice_copy(half):
        return over(
            hid_t.at[half, own_rows], hid_t.at[half, more_rows], slice_send, slice_recv, dp=far
        )

    def hand_x(c):
        return over(
            got_x.at[own_rows, columns(c)], got_x.at[more_rows, columns(c)],
            x_send, x_recv.at[c], dp=partner,
        )

    def hand_cut(d):
        return over(
            da_t.at[units_of(d), own_rows], da_t.at[units_of(d), more_rows],
            cut_send, cut_recv.at[d], dp=partner,
        )

    def chain(i, c):
        return over(
            chain_out.at[i, c], chain_in.at[i, c], chain_send, chain_recv.at[i, c],
            dp=opposite,
        )

    def pass_on(c):
        return over(
            chain_in.at[0, c], chain_in.at[0, c], on_send, on_recv.at[c], dp=partner
        )

    def pair(c):
        return over(
            pair_out.at[c], pair_in.at[c], pair_send, pair_recv.at[c], dp=partner
        )

    others = pl.ds(0, (n_exp - 1) * cap)

    def exchanged(t):
        return over(
            sent.at[t, others], (got_g if t else got_x).at[others],
            send_sem.at[t], recv_sem.at[t], dp=partner,
        )

    def far_exchanged(c):
        return over(
            far_sent.at[others, columns(c)], got_g.at[others, columns(c)],
            far_send.at[c], far_recv.at[c], dp=partner,
        )

    def returned_all():
        return over(back.at[others], returned.at[others], back_send, back_recv, dp=partner)

    loads[0].wait()
    weights = jnp.transpose(
        jnp.broadcast_to(weights_ref[...].astype(F32), (LANES, rows))
    )[:, 0:1]
    loads[1].wait()
    scaled[...] = (weights * grads_ref[...].astype(F32)).astype(BF16)
    loads[2].wait()
    place = placement(ids_ref[...], n_exp, cap)
    pl.semaphore_wait(barrier, n_exp - 1 + 3)

    for copy in raw_first():
        copy.start()

    @pl.when(inner)
    def _():
        raw_last().start()

    @pl.when(outer)
    def _():
        to_relay().start()

    loads[3].wait()
    sent[0] = jnp.dot(place, tokens_ref[...], preferred_element_type=F32).astype(BF16)

    @pl.loop(1, n_exp)
    def _(k):
        exchange(0, peer(k), me, peer(k)).start()

    sent[1] = jnp.dot(place, scaled[...], preferred_element_type=F32).astype(BF16)

    @pl.loop(1, n_exp)
    def _(k):
        exchange(1, peer(k), me, peer(k)).start()

    got_x[block(me)] = sent[0, block(me)]
    got_g[block(me)] = sent[1, block(me)]

    for load in loads[4:]:
        load.wait()

    exchanged(0).wait_recv()

    @pl.when(outer)
    def _():
        hand_x(0).start()

    nt = (((1,), (1,)), ((), ()))
    tn = (((0,), (0,)), ((), ()))

    @pl.loop(0, units // tile)
    def _(j):
        span = pl.ds(pl.multiple_of(j * tile, tile), tile)
        value = lax.dot_general(
            gate[span, :], got_x[0:slots, :], nt, preferred_element_type=F32
        )
        preact[span, :] = value
        hid_t[span, 0:slots] = (value * jax.nn.sigmoid(value)).astype(BF16)

    slice_copy(far_half).start()

    @pl.when(inner)
    def _():
        to_relay().wait_recv()
        from_relay().start()

    @pl.when(outer)
    def _():
        hand_x(1).start()

    def far_dispatch(chunks):
        for c in chunks:
            span = columns(c)
            far_sent[:, span] = jnp.dot(
                far_place, raw[:, span], preferred_element_type=F32
            ).astype(BF16)

            @pl.loop(1, n_exp)
            def _(k):
                far_exchange(c, peer(k), me, peer(k)).start()

            got_g[far_block(me), span] = far_sent[block(me), span]

    for copy in raw_first():
        copy.wait_recv()
    far_place = placement(raw_ids[...], n_exp, cap)
    far_dispatch(range(early))

    def far_rest():
        raw_last().wait_recv()
        far_dispatch(range(early, pieces))

    @pl.when(outer)
    def _():
        far_rest()

    exchanged(1).wait_recv()

    def second(j, total):
        span = pl.ds(pl.multiple_of(j * tile, tile), tile)
        slope = lax.dot_general(
            down[span, :], got_g[0:slots, :], nt, preferred_element_type=F32
        )
        value = preact[span, :]
        sigma = jax.nn.sigmoid(value)
        da_t[span, 0:slots] = (slope * (sigma * (1.0 + value * (1.0 - sigma)))).astype(BF16)
        return total + jnp.sum(hid_t[span, 0:slots].astype(F32) * slope, axis=0, keepdims=True)

    route = lax.fori_loop(0, units // tile, second, jnp.zeros((1, slots), F32))

    @pl.when(outer)
    def _():
        for d in (opposite, far, partner):
            hand_cut(d).start()
        for c in range(2, pieces):
            hand_x(c).start()

    def gate_term(d, c, depth):
        return jnp.dot(
            da_t[units_of(d), 0:depth], got_x[0:depth, columns(c)], preferred_element_type=F32
        )

    def down_term(d, c):
        return jnp.dot(
            hid_t[units_of(d), :], got_g[:, columns(c)], preferred_element_type=F32
        )

    def send_pair(c):
        far_exchanged(c).wait_recv()
        pair_out[c] = down_term(partner, c).astype(BF16)
        pair(c).start()

    def send_chain(i, c):
        d = opposite if i else far
        if c == 0:
            hand_cut(d).wait_recv()
        if i == 0:
            hand_x(c).wait_recv()
        chain_out[i, c] = gate_term(d, c, 2 * slots).astype(BF16)
        chain(i, c).start()

    def forward(c):
        own = gate_term(partner, c, slots)
        chain(0, c).wait_recv()
        chain_in[0, c] = (own + chain_in[0, c].astype(F32)).astype(BF16)
        pass_on(c).start()

    def send_back():
        for c in range(pieces):
            span = columns(c)
            back[:, span] = lax.dot_general(
                da_t[:, 0:slots], gate[:, span], tn, preferred_element_type=F32
            ).astype(BF16)

        tall = jnp.transpose(jnp.broadcast_to(route, (LANES, slots)))
        high = tall.astype(BF16)
        rest = (tall - high.astype(F32)).astype(BF16)
        lane = lax.broadcasted_iota(jnp.int32, (slots, LANES), 1)
        back[:, pl.ds(width, LANES)] = jnp.where(
            lane < 1, high.astype(F32), rest.astype(F32)
        ).astype(BF16)

        @pl.loop(1, n_exp)
        def _(k):
            returning(peer(k), me, peer(k)).start()

        returned[block(me), :] = back[block(me), :]

    slice_copy(near_half).wait_recv()

    @pl.when(inner)
    def _():
        steps = [(send_pair, 0), (send_chain, 0, 0)]
        for c in range(1, pieces):
            ahead = [(send_pair, c), (send_chain, 0, c)]
            steps += (ahead[::-1] if c < early else ahead) + [(send_chain, 1, c - 1), (forward, c - 1)]
            if c == 1:
                steps.insert(3, (far_rest,))
        steps.insert(-2, (send_back,))
        steps += [(send_chain, 1, pieces - 1), (forward, pieces - 1)]
        for step, *args in steps:
            step(*args)

    @pl.when(outer)
    def _():
        for c in range(pieces):
            send_pair(c)
        send_back()

    returned_all().wait_recv()

    for c in range(pieces):
        span = columns(c)
        token_out[:, span] = lax.dot_general(
            place, returned[:, span], tn, preferred_element_type=F32
        ).astype(BF16)

    both = lax.dot_general(
        place, returned[:, pl.ds(width, LANES)], tn, preferred_element_type=F32
    )
    total = jnp.broadcast_to((both[:, 0:1] + both[:, 1:2]) / weights, (rows, LANES))
    route_out[...] = jnp.transpose(total)[0:1, :].astype(BF16)

    for c in range(pieces):
        own = down_term(r, c)
        pair(c).wait_recv()
        down_out[:, columns(c)] = (own + pair_in[c].astype(F32)).astype(BF16)

    @pl.when(inner)
    def _():
        hand_cut(r).wait_recv()
        for c in range(pieces):
            own = gate_term(r, c, 2 * slots)
            chain(1, c).wait_recv()
            gate_out[:, columns(c)] = (own + chain_in[1, c].astype(F32)).astype(BF16)

    @pl.when(outer)
    def _():
        for c in range(pieces):
            own = gate_term(r, c, slots)
            pass_on(c).wait_recv()
            gate_out[:, columns(c)] = (own + chain_in[0, c].astype(F32)).astype(BF16)

    for t in range(2):
        exchanged(t).wait_send()
    for c in range(pieces):
        far_exchanged(c).wait_send()
    returned_all().wait_send()
    for copy in raw_first():
        copy.wait_send()
    slice_copy(far_half).wait_send()
    over(pair_out, pair_in, pair_send, pair_recv.at[0], dp=partner).wait_send()

    @pl.when(inner)
    def _():
        raw_last().wait_send()
        from_relay().wait_send()
        over(chain_out, chain_in, chain_send, chain_recv.at[0, 0], dp=opposite).wait_send()
        over(chain_in.at[0], chain_in.at[0], on_send, on_recv.at[0], dp=partner).wait_send()

    @pl.when(outer)
    def _():
        to_relay().wait_send()
        cuts = pl.ds(0, 3 * part)
        over(
            da_t.at[cuts, own_rows], da_t.at[cuts, more_rows], cut_send, cut_recv.at[0], dp=partner
        ).wait_send()
        over(
            got_x.at[own_rows], got_x.at[more_rows], x_send, x_recv.at[0], dp=partner
        ).wait_send()


def settle(token, route, gate, down, token_out, route_out, gate_out, down_out, sems):
    copies = [
        pltpu.make_async_copy(source, out, sems.at[i])
        for i, (source, out) in enumerate((
            (gate, gate_out), (down, down_out), (token, token_out), (route, route_out),
        ))
    ]
    for copy in copies:
        copy.start()
    for copy in copies:
        copy.wait()


def chain_scratch(n_dp, n_exp, pieces, slots, units, part, width, piece, rows):
    dma = pltpu.SemaphoreType.DMA
    return [
        pltpu.VMEM((2, slots, width), BF16),
        pltpu.VMEM((2, 2 * slots, width), BF16),
        pltpu.VMEM((units, width), BF16),
        pltpu.VMEM((units, width), BF16),
        pltpu.VMEM((units, slots), F32),
        pltpu.VMEM((units, 2 * slots), BF16),
        pltpu.VMEM((units, 2 * slots), BF16),
        pltpu.VMEM((slots, width + LANES), BF16),
        pltpu.VMEM((slots, width + LANES), BF16),
        pltpu.VMEM((2, n_dp - 1, pieces, part, piece), BF16),
        pltpu.VMEM((2, n_dp - 1, pieces, part, piece), BF16),
        dma((2,)),
        dma((2, n_exp)), dma((2, n_exp)), dma((n_exp,)), dma((n_exp,)),
        dma((2, n_dp - 1, pieces)), dma((2, n_dp - 1, pieces)),
        dma((2, n_dp - 1, pieces)), dma((2, n_dp - 1, pieces)),
        dma((n_exp,)), dma((n_exp,)), dma((pieces,)), dma((pieces,)),
        dma((2, n_dp)), dma((2, n_dp)),
    ]


def four_scratch(n_dp, n_exp, pieces, slots, units, part, width, piece, rows):
    dma = pltpu.SemaphoreType.DMA
    return [
        pltpu.VMEM((1, rows), jnp.int32),
        pltpu.VMEM((rows, width), BF16),
        pltpu.VMEM((1, rows), BF16),
        pltpu.VMEM((rows, width), BF16),
        pltpu.VMEM((2, slots, width), BF16),
        pltpu.VMEM((2 * slots, width), BF16),
        pltpu.VMEM((2 * slots, width), BF16),
        pltpu.VMEM((units, width), BF16),
        pltpu.VMEM((units, width), BF16),
        pltpu.VMEM((units, slots), F32),
        pltpu.VMEM((units, 2 * slots), BF16),
        pltpu.VMEM((units, 2 * slots), BF16),
        pltpu.VMEM((slots, width + LANES), BF16),
        pltpu.VMEM((slots, width + LANES), BF16),
        pltpu.VMEM((rows, width), BF16),
        pltpu.VMEM((rows, width), BF16),
        pltpu.VMEM((1, rows), jnp.int32),
        pltpu.VMEM((rows, pieces // 2 * piece), BF16),
        pltpu.VMEM((slots, width), BF16),
        pltpu.VMEM((2, pieces, part, piece), BF16),
        pltpu.VMEM((2, pieces, part, piece), BF16),
        pltpu.VMEM((pieces, part, piece), BF16),
        pltpu.VMEM((pieces, part, piece), BF16),
        dma((6,)), dma((2,)), dma((2,)), dma((3,)), dma((3,)), dma, dma, dma((pieces,)), dma((pieces,)),
        dma, dma, dma, dma((n_dp,)), dma, dma((pieces,)),
        dma, dma((2, pieces)), dma, dma((pieces,)), dma, dma((pieces,)), dma, dma,
    ]


def per_device(tokens, expert_ids, route_weights, out_grad, gate_weight, down_weight):
    rows, width = tokens.shape
    n_exp, n_dp = lax.axis_size("expert"), lax.axis_size("dp")
    top = expert_ids.shape[1]
    assert top == 1 and n_dp >= 4
    cap = -(-max(2, 2 * rows * top // n_exp) // 16) * 16
    slots = n_exp * cap
    units = gate_weight.shape[1]
    part = units // n_dp
    pieces = max(1, width // 512)
    piece = width // pieces
    shapes = (
        jax.ShapeDtypeStruct((rows, width), BF16),
        jax.ShapeDtypeStruct((1, rows), BF16),
        jax.ShapeDtypeStruct((part, width), BF16),
        jax.ShapeDtypeStruct((part, width), BF16),
    )
    vmem = pl.BlockSpec(memory_space=pltpu.VMEM)
    hbm = pl.BlockSpec(memory_space=pl.ANY)
    four = n_dp == 4
    body = (
        functools.partial(kernel_four, n_exp, cap, pieces)
        if four
        else functools.partial(kernel, n_dp, n_exp, cap, pieces)
    )
    scratch = four_scratch if four else chain_scratch
    results = pl.pallas_call(
        body,
        out_shape=tuple(pltpu.VMEM(a.shape, a.dtype) for a in shapes) if four else shapes,
        in_specs=[hbm] * 6 if four else [vmem] * 4 + [hbm] * 2,
        out_specs=(vmem,) * 4,
        scratch_shapes=scratch(n_dp, n_exp, pieces, slots, units, part, width, piece, rows),
        compiler_params=pltpu.CompilerParams(
            collective_id=0, has_side_effects=True,
            vmem_limit_bytes=60_000_000 if four else 67_000_000,

        ),
    )(
        expert_ids.reshape(1, rows), tokens, route_weights.reshape(1, rows), out_grad,
        gate_weight[0], down_weight[0],
    )
    if four:
        results = [pltpu.with_memory_space_constraint(a, pltpu.VMEM) for a in results]
    token_grad, route_grad, gate_grad, down_grad = pl.pallas_call(
        settle,
        out_shape=shapes,
        in_specs=[vmem] * 4,
        out_specs=(hbm,) * 4,
        scratch_shapes=[pltpu.SemaphoreType.DMA((4,))],
    )(*results)
    return token_grad, route_grad.reshape(rows, 1), gate_grad[None], down_grad[None]


def solution(mesh):
    placed = (
        P(("dp", "expert"), None),
        P(("dp", "expert"), None),
        P(("dp", "expert"), None),
        P(("dp", "expert"), None),
        P("expert", None, None),
        P("expert", None, None),
    )
    return jax.shard_map(
        per_device,
        mesh=mesh,
        in_specs=placed,
        out_specs=(
            P(("dp", "expert"), None),
            P(("dp", "expert"), None),
            P("expert", "dp", None),
            P("expert", "dp", None),
        ),
        check_vma=False,
    )
```

```python
import functools

import jax
import jax.numpy as jnp
from jax import lax
from jax.experimental import pallas as pl
from jax.experimental.pallas import tpu as pltpu
from jax.sharding import PartitionSpec as P

MESH = pl.DeviceIdType.MESH
BF16, F32 = jnp.bfloat16, jnp.float32
LANES = 128


def placement(ids, n_exp, cap):
    rows = ids.shape[1]
    slots = n_exp * cap
    names = lax.broadcasted_iota(jnp.int32, (max(n_exp, 16), rows), 0)
    one_hot = (names == ids).astype(F32)
    before = (
        lax.broadcasted_iota(jnp.int32, (rows, rows), 0)
        < lax.broadcasted_iota(jnp.int32, (rows, rows), 1)
    ).astype(F32)
    counts = jnp.dot(one_hot.astype(BF16), before.astype(BF16), preferred_element_type=F32)
    rank = jnp.sum(counts * one_hot, axis=0, keepdims=True).astype(jnp.int32)
    target = ids * cap + rank
    match = lax.broadcasted_iota(jnp.int32, (slots, rows), 0) == target
    return match.astype(F32).astype(BF16)


def kernel(
    n_dp, n_exp, cap, pieces,
    ids_ref, tokens_ref, weights_ref, grads_ref, gate_hbm, down_hbm,
    token_out, route_out, gate_out, down_out,
    sent, got, gate, down, preact, hid_t, da_t, back, returned, right_buf, left_buf,
    load_sem, send_sem, recv_sem, back_send, back_recv, r_send, r_recv, l_send, l_recv,
    x_send, x_recv, g_send, g_recv, cut_send, cut_recv,
):
    rows, width = tokens_ref.shape
    slots = n_exp * cap
    units = gate.shape[0]
    part = units // n_dp
    piece = width // pieces
    tile = 256 if units % 256 == 0 else part
    r = lax.axis_index("dp")
    me = lax.axis_index("expert")

    def peer(k):
        return lax.rem(me + k, n_exp)

    def block(e):
        return pl.ds(pl.multiple_of(e * cap, cap), cap)

    loads = [
        pltpu.make_async_copy(gate_hbm, gate, load_sem.at[0]),
        pltpu.make_async_copy(down_hbm, down, load_sem.at[1]),
    ]
    for load in loads:
        load.start()

    barrier = pltpu.get_barrier_semaphore()

    @pl.loop(1, n_exp)
    def _(k):
        pl.semaphore_signal(barrier, inc=1, device_id={"expert": peer(k)}, device_id_type=MESH)

    up, low = lax.rem(r + 1, n_dp), lax.rem(r + n_dp - 1, n_dp)

    @pl.loop(1, n_dp)
    def _(k):
        other = lax.rem(r + k, n_dp)
        pl.semaphore_signal(barrier, inc=1, device_id={"dp": other}, device_id_type=MESH)

    place = placement(ids_ref[...], n_exp, cap)
    sent[0] = jnp.dot(place, tokens_ref[...], preferred_element_type=F32).astype(BF16)
    pl.semaphore_wait(barrier, n_exp - 1 + n_dp - 1)

    def exchange(t, k):
        to = peer(k)
        return pltpu.make_async_remote_copy(
            src_ref=sent.at[t, block(to)],
            dst_ref=got.at[t, block(me)],
            send_sem=send_sem.at[t, to],
            recv_sem=recv_sem.at[t, me],
            device_id={"expert": to},
            device_id_type=MESH,
        )

    def arrival(t, k):
        of = peer(k)
        return pltpu.make_async_remote_copy(
            src_ref=sent.at[t, block(of)],
            dst_ref=got.at[t, block(of)],
            send_sem=send_sem.at[t, of],
            recv_sem=recv_sem.at[t, of],
            device_id={"expert": of},
            device_id_type=MESH,
        )

    @pl.loop(1, n_exp)
    def _(k):
        exchange(0, k).start()

    got[0, block(me)] = sent[0, block(me)]
    weights = jnp.transpose(
        jnp.broadcast_to(weights_ref[...].astype(F32), (LANES, rows))
    )[:, 0:1]
    scaled = (weights * grads_ref[...].astype(F32)).astype(BF16)
    sent[1] = jnp.dot(place, scaled, preferred_element_type=F32).astype(BF16)

    @pl.loop(1, n_exp)
    def _(k):
        exchange(1, k).start()

    got[1, block(me)] = sent[1, block(me)]

    for load in loads:
        load.wait()

    end = jnp.logical_or(r == 0, r == n_dp - 1)
    after_end = jnp.logical_or(r == 1, r == n_dp - 2)
    inner = jnp.where(r == 0, up, low)
    lower = r < n_dp // 2

    def hand_x(e):
        return pltpu.make_async_remote_copy(
            src_ref=got.at[0, block(e)],
            dst_ref=got.at[0, pl.ds(pl.multiple_of(slots + e * cap, cap), cap)],
            send_sem=x_send.at[e],
            recv_sem=x_recv.at[e],
            device_id={"dp": inner},
            device_id_type=MESH,
        )

    def hand_g(c):
        span = pl.ds(pl.multiple_of(c * piece, piece), piece)
        return pltpu.make_async_remote_copy(
            src_ref=got.at[1, pl.ds(0, slots), span],
            dst_ref=got.at[1, pl.ds(slots, slots), span],
            send_sem=g_send.at[c],
            recv_sem=g_recv.at[c],
            device_id={"dp": inner},
            device_id_type=MESH,
        )

    def hand_cut(t, d):
        left = da_t if t == 0 else hid_t
        own = pl.ds(pl.multiple_of(d * part, part), part)
        return pltpu.make_async_remote_copy(
            src_ref=left.at[own, pl.ds(0, slots)],
            dst_ref=left.at[own, pl.ds(slots, slots)],
            send_sem=cut_send.at[t, d],
            recv_sem=cut_recv.at[t, d],
            device_id={"dp": inner},
            device_id_type=MESH,
        )

    @pl.when(end)
    def _():
        hand_x(me).start()

    @pl.loop(1, n_exp)
    def _(k):
        arrival(0, k).wait_recv()

        @pl.when(end)
        def _():
            hand_x(peer(k)).start()

    nt = (((1,), (1,)), ((), ()))

    @pl.loop(0, units // tile)
    def _(j):
        span = pl.ds(pl.multiple_of(j * tile, tile), tile)
        value = lax.dot_general(
            gate[span, :], got[0, 0:slots, :], nt, preferred_element_type=F32
        )
        preact[span, :] = value
        hid_t[span, 0:slots] = (value * jax.nn.sigmoid(value)).astype(BF16)

    def hand_cuts(t):
        @pl.when(end)
        def _():
            @pl.loop(0, n_dp - 1)
            def _(j):
                hand_cut(t, jnp.where(r == 0, n_dp - 1 - j, j)).start()

    @pl.loop(1, n_exp)
    def _(k):
        arrival(1, k).wait_recv()

    def second(j, total):
        span = pl.ds(pl.multiple_of(j * tile, tile), tile)
        slope = lax.dot_general(
            down[span, :], got[1, 0:slots, :], nt, preferred_element_type=F32
        )
        value = preact[span, :]
        sigma = jax.nn.sigmoid(value)
        da_t[span, 0:slots] = (slope * (sigma * (1.0 + value * (1.0 - sigma)))).astype(BF16)
        return total + jnp.sum(hid_t[span, 0:slots].astype(F32) * slope, axis=0, keepdims=True)

    route = lax.fori_loop(0, units // tile, second, jnp.zeros((1, slots), F32))

    hand_cuts(0)
    hand_cuts(1)

    @pl.when(end)
    def _():
        @pl.loop(0, pieces)
        def _(c):
            hand_g(c).start()

    def term(t, d, span, wide):
        left = da_t if t == 0 else hid_t
        start = d * part if isinstance(d, int) else pl.multiple_of(d * part, part)
        depth = 2 * slots if wide else slots
        return jnp.dot(
            left[pl.ds(start, part), 0:depth],
            got[t, 0:depth, span],
            preferred_element_type=F32,
        )

    def columns(c):
        return pl.ds(pl.multiple_of(c * piece, piece), piece)

    def hop(buf, s_sem, r_sem, t, d, c, to):
        return pltpu.make_async_remote_copy(
            src_ref=buf.at[t, d, c],
            dst_ref=buf.at[t, d, c],
            send_sem=s_sem.at[t, d, c],
            recv_sem=r_sem.at[t, d, c],
            device_id={"dp": to},
            device_id_type=MESH,
        )

    def rightward(t, d, c, to=None):
        return hop(right_buf, r_send, r_recv, t, d - 1, c, up)

    def leftward(t, d, c, to=None):
        return hop(left_buf, l_send, l_recv, t, d, c, low)

    def pass_on(t, d, c, copy, buf, index, first):
        @pl.when(first)
        def _():
            buf[t, index, c] = term(t, d, columns(c), True).astype(BF16)

        @pl.when(jnp.logical_not(first))
        def _():
            own = term(t, d, columns(c), False)
            copy.wait_recv()
            buf[t, index, c] = (own + buf[t, index, c].astype(F32)).astype(BF16)

        copy.start()

    def go_right(t):
        for d in range(n_dp - 1, 1, -1):

            @pl.when(r == 1)
            def _():
                hand_cut(t, d).wait_recv()

            @pl.when(jnp.logical_and(r > 0, r < d))
            def _():
                @pl.loop(0, pieces)
                def _(c):
                    if t == 1 and d == n_dp - 1:

                        @pl.when(r == 1)
                        def _():
                            hand_g(c).wait_recv()

                    pass_on(t, d, c, rightward(t, d, c), right_buf, d - 1, r == 1)

    def go_left(t):
        for d in range(n_dp - 2):

            @pl.when(r == n_dp - 2)
            def _():
                hand_cut(t, d).wait_recv()

            @pl.when(jnp.logical_and(r < n_dp - 1, r > d))
            def _():
                @pl.loop(0, pieces)
                def _(c):
                    if t == 1 and d == 0:

                        @pl.when(r == n_dp - 2)
                        def _():
                            hand_g(c).wait_recv()

                    pass_on(t, d, c, leftward(t, d, c), left_buf, d, r == n_dp - 2)

    def returning(k):
        to = peer(k)
        return pltpu.make_async_remote_copy(
            src_ref=back.at[block(to)],
            dst_ref=returned.at[block(me)],
            send_sem=back_send.at[to],
            recv_sem=back_recv.at[me],
            device_id={"expert": to},
            device_id_type=MESH,
        )

    def homecoming(k):
        of = peer(k)
        return pltpu.make_async_remote_copy(
            src_ref=back.at[block(of)],
            dst_ref=returned.at[block(of)],
            send_sem=back_send.at[of],
            recv_sem=back_recv.at[of],
            device_id={"expert": of},
            device_id_type=MESH,
        )

    def send_back():
        tn = (((0,), (0,)), ((), ()))

        @pl.loop(0, pieces)
        def _(c):
            span = columns(c)
            back[:, span] = lax.dot_general(
                da_t[:, 0:slots], gate[:, span], tn, preferred_element_type=F32
            ).astype(BF16)

        tall = jnp.transpose(jnp.broadcast_to(route, (LANES, slots)))
        high = tall.astype(BF16)
        rest = (tall - high.astype(F32)).astype(BF16)
        lane = lax.broadcasted_iota(jnp.int32, (slots, LANES), 1)
        back[:, pl.ds(width, LANES)] = jnp.where(
            lane < 1, high.astype(F32), rest.astype(F32)
        ).astype(BF16)

        @pl.loop(1, n_exp)
        def _(k):
            returning(k).start()

        returned[block(me), :] = back[block(me), :]

    send_back()

    @pl.when(after_end)
    def _():
        @pl.loop(0, n_exp)
        def _(e):
            hand_x(e).wait_recv()

    for t in range(2):

        @pl.when(lower)
        def _():
            go_right(t)

        go_left(t)

        @pl.when(jnp.logical_not(lower))
        def _():
            go_right(t)

    @pl.loop(1, n_exp)
    def _(k):
        homecoming(k).wait_recv()

    tn = (((0,), (0,)), ((), ()))

    @pl.loop(0, pieces)
    def _(c):
        span = columns(c)
        token_out[:, span] = lax.dot_general(
            place, returned[:, span], tn, preferred_element_type=F32
        ).astype(BF16)

    pair = lax.dot_general(
        place, returned[:, pl.ds(width, LANES)], tn, preferred_element_type=F32
    )
    total = jnp.broadcast_to((pair[:, 0:1] + pair[:, 1:2]) / weights, (rows, LANES))
    route_out[...] = jnp.transpose(total)[0:1, :].astype(BF16)

    for t in range(2):
        out = gate_out if t == 0 else down_out

        @pl.when(after_end)
        def _():
            hand_cut(t, r).wait_recv()

        @pl.loop(0, pieces)
        def _(c):
            span = columns(c)

            def from_right():
                hop(left_buf, l_send, l_recv, t, r, c, low).wait_recv()
                return left_buf[t, r, c].astype(F32)

            def from_left():
                hop(right_buf, r_send, r_recv, t, r - 1, c, up).wait_recv()
                return right_buf[t, r - 1, c].astype(F32)

            @pl.when(r == 0)
            def _():
                out[:, span] = (term(t, r, span, False) + from_right()).astype(BF16)

            @pl.when(r == n_dp - 1)
            def _():
                out[:, span] = (term(t, r, span, False) + from_left()).astype(BF16)

            @pl.when(r == 1)
            def _():
                out[:, span] = (term(t, r, span, True) + from_right()).astype(BF16)

            @pl.when(r == n_dp - 2)
            def _():
                out[:, span] = (term(t, r, span, True) + from_left()).astype(BF16)

            @pl.when(jnp.logical_and(r > 1, r < n_dp - 2))
            def _():
                out[:, span] = (term(t, r, span, False) + from_right() + from_left()).astype(BF16)

    @pl.loop(1, n_exp)
    def _(k):
        exchange(0, k).wait_send()
        exchange(1, k).wait_send()
        returning(k).wait_send()

    @pl.when(end)
    def _():
        @pl.loop(0, n_exp)
        def _(e):
            hand_x(e).wait_send()

        @pl.loop(0, pieces)
        def _(c):
            hand_g(c).wait_send()

        for t in range(2):

            @pl.loop(0, n_dp - 1)
            def _(j):
                hand_cut(t, jnp.where(r == 0, n_dp - 1 - j, j)).wait_send()

    for t in range(2):
        for d in range(n_dp):

            @pl.loop(0, pieces)
            def _(c):
                if d > 1:

                    @pl.when(jnp.logical_and(r > 0, r < d))
                    def _():
                        rightward(t, d, c).wait_send()

                if d < n_dp - 2:

                    @pl.when(jnp.logical_and(r < n_dp - 1, r > d))
                    def _():
                        leftward(t, d, c).wait_send()


def kernel_four(
    n_exp, cap, pieces,
    ids_hbm, tokens_hbm, weights_hbm, grads_hbm, gate_hbm, down_hbm,
    token_out, route_out, gate_out, down_out,
    ids_ref, tokens_ref, weights_ref, grads_ref,
    sent, got_x, got_g, gate, down, preact, hid_t, da_t, back, returned,
    scaled, raw, raw_ids, relay, far_sent, chain_out, chain_in, pair_out, pair_in,
    load_sem, send_sem, recv_sem, raw_send, raw_recv, relay_send, relay_recv, far_send, far_recv,
    slice_send, slice_recv, cut_send, cut_recv, x_send, x_recv,
    chain_send, chain_recv, on_send, on_recv, pair_send, pair_recv, back_send, back_recv,
):
    rows, width = tokens_ref.shape
    slots = n_exp * cap
    units = gate.shape[0]
    part = units // 4
    piece = width // pieces
    early = (pieces + 1) // 2
    half = early * piece
    tile = 256 if units % 256 == 0 else part
    r = lax.axis_index("dp")
    me = lax.axis_index("expert")
    partner = r + 1 - 2 * lax.rem(r, 2)
    far = lax.rem(r + 2, 4)
    opposite = 3 - r
    inner = jnp.logical_or(r == 1, r == 2)
    outer = jnp.logical_or(r == 0, r == 3)

    def peer(k):
        return lax.rem(me + k, n_exp)

    def block(e):
        return pl.ds(pl.multiple_of(e * cap, cap), cap)

    def far_block(e):
        return pl.ds(pl.multiple_of(slots + e * cap, cap), cap)

    def units_of(d):
        return pl.ds(pl.multiple_of(d * part, part), part)

    def columns(c):
        return pl.ds(c * piece, piece)

    near_half, far_half = (
        pl.ds(pl.multiple_of(jnp.where(cond, 0, 2 * part), part), 2 * part)
        for cond in (r < 2, r > 1)
    )
    own_rows, more_rows = pl.ds(0, slots), pl.ds(slots, slots)

    loads = [
        pltpu.make_async_copy(source, held, load_sem.at[i])
        for i, (source, held) in enumerate((
            (weights_hbm, weights_ref), (grads_hbm, grads_ref), (ids_hbm, ids_ref),
            (tokens_hbm, tokens_ref),
            (gate_hbm, gate), (down_hbm, down),
        ))
    ]
    for load in loads[:4]:
        load.start()

    barrier = pltpu.get_barrier_semaphore()

    @pl.loop(1, n_exp)
    def _(k):
        pl.semaphore_signal(barrier, inc=1, device_id={"expert": peer(k)}, device_id_type=MESH)

    @pl.loop(1, 4)
    def _(k):
        other = lax.rem(r + k, 4)
        pl.semaphore_signal(barrier, inc=1, device_id={"dp": other}, device_id_type=MESH)

    for load in loads[4:]:
        load.start()

    def over(src, dst, s_sem, r_sem, **to):
        return pltpu.make_async_remote_copy(
            src_ref=src, dst_ref=dst, send_sem=s_sem, recv_sem=r_sem,
            device_id=to, device_id_type=MESH,
        )

    def exchange(t, to, at, device):
        got = got_g if t else got_x
        return over(
            sent.at[t, block(to)], got.at[block(at)],
            send_sem.at[t], recv_sem.at[t], expert=device,
        )

    def far_exchange(c, to, at, device):
        return over(
            far_sent.at[block(to), columns(c)], got_g.at[far_block(at), columns(c)],
            far_send.at[c], far_recv.at[c], expert=device,
        )

    def returning(to, at, device):
        return over(
            back.at[block(to)], returned.at[block(at)],
            back_send, back_recv, expert=device,
        )

    first, last = pl.ds(0, half), pl.ds(half, width - half)

    def raw_first():
        return [
            over(ids_ref, raw_ids, raw_send.at[0], raw_recv.at[0], dp=far),
            over(scaled.at[:, first], raw.at[:, first], raw_send.at[1], raw_recv.at[1], dp=far),
        ]

    def raw_last():
        return over(scaled.at[:, last], raw.at[:, last], raw_send.at[2], raw_recv.at[2], dp=far)

    def to_relay():
        return over(scaled.at[:, last], relay, relay_send, relay_recv, dp=partner)

    def from_relay():
        return over(relay, raw.at[:, last], relay_send, raw_recv.at[2], dp=opposite)

    def slice_copy(half):
        return over(
            hid_t.at[half, own_rows], hid_t.at[half, more_rows], slice_send, slice_recv, dp=far
        )

    def hand_x(c):
        return over(
            got_x.at[own_rows, columns(c)], got_x.at[more_rows, columns(c)],
            x_send, x_recv.at[c], dp=partner,
        )

    def hand_cut(d):
        return over(
            da_t.at[units_of(d), own_rows], da_t.at[units_of(d), more_rows],
            cut_send, cut_recv.at[d], dp=partner,
        )

    def chain(i, c):
        return over(
            chain_out.at[i, c], chain_in.at[i, c], chain_send, chain_recv.at[i, c],
            dp=opposite,
        )

    def pass_on(c):
        return over(
            chain_in.at[0, c], chain_in.at[0, c], on_send, on_recv.at[c], dp=partner
        )

    def pair(c):
        return over(
            pair_out.at[c], pair_in.at[c], pair_send, pair_recv.at[c], dp=partner
        )

    others = pl.ds(0, (n_exp - 1) * cap)

    def exchanged(t):
        return over(
            sent.at[t, others], (got_g if t else got_x).at[others],
            send_sem.at[t], recv_sem.at[t], dp=partner,
        )

    def far_exchanged(c):
        return over(
            far_sent.at[others, columns(c)], got_g.at[others, columns(c)],
            far_send.at[c], far_recv.at[c], dp=partner,
        )

    def returned_all():
        return over(back.at[others], returned.at[others], back_send, back_recv, dp=partner)

    loads[0].wait()
    weights = jnp.transpose(
        jnp.broadcast_to(weights_ref[...].astype(F32), (LANES, rows))
    )[:, 0:1]
    loads[1].wait()
    scaled[...] = (weights * grads_ref[...].astype(F32)).astype(BF16)
    loads[2].wait()
    place = placement(ids_ref[...], n_exp, cap)
    pl.semaphore_wait(barrier, n_exp - 1 + 3)

    for copy in raw_first():
        copy.start()

    @pl.when(inner)
    def _():
        raw_last().start()

    @pl.when(outer)
    def _():
        to_relay().start()

    loads[3].wait()
    sent[0] = jnp.dot(place, tokens_ref[...], preferred_element_type=F32).astype(BF16)

    @pl.loop(1, n_exp)
    def _(k):
        exchange(0, peer(k), me, peer(k)).start()

    sent[1] = jnp.dot(place, scaled[...], preferred_element_type=F32).astype(BF16)

    @pl.loop(1, n_exp)
    def _(k):
        exchange(1, peer(k), me, peer(k)).start()

    got_x[block(me)] = sent[0, block(me)]
    got_g[block(me)] = sent[1, block(me)]

    for load in loads[4:]:
        load.wait()

    exchanged(0).wait_recv()

    @pl.when(outer)
    def _():
        hand_x(0).start()

    nt = (((1,), (1,)), ((), ()))
    tn = (((0,), (0,)), ((), ()))

    @pl.loop(0, units // tile)
    def _(j):
        span = pl.ds(pl.multiple_of(j * tile, tile), tile)
        value = lax.dot_general(
            gate[span, :], got_x[0:slots, :], nt, preferred_element_type=F32
        )
        preact[span, :] = value
        hid_t[span, 0:slots] = (value * jax.nn.sigmoid(value)).astype(BF16)

    slice_copy(far_half).start()

    @pl.when(inner)
    def _():
        to_relay().wait_recv()
        from_relay().start()

    @pl.when(outer)
    def _():
        hand_x(1).start()

    def far_dispatch(chunks):
        for c in chunks:
            span = columns(c)
            far_sent[:, span] = jnp.dot(
                far_place, raw[:, span], preferred_element_type=F32
            ).astype(BF16)

            @pl.loop(1, n_exp)
            def _(k):
                far_exchange(c, peer(k), me, peer(k)).start()

            got_g[far_block(me), span] = far_sent[block(me), span]

    for copy in raw_first():
        copy.wait_recv()
    far_place = placement(raw_ids[...], n_exp, cap)
    far_dispatch(range(early))

    def far_rest():
        raw_last().wait_recv()
        far_dispatch(range(early, pieces))

    @pl.when(outer)
    def _():
        far_rest()

    exchanged(1).wait_recv()

    def second(j, total):
        span = pl.ds(pl.multiple_of(j * tile, tile), tile)
        slope = lax.dot_general(
            down[span, :], got_g[0:slots, :], nt, preferred_element_type=F32
        )
        value = preact[span, :]
        sigma = jax.nn.sigmoid(value)
        da_t[span, 0:slots] = (slope * (sigma * (1.0 + value * (1.0 - sigma)))).astype(BF16)
        return total + jnp.sum(hid_t[span, 0:slots].astype(F32) * slope, axis=0, keepdims=True)

    route = lax.fori_loop(0, units // tile, second, jnp.zeros((1, slots), F32))

    @pl.when(outer)
    def _():
        for d in (opposite, far):
            hand_cut(d).start()
        for c in range(2, pieces):
            hand_x(c).start()
        hand_cut(partner).start()

    def gate_term(d, c, depth):
        return jnp.dot(
            da_t[units_of(d), 0:depth], got_x[0:depth, columns(c)], preferred_element_type=F32
        )

    def down_term(d, c):
        return jnp.dot(
            hid_t[units_of(d), :], got_g[:, columns(c)], preferred_element_type=F32
        )

    def send_pair(c):
        far_exchanged(c).wait_recv()
        pair_out[c] = down_term(partner, c).astype(BF16)
        pair(c).start()

    def send_chain(i, c):
        d = opposite if i else far
        if c == 0:
            hand_cut(d).wait_recv()
        if i == 0:
            hand_x(c).wait_recv()
        chain_out[i, c] = gate_term(d, c, 2 * slots).astype(BF16)
        chain(i, c).start()

    def forward(c):
        own = gate_term(partner, c, slots)
        chain(0, c).wait_recv()
        chain_in[0, c] = (own + chain_in[0, c].astype(F32)).astype(BF16)
        pass_on(c).start()

    def send_back():
        for c in range(pieces):
            span = columns(c)
            back[:, span] = lax.dot_general(
                da_t[:, 0:slots], gate[:, span], tn, preferred_element_type=F32
            ).astype(BF16)

        tall = jnp.transpose(jnp.broadcast_to(route, (LANES, slots)))
        high = tall.astype(BF16)
        rest = (tall - high.astype(F32)).astype(BF16)
        lane = lax.broadcasted_iota(jnp.int32, (slots, LANES), 1)
        back[:, pl.ds(width, LANES)] = jnp.where(
            lane < 1, high.astype(F32), rest.astype(F32)
        ).astype(BF16)

        @pl.loop(1, n_exp)
        def _(k):
            returning(peer(k), me, peer(k)).start()

        returned[block(me), :] = back[block(me), :]

    slice_copy(near_half).wait_recv()

    @pl.when(inner)
    def _():
        steps = [(send_pair, 0), (send_chain, 0, 0)]
        for c in range(1, pieces):
            ahead = [(send_pair, c), (send_chain, 0, c)]
            rest = [(send_chain, 1, c - 1), (forward, c - 1)]
            steps += (ahead[::-1] if c < early else ahead) + (rest if c < pieces - 1 else rest[::-1])
            if c == 1:
                steps.insert(3, (far_rest,))
        steps.insert(-2, (send_back,))
        steps += [(forward, pieces - 1), (send_chain, 1, pieces - 1)]
        for step, *args in steps:
            step(*args)

    @pl.when(outer)
    def _():
        for c in range(pieces):
            send_pair(c)
        send_back()

    returned_all().wait_recv()

    for c in range(pieces):
        span = columns(c)
        token_out[:, span] = lax.dot_general(
            place, returned[:, span], tn, preferred_element_type=F32
        ).astype(BF16)

    both = lax.dot_general(
        place, returned[:, pl.ds(width, LANES)], tn, preferred_element_type=F32
    )
    total = jnp.broadcast_to((both[:, 0:1] + both[:, 1:2]) / weights, (rows, LANES))
    route_out[...] = jnp.transpose(total)[0:1, :].astype(BF16)

    for c in range(pieces):
        own = down_term(r, c)
        pair(c).wait_recv()
        down_out[:, columns(c)] = (own + pair_in[c].astype(F32)).astype(BF16)

    @pl.when(inner)
    def _():
        hand_cut(r).wait_recv()
        for c in range(pieces):
            own = gate_term(r, c, 2 * slots)
            chain(1, c).wait_recv()
            gate_out[:, columns(c)] = (own + chain_in[1, c].astype(F32)).astype(BF16)

    @pl.when(outer)
    def _():
        for c in range(pieces):
            own = gate_term(r, c, slots)
            pass_on(c).wait_recv()
            gate_out[:, columns(c)] = (own + chain_in[0, c].astype(F32)).astype(BF16)

    for t in range(2):
        exchanged(t).wait_send()
    for c in range(pieces):
        far_exchanged(c).wait_send()
    returned_all().wait_send()
    for copy in raw_first():
        copy.wait_send()
    slice_copy(far_half).wait_send()
    over(pair_out, pair_in, pair_send, pair_recv.at[0], dp=partner).wait_send()

    @pl.when(inner)
    def _():
        raw_last().wait_send()
        from_relay().wait_send()
        over(chain_out, chain_in, chain_send, chain_recv.at[0, 0], dp=opposite).wait_send()
        over(chain_in.at[0], chain_in.at[0], on_send, on_recv.at[0], dp=partner).wait_send()

    @pl.when(outer)
    def _():
        to_relay().wait_send()
        cuts = pl.ds(0, 3 * part)
        over(
            da_t.at[cuts, own_rows], da_t.at[cuts, more_rows], cut_send, cut_recv.at[0], dp=partner
        ).wait_send()
        over(
            got_x.at[own_rows], got_x.at[more_rows], x_send, x_recv.at[0], dp=partner
        ).wait_send()


def settle(token, route, gate, down, token_out, route_out, gate_out, down_out, sems):
    copies = [
        pltpu.make_async_copy(source, out, sems.at[i])
        for i, (source, out) in enumerate((
            (gate, gate_out), (down, down_out), (token, token_out), (route, route_out),
        ))
    ]
    for copy in copies:
        copy.start()
    for copy in copies:
        copy.wait()


def chain_scratch(n_dp, n_exp, pieces, slots, units, part, width, piece, rows):
    dma = pltpu.SemaphoreType.DMA
    return [
        pltpu.VMEM((2, slots, width), BF16),
        pltpu.VMEM((2, 2 * slots, width), BF16),
        pltpu.VMEM((units, width), BF16),
        pltpu.VMEM((units, width), BF16),
        pltpu.VMEM((units, slots), F32),
        pltpu.VMEM((units, 2 * slots), BF16),
        pltpu.VMEM((units, 2 * slots), BF16),
        pltpu.VMEM((slots, width + LANES), BF16),
        pltpu.VMEM((slots, width + LANES), BF16),
        pltpu.VMEM((2, n_dp - 1, pieces, part, piece), BF16),
        pltpu.VMEM((2, n_dp - 1, pieces, part, piece), BF16),
        dma((2,)),
        dma((2, n_exp)), dma((2, n_exp)), dma((n_exp,)), dma((n_exp,)),
        dma((2, n_dp - 1, pieces)), dma((2, n_dp - 1, pieces)),
        dma((2, n_dp - 1, pieces)), dma((2, n_dp - 1, pieces)),
        dma((n_exp,)), dma((n_exp,)), dma((pieces,)), dma((pieces,)),
        dma((2, n_dp)), dma((2, n_dp)),
    ]


def four_scratch(n_dp, n_exp, pieces, slots, units, part, width, piece, rows):
    dma = pltpu.SemaphoreType.DMA
    return [
        pltpu.VMEM((1, rows), jnp.int32),
        pltpu.VMEM((rows, width), BF16),
        pltpu.VMEM((1, rows), BF16),
        pltpu.VMEM((rows, width), BF16),
        pltpu.VMEM((2, slots, width), BF16),
        pltpu.VMEM((2 * slots, width), BF16),
        pltpu.VMEM((2 * slots, width), BF16),
        pltpu.VMEM((units, width), BF16),
        pltpu.VMEM((units, width), BF16),
        pltpu.VMEM((units, slots), F32),
        pltpu.VMEM((units, 2 * slots), BF16),
        pltpu.VMEM((units, 2 * slots), BF16),
        pltpu.VMEM((slots, width + LANES), BF16),
        pltpu.VMEM((slots, width + LANES), BF16),
        pltpu.VMEM((rows, width), BF16),
        pltpu.VMEM((rows, width), BF16),
        pltpu.VMEM((1, rows), jnp.int32),
        pltpu.VMEM((rows, pieces // 2 * piece), BF16),
        pltpu.VMEM((slots, width), BF16),
        pltpu.VMEM((2, pieces, part, piece), BF16),
        pltpu.VMEM((2, pieces, part, piece), BF16),
        pltpu.VMEM((pieces, part, piece), BF16),
        pltpu.VMEM((pieces, part, piece), BF16),
        dma((6,)), dma((2,)), dma((2,)), dma((3,)), dma((3,)), dma, dma, dma((pieces,)), dma((pieces,)),
        dma, dma, dma, dma((n_dp,)), dma, dma((pieces,)),
        dma, dma((2, pieces)), dma, dma((pieces,)), dma, dma((pieces,)), dma, dma,
    ]


def per_device(tokens, expert_ids, route_weights, out_grad, gate_weight, down_weight):
    rows, width = tokens.shape
    n_exp, n_dp = lax.axis_size("expert"), lax.axis_size("dp")
    top = expert_ids.shape[1]
    assert top == 1 and n_dp >= 4
    cap = -(-max(2, 2 * rows * top // n_exp) // 16) * 16
    slots = n_exp * cap
    units = gate_weight.shape[1]
    part = units // n_dp
    pieces = max(1, width // 512)
    piece = width // pieces
    shapes = (
        jax.ShapeDtypeStruct((rows, width), BF16),
        jax.ShapeDtypeStruct((1, rows), BF16),
        jax.ShapeDtypeStruct((part, width), BF16),
        jax.ShapeDtypeStruct((part, width), BF16),
    )
    vmem = pl.BlockSpec(memory_space=pltpu.VMEM)
    hbm = pl.BlockSpec(memory_space=pl.ANY)
    four = n_dp == 4
    body = (
        functools.partial(kernel_four, n_exp, cap, pieces)
        if four
        else functools.partial(kernel, n_dp, n_exp, cap, pieces)
    )
    scratch = four_scratch if four else chain_scratch
    results = pl.pallas_call(
        body,
        out_shape=tuple(pltpu.VMEM(a.shape, a.dtype) for a in shapes) if four else shapes,
        in_specs=[hbm] * 6 if four else [vmem] * 4 + [hbm] * 2,
        out_specs=(vmem,) * 4,
        scratch_shapes=scratch(n_dp, n_exp, pieces, slots, units, part, width, piece, rows),
        compiler_params=pltpu.CompilerParams(
            collective_id=0, has_side_effects=True,
            vmem_limit_bytes=60_000_000 if four else 67_000_000,

        ),
    )(
        expert_ids.reshape(1, rows), tokens, route_weights.reshape(1, rows), out_grad,
        gate_weight[0], down_weight[0],
    )
    if four:
        results = [pltpu.with_memory_space_constraint(a, pltpu.VMEM) for a in results]
    token_grad, route_grad, gate_grad, down_grad = pl.pallas_call(
        settle,
        out_shape=shapes,
        in_specs=[vmem] * 4,
        out_specs=(hbm,) * 4,
        scratch_shapes=[pltpu.SemaphoreType.DMA((4,))],
    )(*results)
    return token_grad, route_grad.reshape(rows, 1), gate_grad[None], down_grad[None]


def solution(mesh):
    placed = (
        P(("dp", "expert"), None),
        P(("dp", "expert"), None),
        P(("dp", "expert"), None),
        P(("dp", "expert"), None),
        P("expert", None, None),
        P("expert", None, None),
    )
    return jax.shard_map(
        per_device,
        mesh=mesh,
        in_specs=placed,
        out_specs=(
            P(("dp", "expert"), None),
            P(("dp", "expert"), None),
            P("expert", "dp", None),
            P("expert", "dp", None),
        ),
        check_vma=False,
    )
```

```python
import functools

import jax
import jax.numpy as jnp
from jax import lax
from jax.experimental import pallas as pl
from jax.experimental.pallas import tpu as pltpu
from jax.sharding import PartitionSpec as P

MESH = pl.DeviceIdType.MESH
BF16, F32 = jnp.bfloat16, jnp.float32
LANES = 128


def placement(ids, n_exp, cap):
    rows = ids.shape[1]
    slots = n_exp * cap
    names = lax.broadcasted_iota(jnp.int32, (max(n_exp, 16), rows), 0)
    one_hot = (names == ids).astype(F32)
    before = (
        lax.broadcasted_iota(jnp.int32, (rows, rows), 0)
        < lax.broadcasted_iota(jnp.int32, (rows, rows), 1)
    ).astype(F32)
    counts = jnp.dot(one_hot.astype(BF16), before.astype(BF16), preferred_element_type=F32)
    rank = jnp.sum(counts * one_hot, axis=0, keepdims=True).astype(jnp.int32)
    target = ids * cap + rank
    match = lax.broadcasted_iota(jnp.int32, (slots, rows), 0) == target
    return match.astype(F32).astype(BF16)


def kernel(
    n_dp, n_exp, cap, pieces,
    ids_ref, tokens_ref, weights_ref, grads_ref, gate_hbm, down_hbm,
    token_out, route_out, gate_out, down_out,
    sent, got, gate, down, preact, hid_t, da_t, back, returned, right_buf, left_buf,
    load_sem, send_sem, recv_sem, back_send, back_recv, r_send, r_recv, l_send, l_recv,
    x_send, x_recv, g_send, g_recv, cut_send, cut_recv,
):
    rows, width = tokens_ref.shape
    slots = n_exp * cap
    units = gate.shape[0]
    part = units // n_dp
    piece = width // pieces
    tile = 256 if units % 256 == 0 else part
    r = lax.axis_index("dp")
    me = lax.axis_index("expert")

    def peer(k):
        return lax.rem(me + k, n_exp)

    def block(e):
        return pl.ds(pl.multiple_of(e * cap, cap), cap)

    loads = [
        pltpu.make_async_copy(gate_hbm, gate, load_sem.at[0]),
        pltpu.make_async_copy(down_hbm, down, load_sem.at[1]),
    ]
    for load in loads:
        load.start()

    barrier = pltpu.get_barrier_semaphore()

    @pl.loop(1, n_exp)
    def _(k):
        pl.semaphore_signal(barrier, inc=1, device_id={"expert": peer(k)}, device_id_type=MESH)

    up, low = lax.rem(r + 1, n_dp), lax.rem(r + n_dp - 1, n_dp)

    @pl.loop(1, n_dp)
    def _(k):
        other = lax.rem(r + k, n_dp)
        pl.semaphore_signal(barrier, inc=1, device_id={"dp": other}, device_id_type=MESH)

    place = placement(ids_ref[...], n_exp, cap)
    sent[0] = jnp.dot(place, tokens_ref[...], preferred_element_type=F32).astype(BF16)
    pl.semaphore_wait(barrier, n_exp - 1 + n_dp - 1)

    def exchange(t, k):
        to = peer(k)
        return pltpu.make_async_remote_copy(
            src_ref=sent.at[t, block(to)],
            dst_ref=got.at[t, block(me)],
            send_sem=send_sem.at[t, to],
            recv_sem=recv_sem.at[t, me],
            device_id={"expert": to},
            device_id_type=MESH,
        )

    def arrival(t, k):
        of = peer(k)
        return pltpu.make_async_remote_copy(
            src_ref=sent.at[t, block(of)],
            dst_ref=got.at[t, block(of)],
            send_sem=send_sem.at[t, of],
            recv_sem=recv_sem.at[t, of],
            device_id={"expert": of},
            device_id_type=MESH,
        )

    @pl.loop(1, n_exp)
    def _(k):
        exchange(0, k).start()

    got[0, block(me)] = sent[0, block(me)]
    weights = jnp.transpose(
        jnp.broadcast_to(weights_ref[...].astype(F32), (LANES, rows))
    )[:, 0:1]
    scaled = (weights * grads_ref[...].astype(F32)).astype(BF16)
    sent[1] = jnp.dot(place, scaled, preferred_element_type=F32).astype(BF16)

    @pl.loop(1, n_exp)
    def _(k):
        exchange(1, k).start()

    got[1, block(me)] = sent[1, block(me)]

    for load in loads:
        load.wait()

    end = jnp.logical_or(r == 0, r == n_dp - 1)
    after_end = jnp.logical_or(r == 1, r == n_dp - 2)
    inner = jnp.where(r == 0, up, low)
    lower = r < n_dp // 2

    def hand_x(e):
        return pltpu.make_async_remote_copy(
            src_ref=got.at[0, block(e)],
            dst_ref=got.at[0, pl.ds(pl.multiple_of(slots + e * cap, cap), cap)],
            send_sem=x_send.at[e],
            recv_sem=x_recv.at[e],
            device_id={"dp": inner},
            device_id_type=MESH,
        )

    def hand_g(c):
        span = pl.ds(pl.multiple_of(c * piece, piece), piece)
        return pltpu.make_async_remote_copy(
            src_ref=got.at[1, pl.ds(0, slots), span],
            dst_ref=got.at[1, pl.ds(slots, slots), span],
            send_sem=g_send.at[c],
            recv_sem=g_recv.at[c],
            device_id={"dp": inner},
            device_id_type=MESH,
        )

    def hand_cut(t, d):
        left = da_t if t == 0 else hid_t
        own = pl.ds(pl.multiple_of(d * part, part), part)
        return pltpu.make_async_remote_copy(
            src_ref=left.at[own, pl.ds(0, slots)],
            dst_ref=left.at[own, pl.ds(slots, slots)],
            send_sem=cut_send.at[t, d],
            recv_sem=cut_recv.at[t, d],
            device_id={"dp": inner},
            device_id_type=MESH,
        )

    @pl.when(end)
    def _():
        hand_x(me).start()

    @pl.loop(1, n_exp)
    def _(k):
        arrival(0, k).wait_recv()

        @pl.when(end)
        def _():
            hand_x(peer(k)).start()

    nt = (((1,), (1,)), ((), ()))

    @pl.loop(0, units // tile)
    def _(j):
        span = pl.ds(pl.multiple_of(j * tile, tile), tile)
        value = lax.dot_general(
            gate[span, :], got[0, 0:slots, :], nt, preferred_element_type=F32
        )
        preact[span, :] = value
        hid_t[span, 0:slots] = (value * jax.nn.sigmoid(value)).astype(BF16)

    def hand_cuts(t):
        @pl.when(end)
        def _():
            @pl.loop(0, n_dp - 1)
            def _(j):
                hand_cut(t, jnp.where(r == 0, n_dp - 1 - j, j)).start()

    @pl.loop(1, n_exp)
    def _(k):
        arrival(1, k).wait_recv()

    def second(j, total):
        span = pl.ds(pl.multiple_of(j * tile, tile), tile)
        slope = lax.dot_general(
            down[span, :], got[1, 0:slots, :], nt, preferred_element_type=F32
        )
        value = preact[span, :]
        sigma = jax.nn.sigmoid(value)
        da_t[span, 0:slots] = (slope * (sigma * (1.0 + value * (1.0 - sigma)))).astype(BF16)
        return total + jnp.sum(hid_t[span, 0:slots].astype(F32) * slope, axis=0, keepdims=True)

    route = lax.fori_loop(0, units // tile, second, jnp.zeros((1, slots), F32))

    hand_cuts(0)
    hand_cuts(1)

    @pl.when(end)
    def _():
        @pl.loop(0, pieces)
        def _(c):
            hand_g(c).start()

    def term(t, d, span, wide):
        left = da_t if t == 0 else hid_t
        start = d * part if isinstance(d, int) else pl.multiple_of(d * part, part)
        depth = 2 * slots if wide else slots
        return jnp.dot(
            left[pl.ds(start, part), 0:depth],
            got[t, 0:depth, span],
            preferred_element_type=F32,
        )

    def columns(c):
        return pl.ds(pl.multiple_of(c * piece, piece), piece)

    def hop(buf, s_sem, r_sem, t, d, c, to):
        return pltpu.make_async_remote_copy(
            src_ref=buf.at[t, d, c],
            dst_ref=buf.at[t, d, c],
            send_sem=s_sem.at[t, d, c],
            recv_sem=r_sem.at[t, d, c],
            device_id={"dp": to},
            device_id_type=MESH,
        )

    def rightward(t, d, c, to=None):
        return hop(right_buf, r_send, r_recv, t, d - 1, c, up)

    def leftward(t, d, c, to=None):
        return hop(left_buf, l_send, l_recv, t, d, c, low)

    def pass_on(t, d, c, copy, buf, index, first):
        @pl.when(first)
        def _():
            buf[t, index, c] = term(t, d, columns(c), True).astype(BF16)

        @pl.when(jnp.logical_not(first))
        def _():
            own = term(t, d, columns(c), False)
            copy.wait_recv()
            buf[t, index, c] = (own + buf[t, index, c].astype(F32)).astype(BF16)

        copy.start()

    def go_right(t):
        for d in range(n_dp - 1, 1, -1):

            @pl.when(r == 1)
            def _():
                hand_cut(t, d).wait_recv()

            @pl.when(jnp.logical_and(r > 0, r < d))
            def _():
                @pl.loop(0, pieces)
                def _(c):
                    if t == 1 and d == n_dp - 1:

                        @pl.when(r == 1)
                        def _():
                            hand_g(c).wait_recv()

                    pass_on(t, d, c, rightward(t, d, c), right_buf, d - 1, r == 1)

    def go_left(t):
        for d in range(n_dp - 2):

            @pl.when(r == n_dp - 2)
            def _():
                hand_cut(t, d).wait_recv()

            @pl.when(jnp.logical_and(r < n_dp - 1, r > d))
            def _():
                @pl.loop(0, pieces)
                def _(c):
                    if t == 1 and d == 0:

                        @pl.when(r == n_dp - 2)
                        def _():
                            hand_g(c).wait_recv()

                    pass_on(t, d, c, leftward(t, d, c), left_buf, d, r == n_dp - 2)

    def returning(k):
        to = peer(k)
        return pltpu.make_async_remote_copy(
            src_ref=back.at[block(to)],
            dst_ref=returned.at[block(me)],
            send_sem=back_send.at[to],
            recv_sem=back_recv.at[me],
            device_id={"expert": to},
            device_id_type=MESH,
        )

    def homecoming(k):
        of = peer(k)
        return pltpu.make_async_remote_copy(
            src_ref=back.at[block(of)],
            dst_ref=returned.at[block(of)],
            send_sem=back_send.at[of],
            recv_sem=back_recv.at[of],
            device_id={"expert": of},
            device_id_type=MESH,
        )

    def send_back():
        tn = (((0,), (0,)), ((), ()))

        @pl.loop(0, pieces)
        def _(c):
            span = columns(c)
            back[:, span] = lax.dot_general(
                da_t[:, 0:slots], gate[:, span], tn, preferred_element_type=F32
            ).astype(BF16)

        tall = jnp.transpose(jnp.broadcast_to(route, (LANES, slots)))
        high = tall.astype(BF16)
        rest = (tall - high.astype(F32)).astype(BF16)
        lane = lax.broadcasted_iota(jnp.int32, (slots, LANES), 1)
        back[:, pl.ds(width, LANES)] = jnp.where(
            lane < 1, high.astype(F32), rest.astype(F32)
        ).astype(BF16)

        @pl.loop(1, n_exp)
        def _(k):
            returning(k).start()

        returned[block(me), :] = back[block(me), :]

    send_back()

    @pl.when(after_end)
    def _():
        @pl.loop(0, n_exp)
        def _(e):
            hand_x(e).wait_recv()

    for t in range(2):

        @pl.when(lower)
        def _():
            go_right(t)

        go_left(t)

        @pl.when(jnp.logical_not(lower))
        def _():
            go_right(t)

    @pl.loop(1, n_exp)
    def _(k):
        homecoming(k).wait_recv()

    tn = (((0,), (0,)), ((), ()))

    @pl.loop(0, pieces)
    def _(c):
        span = columns(c)
        token_out[:, span] = lax.dot_general(
            place, returned[:, span], tn, preferred_element_type=F32
        ).astype(BF16)

    pair = lax.dot_general(
        place, returned[:, pl.ds(width, LANES)], tn, preferred_element_type=F32
    )
    total = jnp.broadcast_to((pair[:, 0:1] + pair[:, 1:2]) / weights, (rows, LANES))
    route_out[...] = jnp.transpose(total)[0:1, :].astype(BF16)

    for t in range(2):
        out = gate_out if t == 0 else down_out

        @pl.when(after_end)
        def _():
            hand_cut(t, r).wait_recv()

        @pl.loop(0, pieces)
        def _(c):
            span = columns(c)

            def from_right():
                hop(left_buf, l_send, l_recv, t, r, c, low).wait_recv()
                return left_buf[t, r, c].astype(F32)

            def from_left():
                hop(right_buf, r_send, r_recv, t, r - 1, c, up).wait_recv()
                return right_buf[t, r - 1, c].astype(F32)

            @pl.when(r == 0)
            def _():
                out[:, span] = (term(t, r, span, False) + from_right()).astype(BF16)

            @pl.when(r == n_dp - 1)
            def _():
                out[:, span] = (term(t, r, span, False) + from_left()).astype(BF16)

            @pl.when(r == 1)
            def _():
                out[:, span] = (term(t, r, span, True) + from_right()).astype(BF16)

            @pl.when(r == n_dp - 2)
            def _():
                out[:, span] = (term(t, r, span, True) + from_left()).astype(BF16)

            @pl.when(jnp.logical_and(r > 1, r < n_dp - 2))
            def _():
                out[:, span] = (term(t, r, span, False) + from_right() + from_left()).astype(BF16)

    @pl.loop(1, n_exp)
    def _(k):
        exchange(0, k).wait_send()
        exchange(1, k).wait_send()
        returning(k).wait_send()

    @pl.when(end)
    def _():
        @pl.loop(0, n_exp)
        def _(e):
            hand_x(e).wait_send()

        @pl.loop(0, pieces)
        def _(c):
            hand_g(c).wait_send()

        for t in range(2):

            @pl.loop(0, n_dp - 1)
            def _(j):
                hand_cut(t, jnp.where(r == 0, n_dp - 1 - j, j)).wait_send()

    for t in range(2):
        for d in range(n_dp):

            @pl.loop(0, pieces)
            def _(c):
                if d > 1:

                    @pl.when(jnp.logical_and(r > 0, r < d))
                    def _():
                        rightward(t, d, c).wait_send()

                if d < n_dp - 2:

                    @pl.when(jnp.logical_and(r < n_dp - 1, r > d))
                    def _():
                        leftward(t, d, c).wait_send()


def kernel_four(
    n_exp, cap, pieces,
    ids_hbm, tokens_hbm, weights_hbm, grads_hbm, gate_hbm, down_hbm,
    token_out, route_out, gate_out, down_out,
    ids_ref, tokens_ref, weights_ref, grads_ref,
    sent, got_x, got_g, gate, down, preact, hid_t, da_t, back, returned,
    scaled, raw, raw_ids, relay, far_sent, chain_out, chain_in, pair_out, pair_in,
    load_sem, send_sem, recv_sem, raw_send, raw_recv, relay_send, relay_recv, far_send, far_recv,
    slice_send, slice_recv, cut_send, cut_recv, x_send, x_recv,
    chain_send, chain_recv, on_send, on_recv, pair_send, pair_recv, back_send, back_recv,
):
    rows, width = tokens_ref.shape
    slots = n_exp * cap
    units = gate.shape[0]
    part = units // 4
    piece = width // pieces
    early = (pieces + 1) // 2
    half = early * piece
    tile = 256 if units % 256 == 0 else part
    r = lax.axis_index("dp")
    me = lax.axis_index("expert")
    partner = r + 1 - 2 * lax.rem(r, 2)
    far = lax.rem(r + 2, 4)
    opposite = 3 - r
    inner = jnp.logical_or(r == 1, r == 2)
    outer = jnp.logical_or(r == 0, r == 3)

    def peer(k):
        return lax.rem(me + k, n_exp)

    def block(e):
        return pl.ds(pl.multiple_of(e * cap, cap), cap)

    def far_block(e):
        return pl.ds(pl.multiple_of(slots + e * cap, cap), cap)

    def units_of(d):
        return pl.ds(pl.multiple_of(d * part, part), part)

    def columns(c):
        return pl.ds(c * piece, piece)

    near_half, far_half = (
        pl.ds(pl.multiple_of(jnp.where(cond, 0, 2 * part), part), 2 * part)
        for cond in (r < 2, r > 1)
    )
    own_rows, more_rows = pl.ds(0, slots), pl.ds(slots, slots)

    loads = [
        pltpu.make_async_copy(source, held, load_sem.at[i])
        for i, (source, held) in enumerate((
            (weights_hbm, weights_ref), (grads_hbm, grads_ref), (ids_hbm, ids_ref),
            (tokens_hbm, tokens_ref),
            (gate_hbm, gate), (down_hbm, down),
        ))
    ]
    for load in loads[:4]:
        load.start()

    barrier = pltpu.get_barrier_semaphore()

    @pl.loop(1, n_exp)
    def _(k):
        pl.semaphore_signal(barrier, inc=1, device_id={"expert": peer(k)}, device_id_type=MESH)

    @pl.loop(1, 4)
    def _(k):
        other = lax.rem(r + k, 4)
        pl.semaphore_signal(barrier, inc=1, device_id={"dp": other}, device_id_type=MESH)

    for load in loads[4:]:
        load.start()

    def over(src, dst, s_sem, r_sem, **to):
        return pltpu.make_async_remote_copy(
            src_ref=src, dst_ref=dst, send_sem=s_sem, recv_sem=r_sem,
            device_id=to, device_id_type=MESH,
        )

    def exchange(t, to, at, device):
        got = got_g if t else got_x
        return over(
            sent.at[t, block(to)], got.at[block(at)],
            send_sem.at[t], recv_sem.at[t], expert=device,
        )

    def far_exchange(c, to, at, device):
        return over(
            far_sent.at[block(to), columns(c)], got_g.at[far_block(at), columns(c)],
            far_send.at[c], far_recv.at[c], expert=device,
        )

    def returning(to, at, device):
        return over(
            back.at[block(to)], returned.at[block(at)],
            back_send, back_recv, expert=device,
        )

    first, last = pl.ds(0, half), pl.ds(half, width - half)

    def raw_first():
        return [
            over(ids_ref, raw_ids, raw_send.at[0], raw_recv.at[0], dp=far),
            over(scaled.at[:, first], raw.at[:, first], raw_send.at[1], raw_recv.at[1], dp=far),
        ]

    def raw_last():
        return over(scaled.at[:, last], raw.at[:, last], raw_send.at[2], raw_recv.at[2], dp=far)

    def to_relay():
        return over(scaled.at[:, last], relay, relay_send, relay_recv, dp=partner)

    def from_relay():
        return over(relay, raw.at[:, last], relay_send, raw_recv.at[2], dp=opposite)

    def slice_copy(half):
        return over(
            hid_t.at[half, own_rows], hid_t.at[half, more_rows], slice_send, slice_recv, dp=far
        )

    def hand_x(c):
        return over(
            got_x.at[own_rows, columns(c)], got_x.at[more_rows, columns(c)],
            x_send, x_recv.at[c], dp=partner,
        )

    def hand_cut(d):
        return over(
            da_t.at[units_of(d), own_rows], da_t.at[units_of(d), more_rows],
            cut_send, cut_recv.at[d], dp=partner,
        )

    def chain(i, c):
        return over(
            chain_out.at[i, c], chain_in.at[i, c], chain_send, chain_recv.at[i, c],
            dp=opposite,
        )

    def pass_on(c):
        return over(
            chain_in.at[0, c], chain_in.at[0, c], on_send, on_recv.at[c], dp=partner
        )

    def pair(c):
        return over(
            pair_out.at[c], pair_in.at[c], pair_send, pair_recv.at[c], dp=partner
        )

    others = pl.ds(0, (n_exp - 1) * cap)

    def exchanged(t):
        return over(
            sent.at[t, others], (got_g if t else got_x).at[others],
            send_sem.at[t], recv_sem.at[t], dp=partner,
        )

    def far_exchanged(c):
        return over(
            far_sent.at[others, columns(c)], got_g.at[others, columns(c)],
            far_send.at[c], far_recv.at[c], dp=partner,
        )

    def returned_all():
        return over(back.at[others], returned.at[others], back_send, back_recv, dp=partner)

    loads[0].wait()
    weights = jnp.transpose(
        jnp.broadcast_to(weights_ref[...].astype(F32), (LANES, rows))
    )[:, 0:1]
    loads[1].wait()
    scaled[...] = (weights * grads_ref[...].astype(F32)).astype(BF16)
    loads[2].wait()
    place = placement(ids_ref[...], n_exp, cap)
    pl.semaphore_wait(barrier, n_exp - 1 + 3)

    for copy in raw_first():
        copy.start()

    @pl.when(inner)
    def _():
        raw_last().start()

    @pl.when(outer)
    def _():
        to_relay().start()

    loads[3].wait()
    sent[0] = jnp.dot(place, tokens_ref[...], preferred_element_type=F32).astype(BF16)

    @pl.loop(1, n_exp)
    def _(k):
        exchange(0, peer(k), me, peer(k)).start()

    sent[1] = jnp.dot(place, scaled[...], preferred_element_type=F32).astype(BF16)

    @pl.loop(1, n_exp)
    def _(k):
        exchange(1, peer(k), me, peer(k)).start()

    got_x[block(me)] = sent[0, block(me)]
    got_g[block(me)] = sent[1, block(me)]

    for load in loads[4:]:
        load.wait()

    exchanged(0).wait_recv()

    @pl.when(outer)
    def _():
        hand_x(0).start()

    nt = (((1,), (1,)), ((), ()))
    tn = (((0,), (0,)), ((), ()))

    @pl.loop(0, units // tile)
    def _(j):
        span = pl.ds(pl.multiple_of(j * tile, tile), tile)
        value = lax.dot_general(
            gate[span, :], got_x[0:slots, :], nt, preferred_element_type=F32
        )
        preact[span, :] = value
        hid_t[span, 0:slots] = (value * jax.nn.sigmoid(value)).astype(BF16)

    slice_copy(far_half).start()

    @pl.when(inner)
    def _():
        to_relay().wait_recv()
        from_relay().start()

    @pl.when(outer)
    def _():
        hand_x(1).start()

    def far_dispatch(chunks):
        for c in chunks:
            span = columns(c)
            far_sent[:, span] = jnp.dot(
                far_place, raw[:, span], preferred_element_type=F32
            ).astype(BF16)

            @pl.loop(1, n_exp)
            def _(k):
                far_exchange(c, peer(k), me, peer(k)).start()

            got_g[far_block(me), span] = far_sent[block(me), span]

    for copy in raw_first():
        copy.wait_recv()
    far_place = placement(raw_ids[...], n_exp, cap)
    far_dispatch(range(early))

    def far_rest():
        raw_last().wait_recv()
        far_dispatch(range(early, pieces))

    @pl.when(outer)
    def _():
        far_rest()

    exchanged(1).wait_recv()

    def second(j, total):
        span = pl.ds(pl.multiple_of(j * tile, tile), tile)
        slope = lax.dot_general(
            down[span, :], got_g[0:slots, :], nt, preferred_element_type=F32
        )
        value = preact[span, :]
        sigma = jax.nn.sigmoid(value)
        da_t[span, 0:slots] = (slope * (sigma * (1.0 + value * (1.0 - sigma)))).astype(BF16)
        return total + jnp.sum(hid_t[span, 0:slots].astype(F32) * slope, axis=0, keepdims=True)

    route = lax.fori_loop(0, units // tile, second, jnp.zeros((1, slots), F32))

    @pl.when(outer)
    def _():
        for d in (opposite, far):
            hand_cut(d).start()
        for c in range(2, pieces):
            hand_x(c).start()
        hand_cut(partner).start()

    def gate_term(d, c, depth):
        return jnp.dot(
            da_t[units_of(d), 0:depth], got_x[0:depth, columns(c)], preferred_element_type=F32
        )

    def down_term(d, c):
        return jnp.dot(
            hid_t[units_of(d), :], got_g[:, columns(c)], preferred_element_type=F32
        )

    def send_pair(c):
        far_exchanged(c).wait_recv()
        pair_out[c] = down_term(partner, c).astype(BF16)
        pair(c).start()

    def send_chain(i, c):
        d = opposite if i else far
        if c == 0:
            hand_cut(d).wait_recv()
        if i == 0:
            hand_x(c).wait_recv()
        chain_out[i, c] = gate_term(d, c, 2 * slots).astype(BF16)
        chain(i, c).start()

    def forward(c):
        own = gate_term(partner, c, slots)
        chain(0, c).wait_recv()
        chain_in[0, c] = (own + chain_in[0, c].astype(F32)).astype(BF16)
        pass_on(c).start()

    def send_back():
        for c in range(pieces):
            span = columns(c)
            back[:, span] = lax.dot_general(
                da_t[:, 0:slots], gate[:, span], tn, preferred_element_type=F32
            ).astype(BF16)

        tall = jnp.transpose(jnp.broadcast_to(route, (LANES, slots)))
        high = tall.astype(BF16)
        rest = (tall - high.astype(F32)).astype(BF16)
        lane = lax.broadcasted_iota(jnp.int32, (slots, LANES), 1)
        back[:, pl.ds(width, LANES)] = jnp.where(
            lane < 1, high.astype(F32), rest.astype(F32)
        ).astype(BF16)

        @pl.loop(1, n_exp)
        def _(k):
            returning(peer(k), me, peer(k)).start()

        returned[block(me), :] = back[block(me), :]

    slice_copy(near_half).wait_recv()

    @pl.when(inner)
    def _():
        steps = [(send_pair, 0), (send_chain, 0, 0)]
        for c in range(1, pieces):
            ahead = [(send_pair, c), (send_chain, 0, c)]
            rest = [(send_chain, 1, c - 1), (forward, c - 1)]
            steps += (ahead[::-1] if c < early else ahead) + (rest if c < pieces - 1 else rest[::-1])
            if c == 1:
                steps.insert(4, (far_rest,))
        steps.insert(-4, (send_back,))
        steps += [(forward, pieces - 1), (send_chain, 1, pieces - 1)]
        for step, *args in steps:
            step(*args)

    @pl.when(outer)
    def _():
        for c in range(pieces):
            send_pair(c)
        send_back()

    returned_all().wait_recv()

    for c in range(pieces):
        span = columns(c)
        token_out[:, span] = lax.dot_general(
            place, returned[:, span], tn, preferred_element_type=F32
        ).astype(BF16)

    both = lax.dot_general(
        place, returned[:, pl.ds(width, LANES)], tn, preferred_element_type=F32
    )
    total = jnp.broadcast_to((both[:, 0:1] + both[:, 1:2]) / weights, (rows, LANES))
    route_out[...] = jnp.transpose(total)[0:1, :].astype(BF16)

    for c in range(pieces):
        own = down_term(r, c)
        pair(c).wait_recv()
        down_out[:, columns(c)] = (own + pair_in[c].astype(F32)).astype(BF16)

    @pl.when(inner)
    def _():
        hand_cut(r).wait_recv()
        for c in range(pieces):
            own = gate_term(r, c, 2 * slots)
            chain(1, c).wait_recv()
            gate_out[:, columns(c)] = (own + chain_in[1, c].astype(F32)).astype(BF16)

    @pl.when(outer)
    def _():
        for c in range(pieces):
            own = gate_term(r, c, slots)
            pass_on(c).wait_recv()
            gate_out[:, columns(c)] = (own + chain_in[0, c].astype(F32)).astype(BF16)

    for t in range(2):
        exchanged(t).wait_send()
    for c in range(pieces):
        far_exchanged(c).wait_send()
    returned_all().wait_send()
    for copy in raw_first():
        copy.wait_send()
    slice_copy(far_half).wait_send()
    over(pair_out, pair_in, pair_send, pair_recv.at[0], dp=partner).wait_send()

    @pl.when(inner)
    def _():
        raw_last().wait_send()
        from_relay().wait_send()
        over(chain_out, chain_in, chain_send, chain_recv.at[0, 0], dp=opposite).wait_send()
        over(chain_in.at[0], chain_in.at[0], on_send, on_recv.at[0], dp=partner).wait_send()

    @pl.when(outer)
    def _():
        to_relay().wait_send()
        cuts = pl.ds(0, 3 * part)
        over(
            da_t.at[cuts, own_rows], da_t.at[cuts, more_rows], cut_send, cut_recv.at[0], dp=partner
        ).wait_send()
        over(
            got_x.at[own_rows], got_x.at[more_rows], x_send, x_recv.at[0], dp=partner
        ).wait_send()


def settle(token, route, gate, down, token_out, route_out, gate_out, down_out, sems):
    copies = [
        pltpu.make_async_copy(source, out, sems.at[i])
        for i, (source, out) in enumerate((
            (gate, gate_out), (down, down_out), (token, token_out), (route, route_out),
        ))
    ]
    for copy in copies:
        copy.start()
    for copy in copies:
        copy.wait()


def chain_scratch(n_dp, n_exp, pieces, slots, units, part, width, piece, rows):
    dma = pltpu.SemaphoreType.DMA
    return [
        pltpu.VMEM((2, slots, width), BF16),
        pltpu.VMEM((2, 2 * slots, width), BF16),
        pltpu.VMEM((units, width), BF16),
        pltpu.VMEM((units, width), BF16),
        pltpu.VMEM((units, slots), F32),
        pltpu.VMEM((units, 2 * slots), BF16),
        pltpu.VMEM((units, 2 * slots), BF16),
        pltpu.VMEM((slots, width + LANES), BF16),
        pltpu.VMEM((slots, width + LANES), BF16),
        pltpu.VMEM((2, n_dp - 1, pieces, part, piece), BF16),
        pltpu.VMEM((2, n_dp - 1, pieces, part, piece), BF16),
        dma((2,)),
        dma((2, n_exp)), dma((2, n_exp)), dma((n_exp,)), dma((n_exp,)),
        dma((2, n_dp - 1, pieces)), dma((2, n_dp - 1, pieces)),
        dma((2, n_dp - 1, pieces)), dma((2, n_dp - 1, pieces)),
        dma((n_exp,)), dma((n_exp,)), dma((pieces,)), dma((pieces,)),
        dma((2, n_dp)), dma((2, n_dp)),
    ]


def four_scratch(n_dp, n_exp, pieces, slots, units, part, width, piece, rows):
    dma = pltpu.SemaphoreType.DMA
    return [
        pltpu.VMEM((1, rows), jnp.int32),
        pltpu.VMEM((rows, width), BF16),
        pltpu.VMEM((1, rows), BF16),
        pltpu.VMEM((rows, width), BF16),
        pltpu.VMEM((2, slots, width), BF16),
        pltpu.VMEM((2 * slots, width), BF16),
        pltpu.VMEM((2 * slots, width), BF16),
        pltpu.VMEM((units, width), BF16),
        pltpu.VMEM((units, width), BF16),
        pltpu.VMEM((units, slots), F32),
        pltpu.VMEM((units, 2 * slots), BF16),
        pltpu.VMEM((units, 2 * slots), BF16),
        pltpu.VMEM((slots, width + LANES), BF16),
        pltpu.VMEM((slots, width + LANES), BF16),
        pltpu.VMEM((rows, width), BF16),
        pltpu.VMEM((rows, width), BF16),
        pltpu.VMEM((1, rows), jnp.int32),
        pltpu.VMEM((rows, pieces // 2 * piece), BF16),
        pltpu.VMEM((slots, width), BF16),
        pltpu.VMEM((2, pieces, part, piece), BF16),
        pltpu.VMEM((2, pieces, part, piece), BF16),
        pltpu.VMEM((pieces, part, piece), BF16),
        pltpu.VMEM((pieces, part, piece), BF16),
        dma((6,)), dma((2,)), dma((2,)), dma((3,)), dma((3,)), dma, dma, dma((pieces,)), dma((pieces,)),
        dma, dma, dma, dma((n_dp,)), dma, dma((pieces,)),
        dma, dma((2, pieces)), dma, dma((pieces,)), dma, dma((pieces,)), dma, dma,
    ]


def per_device(tokens, expert_ids, route_weights, out_grad, gate_weight, down_weight):
    rows, width = tokens.shape
    n_exp, n_dp = lax.axis_size("expert"), lax.axis_size("dp")
    top = expert_ids.shape[1]
    assert top == 1 and n_dp >= 4
    cap = -(-max(2, 2 * rows * top // n_exp) // 16) * 16
    slots = n_exp * cap
    units = gate_weight.shape[1]
    part = units // n_dp
    pieces = max(1, width // 512)
    piece = width // pieces
    shapes = (
        jax.ShapeDtypeStruct((rows, width), BF16),
        jax.ShapeDtypeStruct((1, rows), BF16),
        jax.ShapeDtypeStruct((part, width), BF16),
        jax.ShapeDtypeStruct((part, width), BF16),
    )
    vmem = pl.BlockSpec(memory_space=pltpu.VMEM)
    hbm = pl.BlockSpec(memory_space=pl.ANY)
    four = n_dp == 4
    body = (
        functools.partial(kernel_four, n_exp, cap, pieces)
        if four
        else functools.partial(kernel, n_dp, n_exp, cap, pieces)
    )
    scratch = four_scratch if four else chain_scratch
    results = pl.pallas_call(
        body,
        out_shape=tuple(pltpu.VMEM(a.shape, a.dtype) for a in shapes) if four else shapes,
        in_specs=[hbm] * 6 if four else [vmem] * 4 + [hbm] * 2,
        out_specs=(vmem,) * 4,
        scratch_shapes=scratch(n_dp, n_exp, pieces, slots, units, part, width, piece, rows),
        compiler_params=pltpu.CompilerParams(
            collective_id=0, has_side_effects=True,
            vmem_limit_bytes=60_000_000 if four else 67_000_000,

        ),
    )(
        expert_ids.reshape(1, rows), tokens, route_weights.reshape(1, rows), out_grad,
        gate_weight[0], down_weight[0],
    )
    if four:
        results = [pltpu.with_memory_space_constraint(a, pltpu.VMEM) for a in results]
    token_grad, route_grad, gate_grad, down_grad = pl.pallas_call(
        settle,
        out_shape=shapes,
        in_specs=[vmem] * 4,
        out_specs=(hbm,) * 4,
        scratch_shapes=[pltpu.SemaphoreType.DMA((4,))],
    )(*results)
    return token_grad, route_grad.reshape(rows, 1), gate_grad[None], down_grad[None]


def solution(mesh):
    placed = (
        P(("dp", "expert"), None),
        P(("dp", "expert"), None),
        P(("dp", "expert"), None),
        P(("dp", "expert"), None),
        P("expert", None, None),
        P("expert", None, None),
    )
    return jax.shard_map(
        per_device,
        mesh=mesh,
        in_specs=placed,
        out_specs=(
            P(("dp", "expert"), None),
            P(("dp", "expert"), None),
            P("expert", "dp", None),
            P("expert", "dp", None),
        ),
        check_vma=False,
    )
```
